256 devices in a mesh: seq: 64 (over z, x, core), batch: 4 (over y).
Axes of the slice: x: 4, y: 4, z: 8, core: 2. Of those that a mesh axis runs over, the one named last changes fastest.
Arguments:
- actions: float32 [8, 50, 32], P('batch'), may hold values from -6 to 6
- noise: float32 [8, 2, 50, 32], P('batch'), may hold values from -6 to 6
- times: float32 [8, 2], P('batch'), may hold values from 0.05 to 0.95
- embodiment: int32 [8], P('batch'), may hold values from 0 to 3
- prefix_blocks: int32 [8], P('batch'), may hold values from 1 to 256
- prefix_keys: bfloat16 [8, 32768, 256], P('batch', 'seq'), may hold values from -100 to 100
- prefix_values: bfloat16 [8, 32768, 256], P('batch', 'seq'), may hold values from -6 to 6
- input_heads: float32 [4, 32, 1024], replicated, may hold values from -1 to 1
- attn_gain: float32 [1024], replicated, may hold values from 0.25 to 1.75
- w_query: bfloat16 [1024, 2048], replicated, may hold values from -0.1875 to 0.1875
- w_output: bfloat16 [2048, 1024], replicated, may hold values from -0.125 to 0.125
- out_gain: float32 [1024], replicated, may hold values from 0.25 to 1.75
- output_heads: float32 [4, 1024, 32], replicated, may hold values from -0.1875 to 0.1875
Outputs:
- grad_query: float32 [1024, 2048], P(('seq', 'batch'))
- grad_output: float32 [2048, 1024], P(('seq', 'batch'))
The draws below stay inside these ranges and needn't reach their ends.
All inputs are finite; a program needn't handle non-finite values.
Results may differ from the reference program's by a relative error of at most 0.035.
The reference program's roundings to bfloat16 on the way count: a program that leaves them out, or rounds other values in their place, can miss the bound.
Values sent between devices are 32-bit elements; how exact they have to be, the bound alone decides.
A program may use at most 64 MiB of HBM per device.

```python
import math
import jax
import jax.numpy as jnp
from jax import lax

D = 1024
HEADS = 8
HD = 256
ACT = 50
ADIM = 32
TSTEPS = 2
NEMB = 4
BLOCK = 128
PRE_DEV = 512
SAMPLES = 8
PREFIX = 32768
N_SEQ = 64


def draw_prefix_keys(key, part):
    shape = (SAMPLES, PREFIX, HD)
    first = jax.random.fold_in(key, 11)
    base = jnp.clip(jax.random.normal(first, shape, jnp.float32), -4.0, 4.0)
    return base.astype(jnp.bfloat16)


def set_ends(drawn, key, least, largest):
    extent = drawn.shape
    index_at = [jax.random.randint(jax.random.fold_in(key, axis), (), 0, extent[axis]) for axis in range(len(extent))]
    drawn = drawn.at[tuple(index_at)].set(least)
    longest = extent.index(max(extent))
    index_at[longest] = (index_at[longest] + 1) % extent[longest]
    return drawn.at[tuple(index_at)].set(largest)


def shard_levels(key, dims, split, low, top_value):
    def one(axis_at, parts):
        steps = jax.random.uniform(jax.random.fold_in(jax.random.fold_in(key, 6), axis_at), (parts,), jnp.float32, low / len(split), top_value / len(split))
        return jnp.repeat(jnp.exp(steps), dims[axis_at] // parts).reshape((-1,) + (1,) * (len(dims) - axis_at - 1))

    factor_of = one(*split[0])
    for cut in split[1:]:
        factor_of = factor_of * one(*cut)
    return factor_of


def normal_values(rng, dims, deviation, most, shards=(), kind=jnp.bfloat16):
    drawn = deviation * jax.random.normal(rng, dims, jnp.float32)
    if shards:
        drawn = drawn * shard_levels(rng, dims, shards, -0.22, 0.18)
    return jnp.clip(drawn, -most, most).astype(kind)


def setup_inputs(seed: int = 0) -> dict:
    key_of = jax.random.split(jax.random.key(seed), 14)
    actions = normal_values(key_of[0], (SAMPLES, ACT, ADIM), 1.0, 6.0, ((0, 4),), jnp.float32)
    noise = normal_values(key_of[1], (SAMPLES, TSTEPS, ACT, ADIM), 1.0, 6.0, ((0, 4),), jnp.float32)
    times = jnp.clip(0.05 + 0.9 * jax.random.uniform(key_of[2], (SAMPLES, TSTEPS), jnp.float32) ** shard_levels(key_of[2], (SAMPLES, TSTEPS), ((0, 4),), -0.2, 0.2), 0.05, 0.95)
    embodiment = set_ends(jax.random.randint(key_of[3], (SAMPLES,), 0, NEMB), jax.random.fold_in(key_of[3], 1), 0, NEMB - 1).astype(jnp.int32)
    prefix_blocks = set_ends(jax.random.randint(key_of[4], (SAMPLES,), 1, PREFIX // BLOCK + 1), jax.random.fold_in(key_of[4], 1), 1, (PREFIX // BLOCK + 1) - 1).astype(jnp.int32)
    prefix_keys = draw_prefix_keys(jax.random.fold_in(key_of[13], 71), 0)
    prefix_values = normal_values(key_of[6], (SAMPLES, PREFIX, HD), 1.0, 6.0, ((0, 4), (1, 64)))
    input_heads = normal_values(key_of[7], (NEMB, ADIM, D), ADIM ** -0.5, 1.0, (), jnp.float32)
    attn_gain = jnp.clip(1.0 + 0.15 * jax.random.normal(key_of[8], (D,), jnp.float32), 0.25, 1.75)
    w_query = normal_values(key_of[9], (D, HEADS * HD), D ** -0.5, 0.1875)
    w_output = normal_values(key_of[10], (HEADS * HD, D), (HEADS * HD) ** -0.5, 0.125)
    out_gain = jnp.clip(1.0 + 0.15 * jax.random.normal(key_of[11], (D,), jnp.float32), 0.25, 1.75)
    output_heads = normal_values(key_of[12], (NEMB, D, ADIM), D ** -0.5, 0.1875, (), jnp.float32)
    return {"actions": actions, "noise": noise, "times": times, "embodiment": embodiment, "prefix_blocks": prefix_blocks, "prefix_keys": prefix_keys, "prefix_values": prefix_values, "input_heads": input_heads, "attn_gain": attn_gain, "w_query": w_query, "w_output": w_output, "out_gain": out_gain, "output_heads": output_heads}


PRECISION_LEVEL = lax.Precision.HIGHEST

def embed_time(times):
    half_width = D // 2
    channel = jnp.arange(half_width, dtype=jnp.float32)
    frequency = jnp.exp(-math.log(10000.0) * channel / half_width)
    phase_list = times[..., None] * 1000.0 * frequency
    return jnp.concatenate([jnp.sin(phase_list), jnp.cos(phase_list)], -1)

def select_tables(embodiment, tables):
    one_hot_matrix = (embodiment[:, None] == jnp.arange(tables.shape[0], dtype=jnp.int32)[None, :]).astype(jnp.float32)
    return jnp.einsum('se,eab->sab', one_hot_matrix, tables, precision=PRECISION_LEVEL)

def rms_scale(values):
    return lax.rsqrt(lax.optimization_barrier(jnp.mean(values * values, -1, keepdims=True)) + 1e-06)

def reference(actions, noise, times, embodiment, prefix_blocks, prefix_keys, prefix_values, input_heads, attn_gain, w_query, w_output, out_gain, output_heads):
    samples = actions.shape[0]
    scale = 1.0 / math.sqrt(HD)
    level = times[:, :, None, None]
    noisy = level * noise + (1.0 - level) * actions[:, None]
    in_sel = select_tables(embodiment, input_heads)
    hidden = jnp.einsum('stac,scd->stad', noisy, in_sel, precision=PRECISION_LEVEL) + embed_time(times)[:, :, None, :]
    normed = (hidden * rms_scale(hidden) * attn_gain).astype(jnp.bfloat16)
    rows_normed = normed.reshape(-1, D)
    queries = (jnp.dot(rows_normed, w_query, preferred_element_type=jnp.float32) * scale).astype(jnp.bfloat16)
    queries = queries.reshape(samples, TSTEPS * ACT * HEADS, HD)
    positions = jnp.arange(PREFIX, dtype=jnp.int32)

    def softmax_parts(query_s, keys_s, count_s):
        scores = jnp.dot(query_s, keys_s.T, preferred_element_type=jnp.float32)
        valid = (positions < BLOCK * count_s)[None, :]
        peak = lax.optimization_barrier(jnp.max(jnp.where(valid, scores, -1e+30), -1, keepdims=True))
        weights = jnp.where(valid, jnp.exp(scores - peak), 0.0)
        totals = lax.optimization_barrier(jnp.sum(weights, -1, keepdims=True))
        return (weights, totals)

    def forward_one(items):
        query_s, keys_s, value_shards, count_s = items
        weights, totals = softmax_parts(query_s, keys_s, count_s)
        partial_sum = jnp.dot(weights.astype(jnp.bfloat16), value_shards, preferred_element_type=jnp.float32)
        return (partial_sum / totals).astype(jnp.bfloat16)
    mixed = lax.map(forward_one, (queries, prefix_keys, prefix_values, prefix_blocks))
    attn_rows = mixed.reshape(-1, HEADS * HD)
    hidden_rows = hidden.reshape(-1, D)
    resid = hidden_rows + jnp.dot(attn_rows, w_output, preferred_element_type=jnp.float32)
    inverse = rms_scale(resid)
    out_normed = resid * inverse * out_gain
    out_sel = select_tables(embodiment, output_heads)
    velocity = jnp.einsum('srd,sdc->src', out_normed.reshape(samples, TSTEPS * ACT, D), out_sel, precision=PRECISION_LEVEL)
    target = (noise - actions[:, None]).reshape(samples, TSTEPS * ACT, ADIM)
    dvel = 2.0 * (velocity - target) / (samples * TSTEPS * ACT)
    dnormed = jnp.einsum('src,sdc->srd', dvel, out_sel, precision=PRECISION_LEVEL).reshape(-1, D)
    scaled = dnormed * out_gain
    dresid = inverse * scaled - inverse ** 3 * resid * lax.optimization_barrier(jnp.mean(resid * scaled, -1, keepdims=True))
    dresid_b = dresid.astype(jnp.bfloat16)
    dattn = jnp.dot(dresid_b, w_output.T, preferred_element_type=jnp.float32)
    raw_output = jnp.dot(attn_rows.T, dresid_b, preferred_element_type=jnp.float32)
    dattn_heads = dattn.reshape(samples, TSTEPS * ACT * HEADS, HD)
    delta = lax.optimization_barrier(jnp.sum(dattn_heads * mixed.astype(jnp.float32), -1))
    dattn_b = dattn_heads.astype(jnp.bfloat16)

    def backward_one(items):
        query_s, keys_s, value_shards, count_s, grad_s, delta_s = items
        weights, totals = softmax_parts(query_s, keys_s, count_s)
        dvalues = jnp.dot(grad_s, value_shards.T, preferred_element_type=jnp.float32)
        dscore = (weights / totals * (dvalues - delta_s[:, None])).astype(jnp.bfloat16)
        blocked_layout = dscore.reshape(-1, N_SEQ, PRE_DEV).astype(jnp.float32)
        key_block_list = keys_s.reshape(N_SEQ, PRE_DEV, HD).astype(jnp.float32)
        piece_list = jnp.einsum('fmy,myo->mfo', blocked_layout, key_block_list, precision=PRECISION_LEVEL)
        piece_list = (piece_list * scale).astype(jnp.bfloat16)
        return lax.optimization_barrier(jnp.sum(piece_list.astype(jnp.float32), 0))
    grad_heads = lax.map(backward_one, (queries, prefix_keys, prefix_values, prefix_blocks, dattn_b, delta))
    grad_rows = grad_heads.reshape(-1, HEADS * HD)
    raw_query = jnp.dot(rows_normed.astype(jnp.float32).T, grad_rows, precision=PRECISION_LEVEL)
    norm_value = jnp.sqrt(jnp.sum(raw_query * raw_query) + jnp.sum(raw_output * raw_output))
    factor = jnp.minimum(1.0, 1.0 / (norm_value + 1e-06))
    return (raw_query * factor, raw_output * factor)
```

```python
import math

import jax
import jax.numpy as jnp
from jax import lax
from jax.experimental import pallas as pl
from jax.experimental.pallas import tpu as pltpu
from jax.sharding import Mesh
from jax.sharding import PartitionSpec as P

D = 1024
HEADS = 8
HD = 256
ACT = 50
ADIM = 32
TSTEPS = 2
BLOCK = 128
ROWS = TSTEPS * ACT
PAD = 112
ALL = 2 * PAD
KEYS = 512
NZ = 8
NX = 4
NB = 4
ZT = 7
SEQ = ("seq_0", "seq_1", "seq_2")
SEQ_BATCH = ("seq_0", "seq_1", "seq_2", "batch")
HIGHEST = lax.Precision.HIGHEST
MESH = pl.DeviceIdType.MESH
F32 = jnp.float32
BF16 = jnp.bfloat16
VMEM = pl.BlockSpec(memory_space=pltpu.VMEM)
SMEM = pl.BlockSpec(memory_space=pltpu.SMEM)


def embed_time(times):
    half_width = D // 2
    channel = jnp.arange(half_width, dtype=F32)
    frequency = jnp.exp(-math.log(10000.0) * channel / half_width)
    phase = times[..., None] * 1000.0 * frequency
    return jnp.concatenate([jnp.sin(phase), jnp.cos(phase)], -1)


def dot_nt(a, b):
    return lax.dot_general(a, b, (((1,), (1,)), ((), ())), preferred_element_type=F32)


def dot_tn(a, b):
    return lax.dot_general(a, b, (((0,), (0,)), ((), ())), preferred_element_type=F32)


def lanes_of(shape=(8, 128)):
    return lax.broadcasted_iota(jnp.int32, shape, len(shape) - 1)


def forward_kernel(lim_ref, nrm_ref, wq_ref, k_ref, v_ref, p_ref, s_ref, m_ref):
    lane = lanes_of()
    for c in range(2):
        q = jnp.dot(nrm_ref[...], wq_ref[:, c * 1024 : (c + 1) * 1024], preferred_element_type=F32)
        q = (q * (1.0 / math.sqrt(HD))).astype(BF16)
        for s in range(2):
            qs = jnp.concatenate(
                [q[s * PAD : (s + 1) * PAD, h * HD : (h + 1) * HD] for h in range(4)], axis=0
            )
            scores = dot_nt(qs, k_ref[s])
            valid = lax.broadcasted_iota(jnp.int32, scores.shape, 1) < lim_ref[s]
            scores = jnp.where(valid, scores, -1e30)
            peak = jnp.max(scores, axis=1, keepdims=True)
            weights = jnp.where(valid, jnp.exp(scores - peak), 0.0)
            total = jnp.sum(weights, axis=1, keepdims=True)
            mixed = jnp.dot(weights.astype(BF16), v_ref[s], preferred_element_type=F32)
            for h in range(4):
                p_ref[4 * c + h, s * PAD : (s + 1) * PAD, :] = weights[h * PAD : (h + 1) * PAD]
            for x in (2 * s, 2 * s + 1):
                peaks = jnp.zeros((8, 128), F32)
                totals = jnp.ones((8, 128), F32)
                for z in range(ZT):
                    for h in range(4):
                        j = z * 4 + h
                        row = h * PAD + (7 * x + z - 14 * s) * 8
                        peaks = jnp.where(lane == j, peak[row : row + 8], peaks)
                        totals = jnp.where(lane == j, total[row : row + 8], totals)
                        s_ref[c, x, 2 * j] = mixed[row : row + 8, :128]
                        s_ref[c, x, 2 * j + 1] = mixed[row : row + 8, 128:]
                s_ref[c, x, 56] = peaks
                s_ref[c, x, 57] = totals
                m_ref[c, x] = peaks


def merge(out, parts, count):
    peaks = [p[2 * count] for p in parts]
    top = peaks[0]
    for one in peaks[1:]:
        top = jnp.maximum(top, one)
    scales = [jnp.exp(one - top) for one in peaks]
    total = scales[0] * parts[0][2 * count + 1]
    for scale, p in zip(scales[1:], parts[1:]):
        total = total + scale * p[2 * count + 1]
    for j in range(count):
        columns = [jnp.broadcast_to(scale[:, j : j + 1], (8, 128)) for scale in scales]
        for half in range(2):
            value = columns[0] * parts[0][2 * j + half]
            for column, p in zip(columns[1:], parts[1:]):
                value = value + column * p[2 * j + half]
            out(2 * j + half, value)
    return top, total


def mix_kernel(
    s_ref, hid_ref, tgt_ref, heads_ref, gain_ref, wo_ref, g_ref,
    cbuf, acc, xbuf, zsend, zbuf, psend, prec, attn_all, agsend, gath,
    c_send, c_recv, x_send, x_recv, z_send, z_recv, p_send, p_recv,
    gz_send, gz_recv, gx_send, gx_recv, gc_send, gc_recv,
):
    z = lax.axis_index("seq_0")
    x = lax.axis_index("seq_1")
    c = lax.axis_index("seq_2")
    other = 1 - c
    lane = lanes_of()
    barrier = pltpu.get_barrier_semaphore()
    pl.semaphore_signal(barrier, inc=1, device_id={"seq_2": other}, device_id_type=MESH)
    for d in range(1, NX):
        pl.semaphore_signal(barrier, inc=1, device_id={"seq_1": lax.rem(x + d, NX)}, device_id_type=MESH)
    for d in range(1, NZ):
        pl.semaphore_signal(barrier, inc=1, device_id={"seq_0": lax.rem(z + d, NZ)}, device_id_type=MESH)
    pl.semaphore_wait(barrier, 1 + NX - 1 + NZ - 1)

    def core_copy(d):
        chunk = lax.rem(x + d, NX)
        return pltpu.make_async_remote_copy(
            src_ref=s_ref.at[other, chunk], dst_ref=cbuf.at[chunk],
            send_sem=c_send.at[d], recv_sem=c_recv.at[d],
            device_id={"seq_2": other}, device_id_type=MESH,
        )

    def x_copy(d):
        return pltpu.make_async_remote_copy(
            src_ref=acc.at[lax.rem(x + d, NX)], dst_ref=xbuf.at[x],
            send_sem=x_send.at[d], recv_sem=x_recv.at[d],
            device_id={"seq_1": lax.rem(x + d, NX)}, device_id_type=MESH,
        )

    def x_arrival(d):
        source = lax.rem(x + NX - d, NX)
        return pltpu.make_async_remote_copy(
            src_ref=acc.at[source], dst_ref=xbuf.at[source],
            send_sem=x_send.at[d], recv_sem=x_recv.at[d],
            device_id={"seq_1": source}, device_id_type=MESH,
        )

    order = (2, 1, 3, 0)
    for d in order:
        core_copy(d).start()
    for d in order:
        core_copy(d).wait_recv()
        chunk = lax.rem(x + d, NX)
        target = acc.at[chunk]

        def put(i, value):
            target[i] = value

        top, total = merge(put, (s_ref.at[c, chunk], cbuf.at[chunk]), 28)
        target[56] = top
        target[57] = total
        if d:
            x_copy(d).start()
    for d in (1, 3, 2):
        x_arrival(d).wait_recv()
    parts = [acc.at[x]] + [xbuf.at[lax.rem(x + NX - d, NX)] for d in range(1, NX)]

    def put_z(i, value):
        zsend[i // 8, i % 8] = value

    top, total = merge(put_z, parts, 28)
    for zz in range(ZT):
        t = top if zz == 0 else pltpu.roll(top, 128 - 4 * zz, axis=1)
        shift = (32 - 4 * zz) % 128
        l = pltpu.roll(total, shift, axis=1)
        zsend[zz, 8] = jnp.where(lane < 32, t, l)

    def z_copy(d):
        peer = lax.rem(z + d, NZ)
        return peer, pltpu.make_async_remote_copy(
            src_ref=zsend.at[jnp.minimum(peer, ZT - 1)], dst_ref=zbuf.at[z],
            send_sem=z_send.at[d], recv_sem=z_recv.at[d],
            device_id={"seq_0": peer}, device_id_type=MESH,
        )

    def z_arrival(d):
        source = lax.rem(z + NZ - d, NZ)
        return pltpu.make_async_remote_copy(
            src_ref=zsend.at[0], dst_ref=zbuf.at[source],
            send_sem=z_send.at[d], recv_sem=z_recv.at[d],
            device_id={"seq_0": source}, device_id_type=MESH,
        )

    for d in (4, 3, 5, 2, 6, 1, 7):
        peer, copy = z_copy(d)

        @pl.when(peer < ZT)
        def _():
            copy.start()

    def ag_copy(d):
        peer = lax.rem(z + d, NZ)
        return pltpu.make_async_remote_copy(
            src_ref=agsend.at[peer], dst_ref=gath.at[c, x, jnp.minimum(z, ZT - 1)],
            send_sem=gz_send.at[d], recv_sem=gz_recv.at[d],
            device_id={"seq_0": peer}, device_id_type=MESH,
        )

    def ag_arrival(d):
        source = lax.rem(z + NZ - d, NZ)
        return source, pltpu.make_async_remote_copy(
            src_ref=agsend.at[0], dst_ref=gath.at[c, x, jnp.minimum(source, ZT - 1)],
            send_sem=gz_send.at[d], recv_sem=gz_recv.at[d],
            device_id={"seq_0": source}, device_id_type=MESH,
        )

    pair = pltpu.make_async_remote_copy(
        src_ref=psend, dst_ref=prec, send_sem=p_send, recv_sem=p_recv,
        device_id={"seq_2": other}, device_id_type=MESH,
    )

    @pl.when(z < ZT)
    def _():
        for d in range(1, NZ):
            z_arrival(d).wait_recv()
        sources = [zsend.at[jnp.minimum(z, ZT - 1)]] + [
            zbuf.at[lax.rem(z + NZ - d, NZ)] for d in range(1, NZ)
        ]
        stats = [p[8] for p in sources]
        top = stats[0]
        for one in stats[1:]:
            top = jnp.maximum(top, one)
        scales = [jnp.exp(one - top) for one in stats]
        moved = [pltpu.roll(one, 96, axis=1) for one in stats]
        total = scales[0] * moved[0]
        for scale, one in zip(scales[1:], moved[1:]):
            total = total + scale * one
        first = c == 0
        products = []
        for h in range(4):
            columns = [jnp.broadcast_to(scale[:, h : h + 1], (8, 128)) for scale in scales]
            whole = jnp.broadcast_to(total[:, h : h + 1], (8, 128))
            halves = []
            for half in range(2):
                value = columns[0] * sources[0][2 * h + half]
                for column, p in zip(columns[1:], sources[1:]):
                    value = value + column * p[2 * h + half]
                halves.append((value / whole).astype(BF16))
            attn = jnp.concatenate(halves, axis=1)
            start = pl.multiple_of(c * 1024 + h * HD, HD)
            products.append(
                jnp.dot(attn, wo_ref[pl.ds(start, HD), :], preferred_element_type=F32)
            )
            low, high = halves[0].astype(F32), halves[1].astype(F32)
            attn_all[4 * c + h] = jnp.where(first, low, high)
            psend[8 + h] = jnp.where(first, high, low)
        partial = products[0] + products[1] + products[2] + products[3]
        for i in range(8):
            psend[i] = partial[:, i * 128 : (i + 1) * 128]
        pair.start()
        tile = 7 * x + jnp.minimum(z, ZT - 1)
        hid = hid_ref[tile]
        sample = x // 2
        pair.wait_recv()
        resid = hid + (partial + jnp.concatenate([prec[i] for i in range(8)], axis=1))
        inverse = lax.rsqrt(jnp.mean(resid * resid, axis=1, keepdims=True) + 1e-06)
        gain = gain_ref[...]
        normed = resid * inverse * gain
        target = tgt_ref[tile]
        place = (tile - 14 * sample) * 8 + lax.broadcasted_iota(jnp.int32, (8, 1), 0)
        real = place < ROWS
        back = jnp.zeros((8, D), F32)
        for j in range(ADIM):
            head = heads_ref[sample, j : j + 1, :]
            velocity = jnp.sum(normed * head, axis=1, keepdims=True)
            dvel = 2.0 * (velocity - target[:, j : j + 1]) / (8 * ROWS)
            back = back + jnp.where(real, dvel, 0.0) * head
        scaled = back * gain
        mean = jnp.mean(resid * scaled, axis=1, keepdims=True)
        dresid = inverse * scaled - inverse * inverse * inverse * resid * mean
        dresid = dresid.astype(BF16).astype(F32)
        stats = jnp.where(lane < 32, top, pltpu.roll(total, 32, axis=1))
        for h in range(4):
            delta = jnp.sum(products[h] * dresid, axis=1, keepdims=True)
            stats = jnp.where(lane == 64 + h, delta, stats)
        own = jnp.where(first, dresid[:, :512], dresid[:, 512:])
        for h in range(4):
            attn_all[4 * other + h] = prec[8 + h]
        for peer in range(NZ):
            for i in range(4):
                agsend[peer, i] = own[:, i * 128 : (i + 1) * 128]
            agsend[peer, 4] = stats
            agsend[peer, 5] = attn_all[peer]
        gath[c, x, jnp.minimum(z, ZT - 1)] = agsend[z]
        for d in (4, 3, 5, 2, 6, 1, 7):
            ag_copy(d).start()

    for d in range(1, NZ):
        source, copy = ag_arrival(d)

        @pl.when(source < ZT)
        def _():
            copy.wait_recv()

    def gx_copy(d):
        return pltpu.make_async_remote_copy(
            src_ref=gath.at[c, x], dst_ref=gath.at[c, x],
            send_sem=gx_send.at[d], recv_sem=gx_recv.at[d],
            device_id={"seq_1": lax.rem(x + d, NX)}, device_id_type=MESH,
        )

    def gx_arrival(d):
        source = lax.rem(x + NX - d, NX)
        return pltpu.make_async_remote_copy(
            src_ref=gath.at[c, x], dst_ref=gath.at[c, source],
            send_sem=gx_send.at[d], recv_sem=gx_recv.at[d],
            device_id={"seq_1": source}, device_id_type=MESH,
        )

    def gc_copy(d):
        chunk = lax.rem(x + NX - d, NX)
        return pltpu.make_async_remote_copy(
            src_ref=gath.at[c, chunk], dst_ref=gath.at[c, chunk],
            send_sem=gc_send.at[d], recv_sem=gc_recv.at[d],
            device_id={"seq_2": other}, device_id_type=MESH,
        )

    def gc_arrival(d):
        chunk = lax.rem(x + NX - d, NX)
        return pltpu.make_async_remote_copy(
            src_ref=gath.at[c, chunk], dst_ref=gath.at[other, chunk],
            send_sem=gc_send.at[d], recv_sem=gc_recv.at[d],
            device_id={"seq_2": other}, device_id_type=MESH,
        )

    for d in (2, 1, 3):
        gx_copy(d).start()
    gc_copy(0).start()
    for d in (1, 3, 2):
        gx_arrival(d).wait_recv()
        gc_copy(d).start()
    for d in range(NX):
        gc_arrival(d).wait_recv()
    g_ref[...] = gath[...]
    for d in order:
        core_copy(d).wait_send()
        if d:
            x_copy(d).wait_send()
            gx_copy(d).wait_send()
        gc_copy(d).wait_send()
    for d in range(1, NZ):
        peer, copy = z_copy(d)

        @pl.when(peer < ZT)
        def _():
            copy.wait_send()

    @pl.when(z < ZT)
    def _():
        pair.wait_send()
        for d in range(1, NZ):
            ag_copy(d).wait_send()


def backward_kernel(x_smem, g_ref, m_ref, p_ref, k_ref, v_ref, wo_ref, gq_ref, ro_ref, db, scale_ref, delta_ref, az, ro_all):
    half_core = x_smem[0]
    offset = x_smem[1]
    for t in range(0, 28, 2):
        for core in range(2):
            for i in range(4):
                both = jnp.concatenate(
                    [g_ref[core, u // 7, u % 7, i] for u in (t, t + 1)], axis=0
                )
                lo = core * 512 + i * 128
                db[t * 8 : t * 8 + 16, lo : lo + 128] = both.astype(BF16)
        both = jnp.concatenate([g_ref[half_core, u // 7, u % 7, 5] for u in (t, t + 1)], axis=0)
        az[t * 8 : t * 8 + 16, :] = both.astype(BF16)
    for core in range(2):
        for t in range(28):
            x, z = t // 7, t % 7
            stats = g_ref[core, x, z, 4]
            local = m_ref[core, x]
            if z:
                local = pltpu.roll(local, 128 - 4 * z, axis=1)
            total = pltpu.roll(stats, 96, axis=1)
            scale = jnp.exp(local - stats) / total
            for h in range(4):
                scale_ref[4 * core + h, t * 8 : t * 8 + 8] = jnp.broadcast_to(
                    scale[:, h : h + 1], (8, 128)
                )
                delta_ref[4 * core + h, t * 8 : t * 8 + 8] = jnp.broadcast_to(
                    stats[:, 64 + h : 65 + h], (8, 128)
                )
    for c in range(2):
        dattn = dot_nt(db[...], wo_ref[c * 1024 : (c + 1) * 1024, :]).astype(BF16)
        for s in range(2):
            rows = slice(s * PAD, (s + 1) * PAD)
            stacked = jnp.concatenate(
                [dattn[rows, h * HD : (h + 1) * HD] for h in range(4)], axis=0
            )
            dvalues = dot_nt(stacked, v_ref[s])
            parts = []
            for h in range(4):
                n = 4 * c + h
                delta = delta_ref[n, rows]
                scale = scale_ref[n, rows]
                line = []
                for i in range(4):
                    cols = slice(i * 128, (i + 1) * 128)
                    dv = dvalues[h * PAD : (h + 1) * PAD, cols]
                    line.append((p_ref[n, rows, cols] * scale * (dv - delta)).astype(BF16))
                parts.append(jnp.concatenate(line, axis=1))
            dscore = jnp.concatenate(parts, axis=0)
            gq = jnp.dot(dscore, k_ref[s], preferred_element_type=F32) * (1.0 / math.sqrt(HD))
            gq = gq.astype(BF16).astype(F32)
            for h in range(4):
                gq_ref[4 * c + h, rows, :] = gq[h * PAD : (h + 1) * PAD]
    ro_all[...] = dot_tn(az[...], db[...])
    for b in range(NB):
        ro_ref[b] = ro_all[pl.ds(pl.multiple_of(offset + 8 * b, 8), 8), :]


def grad_kernel(
    gq_ref, ro_ref, nz_ref, q_out, o_out,
    cbuf, acc, xbuf, zsend, zbuf, zsum, full, rsend, drec, yrec, e_send, e_rec, f_send, f_rec,
    c_ss, c_rs, x_ss, x_rs, z_ss, z_rs, g_ss, g_rs, y_ss, y_rs, d_ss, d_rs, e_ss, e_rs, f_ss, f_rs,
):
    z = lax.axis_index("seq_0")
    x = lax.axis_index("seq_1")
    c = lax.axis_index("seq_2")
    b = lax.axis_index("batch")
    other = 1 - c
    me = x * 8 + c * 4 + b

    def plane(k):
        return {"seq_1": k // 8, "seq_2": lax.rem(k // 4, 2), "batch": lax.rem(k, 4)}

    barrier = pltpu.get_barrier_semaphore()

    @pl.loop(1, 32)
    def _(d):
        pl.semaphore_signal(barrier, inc=1, device_id=plane(lax.rem(me + d, 32)), device_id_type=MESH)

    for d in range(1, NZ):
        pl.semaphore_signal(barrier, inc=1, device_id={"seq_0": lax.rem(z + d, NZ)}, device_id_type=MESH)
    pl.semaphore_wait(barrier, 31 + NZ - 1)

    def remote(src, dst, ss, rs, device):
        return pltpu.make_async_remote_copy(
            src_ref=src, dst_ref=dst, send_sem=ss, recv_sem=rs, device_id=device, device_id_type=MESH
        )

    def core_copy(d):
        h = lax.rem(x + d, NX)
        return remote(gq_ref.at[4 * other + h], cbuf.at[h], c_ss.at[d], c_rs.at[d], {"seq_2": other})

    def x_copy(d):
        peer = lax.rem(x + d, NX)
        return remote(acc.at[peer], xbuf.at[x], x_ss.at[d], x_rs.at[d], {"seq_1": peer})

    def x_arrival(d):
        peer = lax.rem(x + NX - d, NX)
        return remote(acc.at[peer], xbuf.at[peer], x_ss.at[d], x_rs.at[d], {"seq_1": peer})

    def y_copy(d):
        peer = lax.rem(b + d, NB)
        return remote(ro_ref.at[peer], yrec.at[b], y_ss.at[d], y_rs.at[d], {"batch": peer})

    def y_arrival(d):
        peer = lax.rem(b + NB - d, NB)
        return remote(ro_ref.at[peer], yrec.at[peer], y_ss.at[d], y_rs.at[d], {"batch": peer})

    order = (2, 1, 3, 0)
    for d in order:
        core_copy(d).start()
    for d in range(1, NB):
        y_copy(d).start()
    for d in order:
        core_copy(d).wait_recv()
        h = lax.rem(x + d, NX)
        acc[h] = gq_ref[4 * c + h] + cbuf[h]
        if d:
            x_copy(d).start()
    for d in (1, 3, 2):
        x_arrival(d).wait_recv()
    summed = acc[x]
    for d in range(1, NX):
        summed = summed + xbuf[lax.rem(x + NX - d, NX)]
    for zz in range(ZT):
        zsend[zz] = summed[zz * 32 : (zz + 1) * 32]

    def z_copy(d):
        peer = lax.rem(z + d, NZ)
        src = zsend.at[jnp.minimum(peer, ZT - 1)]
        return peer, remote(src, zbuf.at[z], z_ss.at[d], z_rs.at[d], {"seq_0": peer})

    def z_arrival(d):
        peer = lax.rem(z + NZ - d, NZ)
        return remote(zsend.at[0], zbuf.at[peer], z_ss.at[d], z_rs.at[d], {"seq_0": peer})

    def g_copy(d):
        peer = lax.rem(z + d, NZ)
        mine = jnp.minimum(z, ZT - 1)
        return remote(zsum, full.at[mine], g_ss.at[d], g_rs.at[d], {"seq_0": peer})

    def g_arrival(d):
        peer = lax.rem(z + NZ - d, NZ)
        slot = full.at[jnp.minimum(peer, ZT - 1)]
        return peer, remote(zsum, slot, g_ss.at[d], g_rs.at[d], {"seq_0": peer})

    for d in (4, 3, 5, 2, 6, 1, 7):
        peer, copy = z_copy(d)

        @pl.when(peer < ZT)
        def _():
            copy.start()

    @pl.when(z < ZT)
    def _():
        mine = jnp.minimum(z, ZT - 1)
        for d in range(1, NZ):
            z_arrival(d).wait_recv()
        value = zsend[mine]
        for d in range(1, NZ):
            value = value + zbuf[lax.rem(z + NZ - d, NZ)]
        zsum[...] = value
        for d in (4, 3, 5, 2, 6, 1, 7):
            g_copy(d).start()
        full[mine] = value

    for d in range(1, NZ):
        peer, copy = g_arrival(d)

        @pl.when(peer < ZT)
        def _():
            copy.wait_recv()

    grads = jnp.concatenate([full[i] for i in range(ZT)], axis=0)
    high = grads.astype(BF16)
    rest = grads - high.astype(F32)
    middle = rest.astype(BF16)
    low = (rest - middle.astype(F32)).astype(BF16)
    nz = nz_ref[...]
    raw = jnp.dot(nz, high, preferred_element_type=F32) + (
        jnp.dot(nz, middle, preferred_element_type=F32) + jnp.dot(nz, low, preferred_element_type=F32)
    )
    for k in range(32):
        rsend[k] = raw[4 * k : 4 * k + 4]

    def d_copy(d):
        peer = lax.rem(me + d, 32)
        return remote(rsend.at[peer], drec.at[me], d_ss.at[d], d_rs.at[d], plane(peer))

    def d_arrival(d):
        peer = lax.rem(me + 32 - d, 32)
        return remote(rsend.at[peer], drec.at[peer], d_ss.at[d], d_rs.at[d], plane(peer))

    @pl.loop(1, 32)
    def _(d):
        d_copy(d).start()

    drec[me] = rsend[me]
    for d in range(1, NB):
        y_arrival(d).wait_recv()
    yrec[b] = ro_ref[b]
    raw_o = yrec[0] + yrec[1] + yrec[2] + yrec[3]

    @pl.loop(1, 32)
    def _(d):
        d_arrival(d).wait_recv()

    blocks = []
    for h in range(HEADS):
        base = (h % 4) * 8 + (h // 4) * 4
        blocks.append(drec[base] + drec[base + 1] + drec[base + 2] + drec[base + 3])
    raw_q = jnp.concatenate(blocks, axis=1)
    squares = jnp.sum(raw_q * raw_q, keepdims=True) + jnp.sum(raw_o * raw_o, keepdims=True)
    e_send[...] = jnp.broadcast_to(squares, (8, 128))

    def e_copy(d):
        return remote(e_send, e_rec.at[me], e_ss.at[d], e_rs.at[d], plane(lax.rem(me + d, 32)))

    def e_arrival(d):
        peer = lax.rem(me + 32 - d, 32)
        return remote(e_send, e_rec.at[peer], e_ss.at[d], e_rs.at[d], plane(peer))

    @pl.loop(1, 32)
    def _(d):
        e_copy(d).start()

    e_rec[me] = e_send[...]

    @pl.loop(1, 32)
    def _(d):
        e_arrival(d).wait_recv()

    f_send[...] = jnp.sum(e_rec[...], axis=0)

    def f_copy(d):
        return remote(f_send, f_rec.at[z], f_ss.at[d], f_rs.at[d], {"seq_0": lax.rem(z + d, NZ)})

    def f_arrival(d):
        peer = lax.rem(z + NZ - d, NZ)
        return remote(f_send, f_rec.at[peer], f_ss.at[d], f_rs.at[d], {"seq_0": peer})

    for d in range(1, NZ):
        f_copy(d).start()
    f_rec[z] = f_send[...]
    for d in range(1, NZ):
        f_arrival(d).wait_recv()
    norm = jnp.sqrt(jnp.sum(f_rec[...], axis=0))
    factor = jnp.minimum(1.0, 1.0 / (norm + 1e-06))
    q_out[...] = raw_q * factor[0:1, 0:1]
    o_out[...] = raw_o * factor[0:1, 0:1]
    for d in range(NX):
        core_copy(d).wait_send()
        if d:
            x_copy(d).wait_send()
            y_copy(d).wait_send()
    for d in range(1, NZ):
        f_copy(d).wait_send()
        peer, copy = z_copy(d)

        @pl.when(peer < ZT)
        def _():
            copy.wait_send()

        @pl.when(z < ZT)
        def _():
            g_copy(d).wait_send()

    @pl.loop(1, 32)
    def _(d):
        d_copy(d).wait_send()
        e_copy(d).wait_send()


def local(
    actions,
    noise,
    times,
    embodiment,
    prefix_blocks,
    prefix_keys,
    prefix_values,
    input_heads,
    attn_gain,
    w_query,
    w_output,
    out_gain,
    output_heads,
):
    sz = lax.axis_index("seq_0")
    sx = lax.axis_index("seq_1")
    sc = lax.axis_index("seq_2")
    level = times[:, :, None, None]
    noisy = level * noise + (1.0 - level) * actions[:, None]
    one_hot = (embodiment[:, None] == jnp.arange(4, dtype=jnp.int32)[None, :]).astype(F32)
    in_sel = jnp.einsum("se,eab->sab", one_hot, input_heads, precision=HIGHEST)
    heads_t = jnp.einsum("se,eab->sba", one_hot, output_heads, precision=HIGHEST)
    hidden = (
        jnp.einsum("stac,scd->stad", noisy, in_sel, precision=HIGHEST)
        + embed_time(times)[:, :, None, :]
    ).reshape(2, ROWS, D)
    inverse = lax.rsqrt(jnp.mean(hidden * hidden, -1, keepdims=True) + 1e-06)
    normed = (hidden * inverse * attn_gain).astype(BF16)
    normed = jnp.pad(normed, ((0, 0), (0, PAD - ROWS), (0, 0))).reshape(ALL, D)
    hid = jnp.pad(hidden, ((0, 0), (0, PAD - ROWS), (0, 0))).reshape(28, 8, D)
    target = (noise - actions[:, None]).reshape(2, ROWS, ADIM)
    target = jnp.pad(target, ((0, 0), (0, PAD - ROWS), (0, 0))).reshape(28, 8, ADIM)
    nz = lax.dynamic_slice_in_dim(normed, sz * 128, 128, 1).T
    limit = BLOCK * prefix_blocks - ((sz * NX + sx) * 2 + sc) * KEYS
    params = dict(vmem_limit_bytes=48 * 1024 * 1024)
    weights, sums, peaks = pl.pallas_call(
        forward_kernel,
        out_shape=(
            jax.ShapeDtypeStruct((HEADS, ALL, KEYS), F32),
            jax.ShapeDtypeStruct((2, NX, 58, 8, 128), F32),
            jax.ShapeDtypeStruct((2, NX, 8, 128), F32),
        ),
        in_specs=[SMEM, VMEM, VMEM, VMEM, VMEM],
        out_specs=(VMEM, VMEM, VMEM),
        compiler_params=pltpu.CompilerParams(**params),
    )(limit, normed, w_query, prefix_keys, prefix_values)
    dma = pltpu.SemaphoreType.DMA
    gathered = pl.pallas_call(
        mix_kernel,
        out_shape=jax.ShapeDtypeStruct((2, NX, ZT, 6, 8, 128), F32),
        in_specs=[VMEM] * 6,
        out_specs=VMEM,
        scratch_shapes=[
            pltpu.VMEM((NX, 58, 8, 128), F32),
            pltpu.VMEM((NX, 58, 8, 128), F32),
            pltpu.VMEM((NX, 58, 8, 128), F32),
            pltpu.VMEM((ZT, 9, 8, 128), F32),
            pltpu.VMEM((NZ, 9, 8, 128), F32),
            pltpu.VMEM((12, 8, 128), F32),
            pltpu.VMEM((12, 8, 128), F32),
            pltpu.VMEM((8, 8, 128), F32),
            pltpu.VMEM((NZ, 6, 8, 128), F32),
            pltpu.VMEM((2, NX, ZT, 6, 8, 128), F32),
            dma((NX,)), dma((NX,)), dma((NX,)), dma((NX,)), dma((NZ,)), dma((NZ,)), dma, dma,
            dma((NZ,)), dma((NZ,)), dma((NX,)), dma((NX,)), dma((NX,)), dma((NX,)),
        ],
        compiler_params=pltpu.CompilerParams(collective_id=0, has_side_effects=True, **params),
    )(sums, hid, target, heads_t, out_gain[None, :], w_output)
    where = jnp.stack([sx // 2, lax.rem(sx, 2) * 64 + sc * 32]).astype(jnp.int32)
    grads, outer = pl.pallas_call(
        backward_kernel,
        out_shape=(
            jax.ShapeDtypeStruct((HEADS, ALL, HD), F32),
            jax.ShapeDtypeStruct((NB, 8, D), F32),
        ),
        in_specs=[SMEM] + [VMEM] * 6,
        out_specs=(VMEM, VMEM),
        scratch_shapes=[
            pltpu.VMEM((ALL, D), BF16),
            pltpu.VMEM((HEADS, ALL, 128), F32),
            pltpu.VMEM((HEADS, ALL, 128), F32),
            pltpu.VMEM((ALL, 128), BF16),
            pltpu.VMEM((128, D), F32),
        ],
        compiler_params=pltpu.CompilerParams(**params),
    )(where, gathered, peaks, weights, prefix_keys, prefix_values, w_output)
    return pl.pallas_call(
        grad_kernel,
        out_shape=(
            jax.ShapeDtypeStruct((4, HEADS * HD), F32),
            jax.ShapeDtypeStruct((8, D), F32),
        ),
        in_specs=[VMEM] * 3,
        out_specs=(VMEM, VMEM),
        scratch_shapes=[
            pltpu.VMEM((NX, ALL, HD), F32),
            pltpu.VMEM((NX, ALL, HD), F32),
            pltpu.VMEM((NX, ALL, HD), F32),
            pltpu.VMEM((ZT, 32, HD), F32),
            pltpu.VMEM((NZ, 32, HD), F32),
            pltpu.VMEM((32, HD), F32),
            pltpu.VMEM((ZT, 32, HD), F32),
            pltpu.VMEM((32, 4, HD), F32),
            pltpu.VMEM((32, 4, HD), F32),
            pltpu.VMEM((NB, 8, D), F32),
            pltpu.VMEM((8, 128), F32),
            pltpu.VMEM((32, 8, 128), F32),
            pltpu.VMEM((8, 128), F32),
            pltpu.VMEM((NZ, 8, 128), F32),
            dma((NX,)), dma((NX,)), dma((NX,)), dma((NX,)), dma((NZ,)), dma((NZ,)), dma((NZ,)), dma((NZ,)),
            dma((NB,)), dma((NB,)), dma((32,)), dma((32,)), dma((32,)), dma((32,)), dma((NZ,)), dma((NZ,)),
        ],
        compiler_params=pltpu.CompilerParams(collective_id=1, has_side_effects=True, **params),
    )(grads, outer, nz)


def solution(mesh):
    torus = Mesh(
        mesh.devices.reshape(NZ, NX, 2, mesh.shape["batch"]), ("seq_0", "seq_1", "seq_2", "batch")
    )
    placed = (
        P("batch", None, None),
        P("batch", None, None, None),
        P("batch", None),
        P("batch"),
        P("batch"),
        P("batch", SEQ, None),
        P("batch", SEQ, None),
        P(),
        P(),
        P(),
        P(),
        P(),
        P(),
    )
    return jax.shard_map(
        local,
        mesh=torus,
        in_specs=placed,
        out_specs=(P(SEQ_BATCH, None), P(SEQ_BATCH, None)),
        check_vma=False,
    )
```

```python
import math

import jax
import jax.numpy as jnp
from jax import lax
from jax.experimental import pallas as pl
from jax.experimental.pallas import tpu as pltpu
from jax.sharding import Mesh
from jax.sharding import PartitionSpec as P

D = 1024
HEADS = 8
HD = 256
ACT = 50
ADIM = 32
TSTEPS = 2
BLOCK = 128
ROWS = TSTEPS * ACT
PAD = 112
HALF = 56
ALL = 2 * PAD
KEYS = 512
NZ = 8
NX = 4
NB = 4
ZT = 7
SEQ = ("seq_0", "seq_1", "seq_2")
SEQ_BATCH = ("seq_0", "seq_1", "seq_2", "batch")
HIGHEST = lax.Precision.HIGHEST
MESH = pl.DeviceIdType.MESH
F32 = jnp.float32
BF16 = jnp.bfloat16
VMEM = pl.BlockSpec(memory_space=pltpu.VMEM)
ANY = pl.BlockSpec(memory_space=pl.ANY)
SMEM = pl.BlockSpec(memory_space=pltpu.SMEM)


def embed_time(times):
    half_width = D // 2
    channel = jnp.arange(half_width, dtype=F32)
    frequency = jnp.exp(-math.log(10000.0) * channel / half_width)
    phase = times[..., None] * 1000.0 * frequency
    return jnp.concatenate([jnp.sin(phase), jnp.cos(phase)], -1)


def dot_nt(a, b):
    return lax.dot_general(a, b, (((1,), (1,)), ((), ())), preferred_element_type=F32)


def dot_tn(a, b):
    return lax.dot_general(a, b, (((0,), (0,)), ((), ())), preferred_element_type=F32)


def lanes_of(shape=(8, 128)):
    return lax.broadcasted_iota(jnp.int32, shape, len(shape) - 1)


def merge(out, parts, count):
    peaks = [p[2 * count] for p in parts]
    top = peaks[0]
    for one in peaks[1:]:
        top = jnp.maximum(top, one)
    scales = [jnp.exp(one - top) for one in peaks]
    total = scales[0] * parts[0][2 * count + 1]
    for scale, p in zip(scales[1:], parts[1:]):
        total = total + scale * p[2 * count + 1]
    for j in range(count):
        columns = [jnp.broadcast_to(scale[:, j : j + 1], (8, 128)) for scale in scales]
        for half in range(2):
            value = columns[0] * parts[0][2 * j + half]
            for column, p in zip(columns[1:], parts[1:]):
                value = value + column * p[2 * j + half]
            out(2 * j + half, value)
    return top, total


def thirds(value):
    high = value.astype(BF16)
    rest = value - high.astype(F32)
    middle = rest.astype(BF16)
    return high, middle, (rest - middle.astype(F32)).astype(BF16)


def remote(src, dst, ss, rs, device):
    return pltpu.make_async_remote_copy(
        src_ref=src, dst_ref=dst, send_sem=ss, recv_sem=rs, device_id=device, device_id_type=MESH
    )


def step_kernel(
    times_ref, emb_ref, blocks_ref,
    temb_ref, act_ref, noise_ref, ih_ref, ag_ref, og_ref, k_ref, v_ref, wq_hbm, wo_hbm, oh_hbm,
    q_out, o_out,
    wq, wo, oh, noisy, goal, hid, nrm, nperm, heads_t,
    weights_ref, local_peak, sums, cbuf, acc, xbuf, zsend, zbuf, psend, prec, attn_all, agsend, gath,
    db, scale_ref, delta_ref, az, ro_all, ro, gq, cbuf2, acc2, xbuf2, zsend2, zbuf2,
    bsend, brec, yrec, drows, drec, e_send, e_rec, f_send, f_rec,
    load, c_ss, c_rs, x_ss, x_rs, z_ss, z_rs, p_ss, p_rs, gz_ss, gz_rs, gx_ss, gx_rs, gc_ss, gc_rs,
    c2_ss, c2_rs, x2_ss, x2_rs, z2_ss, z2_rs, y_ss, y_rs, b_ss, b_rs, d_ss, d_rs, e_ss, e_rs, f_ss, f_rs,
):
    z = lax.axis_index("seq_0")
    x = lax.axis_index("seq_1")
    c = lax.axis_index("seq_2")
    b = lax.axis_index("batch")
    other = 1 - c
    me = (z * NX + x) * 2 + c
    flat = x * NB + b
    deep = z * 2 + c
    tile = jnp.minimum(z, ZT - 1)
    lane = lanes_of()

    def seq_peer(k):
        return {"seq_0": k // 8, "seq_1": lax.rem(k // 2, NX), "seq_2": lax.rem(k, 2)}

    def flat_peer(k):
        return {"seq_1": k // NB, "batch": lax.rem(k, NB)}

    def deep_peer(k):
        return {"seq_0": k // 2, "seq_2": lax.rem(k, 2)}

    def loads(i):
        if i < 2:
            half = other if i == 0 else c
            cols = pl.ds(pl.multiple_of(half * 1024, 1024), 1024)
            return pltpu.make_async_copy(wq_hbm.at[:, cols], wq.at[i], load.at[i])
        return pltpu.make_async_copy((wo_hbm, oh_hbm)[i - 2], (wo, oh)[i - 2], load.at[i])

    for i in range(4):
        loads(i).start()
    barrier = pltpu.get_barrier_semaphore()

    @pl.loop(1, 64)
    def _(d):
        pl.semaphore_signal(barrier, inc=1, device_id=seq_peer(lax.rem(me + d, 64)), device_id_type=MESH)

    @pl.loop(1, 16)
    def _(d):
        pl.semaphore_signal(barrier, inc=1, device_id=flat_peer(lax.rem(flat + d, 16)), device_id_type=MESH)

    for s in range(2):
        act = act_ref[s]
        for t in range(2):
            noise = noise_ref[s, t]
            level = times_ref[s, t]
            row = s * PAD + t * HALF
            noisy[row : row + HALF, :] = jnp.zeros((HALF, ADIM), F32)
            noisy[row : row + ACT, :] = level * noise + (1.0 - level) * act
            goal[2 * s + t] = jnp.zeros((HALF, ADIM), F32)
            goal[2 * s + t, 0:ACT] = noise - act
    for s in range(2):
        wh, wm, wl = thirds(ih_ref[emb_ref[s]])
        ah, am, al = (part.astype(F32) for part in thirds(noisy[s * PAD : (s + 1) * PAD]))
        left = jnp.concatenate([ah, ah, am, ah, am, al], axis=1).astype(BF16)
        right = jnp.concatenate([wh, wm, wh, wl, wm, wh], axis=0)
        product = jnp.dot(left, right, preferred_element_type=F32)
        for t in range(2):
            hidden = product[t * HALF : (t + 1) * HALF] + temb_ref[2 * s + t : 2 * s + t + 1, :]
            hid[2 * s + t] = hidden
        hidden = jnp.concatenate([hid[2 * s], hid[2 * s + 1]], axis=0)
        inverse = lax.rsqrt(jnp.mean(hidden * hidden, axis=1, keepdims=True) + 1e-06)
        nrm[s * PAD : (s + 1) * PAD, :] = (hidden * inverse * ag_ref[...]).astype(BF16)

    def core_copy(chunk):
        return remote(sums.at[0, chunk], cbuf.at[chunk], c_ss.at[chunk], c_rs.at[chunk], {"seq_2": other})

    for i in range(2):
        half = other if i == 0 else c
        loads(i).wait()
        q = jnp.dot(nrm[...], wq[i], preferred_element_type=F32)
        q = (q * (1.0 / math.sqrt(HD))).astype(BF16)
        for s in range(2):
            qs = jnp.concatenate(
                [q[s * PAD : (s + 1) * PAD, h * HD : (h + 1) * HD] for h in range(4)], axis=0
            )
            scores = dot_nt(qs, k_ref[s])
            limit = BLOCK * blocks_ref[s] - me * KEYS
            valid = lax.broadcasted_iota(jnp.int32, scores.shape, 1) < limit
            scores = jnp.where(valid, scores, -1e30)
            peak = jnp.max(scores, axis=1, keepdims=True)
            weights = jnp.where(valid, jnp.exp(scores - peak), 0.0)
            total = jnp.sum(weights, axis=1, keepdims=True)
            mixed = jnp.dot(weights.astype(BF16), v_ref[s], preferred_element_type=F32)
            for h in range(4):
                weights_ref[i, h, s * PAD : (s + 1) * PAD, :] = weights[h * PAD : (h + 1) * PAD]
            for xx in (2 * s, 2 * s + 1):
                peaks = jnp.zeros((8, 128), F32)
                totals = jnp.ones((8, 128), F32)
                for zz in range(ZT):
                    for h in range(4):
                        j = zz * 4 + h
                        row = h * PAD + (7 * xx + zz - 14 * s) * 8
                        peaks = jnp.where(lane == j, peak[row : row + 8], peaks)
                        totals = jnp.where(lane == j, total[row : row + 8], totals)
                        sums[i, xx, 2 * j] = mixed[row : row + 8, :128]
                        sums[i, xx, 2 * j + 1] = mixed[row : row + 8, 128:]
                sums[i, xx, 56] = peaks
                sums[i, xx, 57] = totals
                local_peak[i, xx] = peaks
            if i == 0:
                if s == 0:
                    pl.semaphore_wait(barrier, 63 + 15)
                core_copy(2 * s).start()
                core_copy(2 * s + 1).start()

    def x_copy(d):
        peer = lax.rem(x + d, NX)
        return remote(acc.at[peer], xbuf.at[x], x_ss.at[d], x_rs.at[d], {"seq_1": peer})

    def x_arrival(d):
        peer = lax.rem(x + NX - d, NX)
        return remote(acc.at[peer], xbuf.at[peer], x_ss.at[d], x_rs.at[d], {"seq_1": peer})

    for chunk in range(NX):
        core_copy(chunk).wait_recv()
    for d in (2, 1, 3, 0):
        chunk = lax.rem(x + d, NX)
        target = acc.at[chunk]

        def put(i, value):
            target[i] = value

        top, total = merge(put, (sums.at[1, chunk], cbuf.at[chunk]), 28)
        target[56] = top
        target[57] = total
        if d:
            x_copy(d).start()

    loads(2).wait()
    loads(3).wait()
    for s in range(2):
        heads_t[s] = oh[emb_ref[s]].T
    for bb in range(NB):
        col = lax.broadcasted_iota(jnp.int32, (D, 256), 1)
        natural = (col // 4) * 16 + bb * 4 + lax.rem(col, 4)
        pick = (lax.broadcasted_iota(jnp.int32, (D, 256), 0) == natural).astype(F32).astype(BF16)
        nperm[0:ALL, bb * 256 : (bb + 1) * 256] = jnp.dot(
            nrm[...], pick, preferred_element_type=F32
        ).astype(BF16)
    nperm[ALL:256, :] = jnp.zeros((256 - ALL, D), BF16)

    for d in (1, 3, 2):
        x_arrival(d).wait_recv()
    parts = [acc.at[x]] + [xbuf.at[lax.rem(x + NX - d, NX)] for d in range(1, NX)]

    def put_z(i, value):
        zsend[i // 8, i % 8] = value

    top, total = merge(put_z, parts, 28)
    for zz in range(ZT):
        t = top if zz == 0 else pltpu.roll(top, 128 - 4 * zz, axis=1)
        zsend[zz, 8] = jnp.where(lane < 32, t, pltpu.roll(total, (32 - 4 * zz) % 128, axis=1))

    def z_copy(d):
        peer = lax.rem(z + d, NZ)
        src = zsend.at[jnp.minimum(peer, ZT - 1)]
        return peer, remote(src, zbuf.at[z], z_ss.at[d], z_rs.at[d], {"seq_0": peer})

    def z_arrival(d):
        peer = lax.rem(z + NZ - d, NZ)
        return remote(zsend.at[0], zbuf.at[peer], z_ss.at[d], z_rs.at[d], {"seq_0": peer})

    far_first = (4, 3, 5, 2, 6, 1, 7)
    for d in far_first:
        peer, copy = z_copy(d)

        @pl.when(peer < ZT)
        def _():
            copy.start()

    def ag_copy(d):
        peer = lax.rem(z + d, NZ)
        return remote(agsend.at[peer], gath.at[c, x, tile], gz_ss.at[d], gz_rs.at[d], {"seq_0": peer})

    def ag_arrival(d):
        peer = lax.rem(z + NZ - d, NZ)
        slot = gath.at[c, x, jnp.minimum(peer, ZT - 1)]
        return peer, remote(agsend.at[0], slot, gz_ss.at[d], gz_rs.at[d], {"seq_0": peer})

    pair = remote(psend, prec, p_ss, p_rs, {"seq_2": other})

    @pl.when(z < ZT)
    def _():
        for d in range(1, NZ):
            z_arrival(d).wait_recv()
        sources = [zsend.at[tile]] + [zbuf.at[lax.rem(z + NZ - d, NZ)] for d in range(1, NZ)]
        stats = [p[8] for p in sources]
        top = stats[0]
        for one in stats[1:]:
            top = jnp.maximum(top, one)
        scales = [jnp.exp(one - top) for one in stats]
        moved = [pltpu.roll(one, 96, axis=1) for one in stats]
        total = scales[0] * moved[0]
        for scale, one in zip(scales[1:], moved[1:]):
            total = total + scale * one
        first = c == 0
        products = []
        for h in range(4):
            columns = [jnp.broadcast_to(scale[:, h : h + 1], (8, 128)) for scale in scales]
            whole = jnp.broadcast_to(total[:, h : h + 1], (8, 128))
            halves = []
            for half in range(2):
                value = columns[0] * sources[0][2 * h + half]
                for column, p in zip(columns[1:], sources[1:]):
                    value = value + column * p[2 * h + half]
                halves.append((value / whole).astype(BF16))
            attn = jnp.concatenate(halves, axis=1)
            start = pl.multiple_of(c * 1024 + h * HD, HD)
            products.append(jnp.dot(attn, wo[pl.ds(start, HD), :], preferred_element_type=F32))
            low, high = halves[0].astype(F32), halves[1].astype(F32)
            attn_all[4 * c + h] = jnp.where(first, low, high)
            psend[8 + h] = jnp.where(first, high, low)
        partial = products[0] + products[1] + products[2] + products[3]
        for i in range(8):
            psend[i] = partial[:, i * 128 : (i + 1) * 128]
        pair.start()
        start = pl.multiple_of(tile * 8, 8)
        near = hid[x, pl.ds(start, 8), :]
        target = goal[x, pl.ds(start, 8), :]
        sample = x // 2
        pair.wait_recv()
        resid = near + (partial + jnp.concatenate([prec[i] for i in range(8)], axis=1))
        inverse = lax.rsqrt(jnp.mean(resid * resid, axis=1, keepdims=True) + 1e-06)
        gain = og_ref[...]
        normed = resid * inverse * gain
        real = start + lax.broadcasted_iota(jnp.int32, (8, 1), 0) < ACT
        back = jnp.zeros((8, D), F32)
        for j in range(ADIM):
            head = heads_t[sample, j : j + 1, :]
            velocity = jnp.sum(normed * head, axis=1, keepdims=True)
            dvel = 2.0 * (velocity - target[:, j : j + 1]) / (8 * ROWS)
            back = back + jnp.where(real, dvel, 0.0) * head
        scaled = back * gain
        mean = jnp.mean(resid * scaled, axis=1, keepdims=True)
        dresid = inverse * scaled - inverse * inverse * inverse * resid * mean
        dresid = dresid.astype(BF16).astype(F32)
        stats = jnp.where(lane < 32, top, pltpu.roll(total, 32, axis=1))
        for h in range(4):
            delta = jnp.sum(products[h] * dresid, axis=1, keepdims=True)
            stats = jnp.where(lane == 64 + h, delta, stats)
        own = jnp.where(first, dresid[:, :512], dresid[:, 512:])
        for h in range(4):
            attn_all[4 * other + h] = prec[8 + h]
        for peer in range(NZ):
            for i in range(4):
                agsend[peer, i] = own[:, i * 128 : (i + 1) * 128]
            agsend[peer, 4] = stats
            agsend[peer, 5] = attn_all[peer]
        gath[c, x, tile] = agsend[z]
        for d in far_first:
            ag_copy(d).start()

    for d in range(1, NZ):
        peer, copy = ag_arrival(d)

        @pl.when(peer < ZT)
        def _():
            copy.wait_recv()

    def gx_copy(d):
        peer = lax.rem(x + d, NX)
        return remote(gath.at[c, x], gath.at[c, x], gx_ss.at[d], gx_rs.at[d], {"seq_1": peer})

    def gx_arrival(d):
        peer = lax.rem(x + NX - d, NX)
        return remote(gath.at[c, x], gath.at[c, peer], gx_ss.at[d], gx_rs.at[d], {"seq_1": peer})

    def gc_copy(d):
        chunk = lax.rem(x + NX - d, NX)
        return remote(gath.at[c, chunk], gath.at[c, chunk], gc_ss.at[d], gc_rs.at[d], {"seq_2": other})

    def gc_arrival(d):
        chunk = lax.rem(x + NX - d, NX)
        return remote(gath.at[c, chunk], gath.at[other, chunk], gc_ss.at[d], gc_rs.at[d], {"seq_2": other})

    for d in (2, 1, 3):
        gx_copy(d).start()
    gc_copy(0).start()
    for d in (1, 3, 2):
        gx_arrival(d).wait_recv()
        gc_copy(d).start()
    for d in range(NX):
        gc_arrival(d).wait_recv()

    for t in range(0, 28, 2):
        for core in range(2):
            for i in range(4):
                both = jnp.concatenate([gath[core, u // 7, u % 7, i] for u in (t, t + 1)], axis=0)
                lo = core * 512 + i * 128
                db[t * 8 : t * 8 + 16, lo : lo + 128] = both.astype(BF16)
    for i in range(2):
        half = other if i == 0 else c
        for t in range(28):
            xx, zz = t // 7, t % 7
            stats = gath[half, xx, zz, 4]
            near = local_peak[i, xx]
            if zz:
                near = pltpu.roll(near, 128 - 4 * zz, axis=1)
            scale = jnp.exp(near - stats) / pltpu.roll(stats, 96, axis=1)
            for h in range(4):
                scale_ref[h, t * 8 : t * 8 + 8] = jnp.broadcast_to(scale[:, h : h + 1], (8, 128))
                delta_ref[h, t * 8 : t * 8 + 8] = jnp.broadcast_to(stats[:, 64 + h : 65 + h], (8, 128))
        start = pl.multiple_of(half * 1024, 1024)
        dattn = dot_nt(db[...], wo[pl.ds(start, 1024), :]).astype(BF16)
        for s in range(2):
            rows = slice(s * PAD, (s + 1) * PAD)
            stacked = jnp.concatenate(
                [dattn[rows, h * HD : (h + 1) * HD] for h in range(4)], axis=0
            )
            dvalues = dot_nt(stacked, v_ref[s])
            parts = []
            for h in range(4):
                delta = delta_ref[h, rows]
                scale = scale_ref[h, rows]
                line = []
                for k in range(4):
                    cols = slice(k * 128, (k + 1) * 128)
                    dv = dvalues[h * PAD : (h + 1) * PAD, cols]
                    line.append((weights_ref[i, h, rows, cols] * scale * (dv - delta)).astype(BF16))
                parts.append(jnp.concatenate(line, axis=1))
            dscore = jnp.concatenate(parts, axis=0)
            grads = jnp.dot(dscore, k_ref[s], preferred_element_type=F32) * (1.0 / math.sqrt(HD))
            grads = grads.astype(BF16).astype(F32)
            for h in range(4):
                gq[i, h, s] = grads[h * PAD : (h + 1) * PAD]
            if i == 0:
                for h in range(4):
                    remote(
                        gq.at[0, h, s], cbuf2.at[h, s], c2_ss.at[h, s], c2_rs.at[h, s], {"seq_2": other}
                    ).start()

    def core2(h, s):
        return remote(gq.at[0, h, s], cbuf2.at[h, s], c2_ss.at[h, s], c2_rs.at[h, s], {"seq_2": other})

    def x2_copy(d):
        peer = lax.rem(x + d, NX)
        return remote(acc2.at[peer], xbuf2.at[x], x2_ss.at[d], x2_rs.at[d], {"seq_1": peer})

    def x2_arrival(d):
        peer = lax.rem(x + NX - d, NX)
        return remote(acc2.at[peer], xbuf2.at[peer], x2_ss.at[d], x2_rs.at[d], {"seq_1": peer})

    for h in range(4):
        for s in range(2):
            core2(h, s).wait_recv()
    for d in (2, 1, 3, 0):
        h = lax.rem(x + d, NX)
        acc2[h] = gq[1, h] + cbuf2[h]
        if d:
            x2_copy(d).start()

    half_core = x // 2
    for t in range(0, 28, 2):
        both = jnp.concatenate([gath[half_core, u // 7, u % 7, 5] for u in (t, t + 1)], axis=0)
        az[t * 8 : t * 8 + 16, :] = both.astype(BF16)
    ro_all[...] = dot_tn(az[...], db[...])
    offset = lax.rem(x, 2) * 64 + c * 32
    for bb in range(NB):
        ro[bb] = ro_all[pl.ds(pl.multiple_of(offset + 8 * bb, 8), 8), :]

    def y_copy(d):
        peer = lax.rem(b + d, NB)
        return remote(ro.at[peer], yrec.at[b], y_ss.at[d], y_rs.at[d], {"batch": peer})

    def y_arrival(d):
        peer = lax.rem(b + NB - d, NB)
        return remote(ro.at[peer], yrec.at[peer], y_ss.at[d], y_rs.at[d], {"batch": peer})

    for d in range(1, NB):
        y_copy(d).start()
    yrec[b] = ro[b]
    for d in range(1, NB):
        y_arrival(d).wait_recv()
    raw_o = yrec[0] + yrec[1] + yrec[2] + yrec[3]
    ro_all[0:8] = raw_o
    squares_o = jnp.sum(raw_o * raw_o, keepdims=True)

    for d in (1, 3, 2):
        x2_arrival(d).wait_recv()
    summed = acc2[x]
    for d in range(1, NX):
        summed = summed + xbuf2[lax.rem(x + NX - d, NX)]
    turned = jnp.concatenate([summed[0], summed[1], jnp.zeros((256 - ALL, HD), F32)], axis=0).T
    for zz in range(NZ):
        zsend2[zz] = turned[zz * 32 : (zz + 1) * 32]

    def z2_copy(d):
        peer = lax.rem(z + d, NZ)
        return remote(zsend2.at[peer], zbuf2.at[z], z2_ss.at[d], z2_rs.at[d], {"seq_0": peer})

    def z2_arrival(d):
        peer = lax.rem(z + NZ - d, NZ)
        return remote(zsend2.at[peer], zbuf2.at[peer], z2_ss.at[d], z2_rs.at[d], {"seq_0": peer})

    for d in far_first:
        z2_copy(d).start()
    zbuf2[z] = zsend2[z]
    for d in range(1, NZ):
        z2_arrival(d).wait_recv()
    columns = zbuf2[0]
    for zz in range(1, NZ):
        columns = columns + zbuf2[zz]
    product = jnp.dot(jnp.concatenate(thirds(columns), axis=0), nperm[...], preferred_element_type=F32)
    product = product[0:32] + (product[32:64] + product[64:96])
    for bb in range(NB):
        bsend[bb] = product[:, bb * 256 : (bb + 1) * 256]

    def b_copy(d):
        peer = lax.rem(b + d, NB)
        return remote(bsend.at[peer], brec.at[b], b_ss.at[d], b_rs.at[d], {"batch": peer})

    def b_arrival(d):
        peer = lax.rem(b + NB - d, NB)
        return remote(bsend.at[peer], brec.at[peer], b_ss.at[d], b_rs.at[d], {"batch": peer})

    for d in (2, 1, 3):
        b_copy(d).start()
    brec[b] = bsend[b]
    for d in range(1, NB):
        b_arrival(d).wait_recv()
    raw_t = brec[0] + brec[1] + brec[2] + brec[3]
    squares = jnp.sum(raw_t * raw_t, keepdims=True) + squares_o
    e_send[...] = jnp.broadcast_to(squares, (8, 128))

    def e_copy(d):
        return remote(e_send, e_rec.at[flat], e_ss.at[d], e_rs.at[d], flat_peer(lax.rem(flat + d, 16)))

    def e_arrival(d):
        peer = lax.rem(flat + 16 - d, 16)
        return remote(e_send, e_rec.at[peer], e_ss.at[d], e_rs.at[d], flat_peer(peer))

    @pl.loop(1, 16)
    def _(d):
        e_copy(d).start()

    e_rec[flat] = e_send[...]
    quarter = lax.rem(z, 4)
    spread = jnp.concatenate([jnp.where(quarter == i, raw_t, 0.0) for i in range(4)], axis=0).T
    for i in range(64):
        drows[i] = spread[4 * i : 4 * i + 4]

    def d_copy(d):
        peer = lax.rem(me + d, 64)
        return remote(drows.at[peer], drec.at[me], d_ss.at[d], d_rs.at[d], seq_peer(peer))

    def d_arrival(d):
        peer = lax.rem(me + 64 - d, 64)
        return remote(drows.at[peer], drec.at[peer], d_ss.at[d], d_rs.at[d], seq_peer(peer))

    @pl.loop(1, 64)
    def _(d):
        d_copy(d).start()

    drec[me] = drows[me]

    @pl.loop(1, 16)
    def _(d):
        e_arrival(d).wait_recv()

    f_send[...] = jnp.sum(e_rec[...], axis=0)

    def f_copy(d):
        return remote(f_send, f_rec.at[deep], f_ss.at[d], f_rs.at[d], deep_peer(lax.rem(deep + d, 16)))

    def f_arrival(d):
        peer = lax.rem(deep + 16 - d, 16)
        return remote(f_send, f_rec.at[peer], f_ss.at[d], f_rs.at[d], deep_peer(peer))

    @pl.loop(1, 16)
    def _(d):
        f_copy(d).start()

    f_rec[deep] = f_send[...]

    @pl.loop(1, 64)
    def _(d):
        d_arrival(d).wait_recv()

    blocks = []
    for h in range(HEADS):
        for zh in range(2):
            base = zh * 32 + (h % 4) * 2 + h // 4
            blocks.append(drec[base] + drec[base + 8] + drec[base + 16] + drec[base + 24])
    raw_q = jnp.concatenate(blocks, axis=1)

    @pl.loop(1, 16)
    def _(d):
        f_arrival(d).wait_recv()

    norm = jnp.sqrt(jnp.sum(f_rec[...], axis=0))
    factor = jnp.minimum(1.0, 1.0 / (norm + 1e-06))
    q_out[...] = raw_q * factor[0:1, 0:1]
    o_out[...] = ro_all[0:8] * factor[0:1, 0:1]

    for d in range(NX):
        core_copy(d).wait_send()
        gc_copy(d).wait_send()
        for s in range(2):
            core2(d, s).wait_send()
        if d:
            x_copy(d).wait_send()
            gx_copy(d).wait_send()
            x2_copy(d).wait_send()
            y_copy(d).wait_send()
            b_copy(d).wait_send()
    for d in range(1, NZ):
        z2_copy(d).wait_send()
        peer, copy = z_copy(d)

        @pl.when(peer < ZT)
        def _():
            copy.wait_send()

    @pl.when(z < ZT)
    def _():
        pair.wait_send()
        for d in range(1, NZ):
            ag_copy(d).wait_send()

    @pl.loop(1, 16)
    def _(d):
        e_copy(d).wait_send()
        f_copy(d).wait_send()

    @pl.loop(1, 64)
    def _(d):
        d_copy(d).wait_send()


def local(
    actions,
    noise,
    times,
    embodiment,
    prefix_blocks,
    prefix_keys,
    prefix_values,
    input_heads,
    attn_gain,
    w_query,
    w_output,
    out_gain,
    output_heads,
):
    temb = embed_time(times).reshape(4, D)
    dma = pltpu.SemaphoreType.DMA

    def v(*shape, kind=F32):
        return pltpu.VMEM(shape, kind)

    return pl.pallas_call(
        step_kernel,
        out_shape=(
            jax.ShapeDtypeStruct((4, HEADS * HD), F32),
            jax.ShapeDtypeStruct((8, D), F32),
        ),
        in_specs=[SMEM] * 3 + [VMEM] * 8 + [ANY] * 3,
        out_specs=(VMEM, VMEM),
        scratch_shapes=[
            v(2, D, 1024, kind=BF16), v(2048, D, kind=BF16), v(4, D, ADIM), v(ALL, ADIM),
            v(4, HALF, ADIM), v(4, HALF, D), v(ALL, D, kind=BF16), v(256, D, kind=BF16), v(2, ADIM, D),
            v(2, 4, ALL, KEYS), v(2, NX, 8, 128), v(2, NX, 58, 8, 128), v(NX, 58, 8, 128),
            v(NX, 58, 8, 128), v(NX, 58, 8, 128), v(ZT, 9, 8, 128), v(NZ, 9, 8, 128),
            v(12, 8, 128), v(12, 8, 128), v(8, 8, 128), v(NZ, 6, 8, 128), v(2, NX, ZT, 6, 8, 128),
            v(ALL, D, kind=BF16), v(4, ALL, 128), v(4, ALL, 128), v(ALL, 128, kind=BF16), v(128, D),
            v(NB, 8, D), v(2, 4, 2, PAD, HD), v(4, 2, PAD, HD), v(4, 2, PAD, HD), v(4, 2, PAD, HD),
            v(NZ, 32, 256), v(NZ, 32, 256), v(NB, 32, 256), v(NB, 32, 256), v(NB, 8, D),
            v(64, 4, 128), v(64, 4, 128), v(8, 128), v(16, 8, 128), v(8, 128), v(16, 8, 128),
            dma((4,)), dma((NX,)), dma((NX,)), dma((NX,)), dma((NX,)), dma((NZ,)), dma((NZ,)), dma, dma,
            dma((NZ,)), dma((NZ,)), dma((NX,)), dma((NX,)), dma((NX,)), dma((NX,)),
            dma((4, 2)), dma((4, 2)), dma((NX,)), dma((NX,)), dma((NZ,)), dma((NZ,)),
            dma((NB,)), dma((NB,)), dma((NB,)), dma((NB,)), dma((64,)), dma((64,)),
            dma((16,)), dma((16,)), dma((16,)), dma((16,)),
        ],
        compiler_params=pltpu.CompilerParams(
            collective_id=0, has_side_effects=True, vmem_limit_bytes=56 * 1024 * 1024
        ),
    )(
        times, embodiment, prefix_blocks, temb, actions, noise, input_heads, attn_gain[None, :],
        out_gain[None, :], prefix_keys, prefix_values, w_query, w_output, output_heads,
    )


def solution(mesh):
    torus = Mesh(
        mesh.devices.reshape(NZ, NX, 2, mesh.shape["batch"]), ("seq_0", "seq_1", "seq_2", "batch")
    )
    placed = (
        P("batch", None, None),
        P("batch", None, None, None),
        P("batch", None),
        P("batch"),
        P("batch"),
        P("batch", SEQ, None),
        P("batch", SEQ, None),
        P(),
        P(),
        P(),
        P(),
        P(),
        P(),
    )
    return jax.shard_map(
        local,
        mesh=torus,
        in_specs=placed,
        out_specs=(P(SEQ_BATCH, None), P(SEQ_BATCH, None)),
        check_vma=False,
    )
```

```python
import math

import jax
import jax.numpy as jnp
from jax import lax
from jax.experimental import pallas as pl
from jax.experimental.pallas import tpu as pltpu
from jax.sharding import Mesh
from jax.sharding import PartitionSpec as P

D = 1024
HEADS = 8
HD = 256
ACT = 50
ADIM = 32
TSTEPS = 2
BLOCK = 128
ROWS = TSTEPS * ACT
PAD = 112
HALF = 56
ALL = 2 * PAD
KEYS = 512
NZ = 8
NX = 4
NB = 4
ZT = 7
SEQ = ("seq_0", "seq_1", "seq_2")
SEQ_BATCH = ("seq_0", "seq_1", "seq_2", "batch")
MESH = pl.DeviceIdType.MESH
F32 = jnp.float32
BF16 = jnp.bfloat16
VMEM = pl.BlockSpec(memory_space=pltpu.VMEM)
ANY = pl.BlockSpec(memory_space=pl.ANY)
SMEM = pl.BlockSpec(memory_space=pltpu.SMEM)


def dot_nt(a, b):
    return lax.dot_general(a, b, (((1,), (1,)), ((), ())), preferred_element_type=F32)


def dot_tn(a, b):
    return lax.dot_general(a, b, (((0,), (0,)), ((), ())), preferred_element_type=F32)


def lanes_of(shape=(8, 128)):
    return lax.broadcasted_iota(jnp.int32, shape, len(shape) - 1)


def thirds(value):
    high = value.astype(BF16)
    rest = value - high.astype(F32)
    middle = rest.astype(BF16)
    return high, middle, (rest - middle.astype(F32)).astype(BF16)


def remote(src, dst, ss, rs, device):
    return pltpu.make_async_remote_copy(
        src_ref=src, dst_ref=dst, send_sem=ss, recv_sem=rs, device_id=device, device_id_type=MESH
    )


def rolled(value, lanes):
    lanes = lanes % 128
    return pltpu.roll(value, lanes, axis=1) if lanes else value


def merge(parts, peaks, totals, entries, put):
    top = peaks[0]
    for one in peaks[1:]:
        top = jnp.maximum(top, one)
    scales = [jnp.exp(one - top) for one in peaks]
    total = scales[0] * totals[0]
    for scale, one in zip(scales[1:], totals[1:]):
        total = total + scale * one
    for column, first, key in entries:
        wide = [jnp.broadcast_to(scale[:, column : column + 1], (8, 128)) for scale in scales]
        for half in range(2):
            value = wide[0] * parts[0][first + half]
            for scale, part in zip(wide[1:], parts[1:]):
                value = value + scale * part[first + half]
            put(key, half, value)
    return top, total


def merge_packed(parts, stat, entries, put):
    stats = [part[stat] for part in parts]
    return merge(parts, stats, [rolled(one, 96) for one in stats], entries, put)


def step_kernel(
    times_ref, emb_ref, blocks_ref,
    act_ref, noise_ref, ag_ref, og_ref, ih_hbm, k_hbm, v_hbm, wq_hbm, wo_hbm, oh_hbm,
    q_out, o_out,
    ih, k_ref, v_ref, wq, wo, oh, mixed_in, goal, hid, nrm, nperm,
    weights_ref, local_peak, sums, cbuf, acc, xbuf, zf, zfbuf, zx, zxbuf, zsend, zbuf,
    psend, prec, attn_all, agz, agx, aga, gz, gx, ga,
    db, scale_ref, delta_ref, az, ro_all, ro, gq, cbuf2, zs2, zbuf2, zx2, zxbuf2, xs2, xbuf2, ws2, wbuf2,
    bsend, brec, yrec, drows, drec, e_send, e_rec, f_send, f_rec,
    load, c_ss, c_rs, x_ss, x_rs, zf_ss, zf_rs, zx_ss, zx_rs, z_ss, z_rs, p_ss, p_rs,
    gz_ss, gz_rs, gzx_ss, gzx_rs, gzc_ss, gzc_rs, gx_ss, gx_rs, gxz_ss, gxz_rs, gxc_ss, gxc_rs,
    ga_ss, ga_rs, gax_ss, gax_rs, gac_ss, gac_rs,
    c2_ss, c2_rs, z2_ss, z2_rs, zx2_ss, zx2_rs, x2_ss, x2_rs, w2_ss, w2_rs,
    y_ss, y_rs, b_ss, b_rs, d_ss, d_rs, e_ss, e_rs, f_ss, f_rs,
):
    z = lax.axis_index("seq_0")
    x = lax.axis_index("seq_1")
    c = lax.axis_index("seq_2")
    b = lax.axis_index("batch")
    other = 1 - c
    me = (z * NX + x) * 2 + c
    flat = x * NB + b
    deep = z * 2 + c
    tile = jnp.minimum(z, ZT - 1)
    active = z < ZT
    lane = lanes_of()
    zp = [lax.rem(z + d, NZ) for d in range(NZ)]
    zm = [lax.rem(z + NZ - d, NZ) for d in range(NZ)]
    xp = [lax.rem(x + d, NX) for d in range(NX)]
    xm = [lax.rem(x + NX - d, NX) for d in range(NX)]
    bp = [lax.rem(b + d, NB) for d in range(NB)]
    bm = [lax.rem(b + NB - d, NB) for d in range(NB)]
    cp = [c, other]
    zt = [jnp.minimum(one, ZT - 1) for one in zp]
    zmt = [jnp.minimum(one, ZT - 1) for one in zm]
    far = (4, 3, 5, 2, 6, 1, 7)
    near = (2, 1, 3)
    sibling = {"seq_2": other}

    barrier = pltpu.get_barrier_semaphore()
    pl.semaphore_signal(barrier, inc=1, device_id=sibling, device_id_type=MESH)
    for d in far:
        pl.semaphore_signal(barrier, inc=1, device_id={"seq_0": zp[d]}, device_id_type=MESH)
    for d in near:
        pl.semaphore_signal(barrier, inc=1, device_id={"seq_1": xp[d]}, device_id_type=MESH)
        pl.semaphore_signal(barrier, inc=1, device_id={"batch": bp[d]}, device_id_type=MESH)

    def loads(i):
        if i == 1 or i == 4:
            half = other if i == 1 else c
            cols = pl.ds(pl.multiple_of(half * 1024, 1024), 1024)
            return pltpu.make_async_copy(wq_hbm.at[:, cols], wq.at[i // 4], load.at[i])
        src = (ih_hbm, None, k_hbm, v_hbm, None, wo_hbm, oh_hbm)[i]
        dst = (ih, None, k_ref, v_ref, None, wo, oh)[i]
        return pltpu.make_async_copy(src, dst, load.at[i])

    for i in range(7):
        loads(i).start()

    channel = lax.broadcasted_iota(jnp.int32, (8, 512), 1).astype(F32)
    frequency = jnp.exp(-math.log(10000.0) * channel / 512)
    row = lax.broadcasted_iota(jnp.int32, (8, 512), 0)
    moment = jnp.zeros((8, 512), F32)
    for st in range(4):
        moment = jnp.where(row == st, times_ref[st // 2, st % 2], moment)
    phase = moment * 1000.0 * frequency
    temb = jnp.concatenate([jnp.sin(phase), jnp.cos(phase)], axis=1)
    mixed_in[...] = jnp.zeros((4, ADIM, 128), F32)
    for s in range(2):
        act = act_ref[s]
        for t in range(2):
            noise = noise_ref[s, t]
            level = times_ref[s, t]
            mixed_in[2 * s + t, :, 0:ACT] = noise - act
            goal[2 * s + t] = mixed_in[2 * s + t].T
            mixed_in[2 * s + t, :, 0:ACT] = level * noise + (1.0 - level) * act
    loads(0).wait()
    for s in range(2):
        wh, wm, wl = thirds(ih[emb_ref[s]])
        right = jnp.concatenate([wh, wm, wh, wl, wm, wh], axis=0)
        both = []
        for t in range(2):
            ah, am, al = thirds(mixed_in[2 * s + t])
            left = jnp.concatenate([ah, ah, am, ah, am, al], axis=0)
            hidden = dot_tn(left, right)[0:HALF] + temb[2 * s + t : 2 * s + t + 1, :]
            hid[2 * s + t] = hidden
            both.append(hidden)
        hidden = jnp.concatenate(both, axis=0)
        inverse = lax.rsqrt(jnp.mean(hidden * hidden, axis=1, keepdims=True) + 1e-06)
        nrm[s * PAD : (s + 1) * PAD, :] = (hidden * inverse * ag_ref[...]).astype(BF16)

    def core_copy(chunk):
        return remote(sums.at[0, chunk], cbuf.at[chunk], c_ss.at[chunk], c_rs.at[chunk], sibling)

    for i in range(2):
        loads(1 if i == 0 else 4).wait()
        q = jnp.dot(nrm[...], wq[i], preferred_element_type=F32)
        q = (q * (1.0 / math.sqrt(HD))).astype(BF16)
        if i == 0:
            loads(2).wait()
            loads(3).wait()
        for s in range(2):
            qs = jnp.concatenate(
                [q[s * PAD : (s + 1) * PAD, h * HD : (h + 1) * HD] for h in range(4)], axis=0
            )
            scores = dot_nt(qs, k_ref[s])
            limit = BLOCK * blocks_ref[s] - me * KEYS
            valid = lax.broadcasted_iota(jnp.int32, scores.shape, 1) < limit
            scores = jnp.where(valid, scores, -1e30)
            peak = jnp.max(scores, axis=1, keepdims=True)
            weights = jnp.where(valid, jnp.exp(scores - peak), 0.0)
            total = jnp.sum(weights, axis=1, keepdims=True)
            mixed = jnp.dot(weights.astype(BF16), v_ref[s], preferred_element_type=F32)
            for h in range(4):
                weights_ref[i, h, s * PAD : (s + 1) * PAD, :] = weights[h * PAD : (h + 1) * PAD]
            for xx in (2 * s, 2 * s + 1):
                peaks = jnp.zeros((8, 128), F32)
                totals = jnp.ones((8, 128), F32)
                for zz in range(ZT):
                    for h in range(4):
                        j = zz * 4 + h
                        at = h * PAD + (7 * xx + zz - 14 * s) * 8
                        peaks = jnp.where(lane == j, peak[at : at + 8], peaks)
                        totals = jnp.where(lane == j, total[at : at + 8], totals)
                        sums[i, xx, 2 * j] = mixed[at : at + 8, :128]
                        sums[i, xx, 2 * j + 1] = mixed[at : at + 8, 128:]
                sums[i, xx, 56] = peaks
                sums[i, xx, 57] = totals
                local_peak[i, xx] = peaks
            if i == 0:
                if s == 0:
                    pl.semaphore_wait(barrier, 1 + NX - 1 + NZ - 1 + NB - 1)
                core_copy(2 * s).start()
                core_copy(2 * s + 1).start()

    def x_copy(xx):
        return remote(acc.at[xx], xbuf.at[x], x_ss.at[xx], x_rs.at[x], {"seq_1": xx})

    def x_arrival(d):
        return remote(acc.at[xm[d]], xbuf.at[xm[d]], x_ss.at[xm[d]], x_rs.at[xm[d]], {"seq_1": xm[d]})

    def zf_copy(d):
        return remote(zf.at[zt[d]], zfbuf.at[z], zf_ss.at[d], zf_rs.at[d], {"seq_0": zp[d]})

    def zf_arrival(d):
        return remote(zf.at[0], zfbuf.at[zm[d]], zf_ss.at[d], zf_rs.at[d], {"seq_0": zm[d]})

    tops = []
    for xx in range(NX):
        core_copy(xx).wait_recv()

        def put_core(key, half, value):
            zz, h = key
            if h < 3:
                acc[xx, (zz * 3 + h) * 2 + half] = value
            else:
                zf[zz, xx * 2 + half] = value

        parts = (sums.at[1, xx], cbuf.at[xx])
        entries = [(zz * 4 + h, 2 * (zz * 4 + h), (zz, h)) for zz in range(ZT) for h in range(4)]
        top, total = merge(parts, [p[56] for p in parts], [p[57] for p in parts], entries, put_core)
        acc[xx, 42] = top
        acc[xx, 43] = total
        tops.append((top, total))

        @pl.when(x != xx)
        def _():
            x_copy(xx).start()

    for zz in range(ZT):
        stats = jnp.zeros((8, 128), F32)
        for xx in range(NX):
            top, total = tops[xx]
            stats = jnp.where(lane == xx, rolled(top, xx - 4 * zz - 3), stats)
            stats = jnp.where(lane == 32 + xx, rolled(total, 32 + xx - 4 * zz - 3), stats)
        zf[zz, 8] = stats
    for d in far:

        @pl.when(zp[d] < ZT)
        def _():
            zf_copy(d).start()

    for bb in range(NB):
        col = lax.broadcasted_iota(jnp.int32, (D, 256), 1)
        natural = (col // 4) * 16 + bb * 4 + lax.rem(col, 4)
        pick = (lax.broadcasted_iota(jnp.int32, (D, 256), 0) == natural).astype(F32).astype(BF16)
        placed = jnp.dot(nrm[...], pick, preferred_element_type=F32).astype(BF16)
        cols = slice(bb * 256, (bb + 1) * 256)
        nperm[0:PAD, cols] = placed[0:PAD]
        nperm[128 : 128 + PAD, cols] = placed[PAD:]
    nperm[PAD:128, :] = jnp.zeros((16, D), BF16)
    nperm[128 + PAD :, :] = jnp.zeros((16, D), BF16)
    loads(5).wait()
    loads(6).wait()

    def zx_copy(d):
        return remote(zx.at[xp[d]], zxbuf.at[x], zx_ss.at[d], zx_rs.at[d], {"seq_1": xp[d]})

    def zx_arrival(d):
        return remote(zx.at[xm[d]], zxbuf.at[xm[d]], zx_ss.at[d], zx_rs.at[d], {"seq_1": xm[d]})

    @pl.when(active)
    def _():
        for d in range(1, NZ):
            zf_arrival(d).wait_recv()

        def put_zx(key, half, value):
            zx[key, half] = value

        parts = [zf.at[tile]] + [zfbuf.at[zm[d]] for d in range(1, NZ)]
        top, total = merge_packed(parts, 8, [(xx, 2 * xx, xx) for xx in range(NX)], put_zx)
        for xx in range(NX):
            zx[xx, 2] = jnp.where(lane < 32, rolled(top, -xx), rolled(total, 32 - xx))
        for d in near:
            zx_copy(d).start()

    for d in (1, 3, 2):
        x_arrival(d).wait_recv()

    def put_z(key, half, value):
        zz, h = key
        zsend[zz, h * 2 + half] = value

    parts = [acc.at[x]] + [xbuf.at[xm[d]] for d in range(1, NX)]
    entries = [(zz * 4 + h, 2 * (zz * 3 + h), (zz, h)) for zz in range(ZT) for h in range(3)]
    top, total = merge(parts, [p[42] for p in parts], [p[43] for p in parts], entries, put_z)
    for zz in range(ZT):
        zsend[zz, 6] = jnp.where(lane < 32, rolled(top, -4 * zz), rolled(total, 32 - 4 * zz))

    def z_copy(d):
        return remote(zsend.at[zt[d]], zbuf.at[z], z_ss.at[d], z_rs.at[d], {"seq_0": zp[d]})

    def z_arrival(d):
        return remote(zsend.at[0], zbuf.at[zm[d]], z_ss.at[d], z_rs.at[d], {"seq_0": zm[d]})

    for d in far:

        @pl.when(zp[d] < ZT)
        def _():
            z_copy(d).start()

    pair = remote(psend, prec, p_ss, p_rs, sibling)

    def gz_copy(d):
        return remote(agz, gz.at[c, x, tile], gz_ss.at[d], gz_rs.at[d], {"seq_0": zp[d]})

    def gz_arrival(d):
        return remote(agz, gz.at[c, x, zmt[d]], gz_ss.at[d], gz_rs.at[d], {"seq_0": zm[d]})

    def gx_copy(d):
        return remote(agx, gx.at[c, tile, x], gx_ss.at[d], gx_rs.at[d], {"seq_1": xp[d]})

    def gx_arrival(d):
        return remote(agx, gx.at[c, tile, xm[d]], gx_ss.at[d], gx_rs.at[d], {"seq_1": xm[d]})

    def gxz_copy(d):
        return remote(gx.at[c, tile], gx.at[c, tile], gxz_ss.at[d], gxz_rs.at[d], {"seq_0": zp[d]})

    def gxz_arrival(d):
        return remote(gx.at[c, zmt[d]], gx.at[c, zmt[d]], gxz_ss.at[d], gxz_rs.at[d], {"seq_0": zm[d]})

    def ga_copy(d):
        return remote(aga.at[zp[d]], ga.at[c, x, tile], ga_ss.at[d], ga_rs.at[d], {"seq_0": zp[d]})

    def ga_arrival(d):
        return remote(aga.at[0], ga.at[c, x, zmt[d]], ga_ss.at[d], ga_rs.at[d], {"seq_0": zm[d]})

    @pl.when(active)
    def _():
        for d in range(1, NX):
            zx_arrival(d).wait_recv()
        values = {}

        def keep(key, half, value):
            values[key, half] = value

        parts = [zx.at[x]] + [zxbuf.at[xm[d]] for d in range(1, NX)]
        last_top, last_total = merge_packed(parts, 2, [(0, 0, 3)], keep)
        for d in range(1, NZ):
            z_arrival(d).wait_recv()
        parts = [zsend.at[tile]] + [zbuf.at[zm[d]] for d in range(1, NZ)]
        top, total = merge_packed(parts, 6, [(h, 2 * h, h) for h in range(3)], keep)
        top = jnp.where(lane == 3, rolled(last_top, 3), top)
        total = jnp.where(lane == 3, rolled(last_total, 3), total)
        first = c == 0
        products = []
        for h in range(4):
            whole = jnp.broadcast_to(total[:, h : h + 1], (8, 128))
            halves = [(values[h, half] / whole).astype(BF16) for half in range(2)]
            attn = jnp.concatenate(halves, axis=1)
            start = pl.multiple_of(c * 1024 + h * HD, HD)
            products.append(jnp.dot(attn, wo[pl.ds(start, HD), :], preferred_element_type=F32))
            low, high = halves[0].astype(F32), halves[1].astype(F32)
            attn_all[4 * c + h] = jnp.where(first, low, high)
            psend[8 + h] = jnp.where(first, high, low)
        partial = products[0] + products[1] + products[2] + products[3]
        for i in range(8):
            psend[i] = partial[:, i * 128 : (i + 1) * 128]
        pair.start()
        start = pl.multiple_of(tile * 8, 8)
        own_hidden = hid[x, pl.ds(start, 8), :]
        target = goal[x, pl.ds(start, 8), :]
        which = emb_ref[x // 2]
        pair.wait_recv()
        resid = own_hidden + (partial + jnp.concatenate([prec[i] for i in range(8)], axis=1))
        inverse = lax.rsqrt(jnp.mean(resid * resid, axis=1, keepdims=True) + 1e-06)
        gain = og_ref[...]
        normed = resid * inverse * gain
        real = start + lax.broadcasted_iota(jnp.int32, (8, 1), 0) < ACT
        heads = oh[which]
        back = jnp.zeros((8, D), F32)
        for j in range(ADIM):
            head = heads[j : j + 1, :]
            velocity = jnp.sum(normed * head, axis=1, keepdims=True)
            dvel = 2.0 * (velocity - target[:, j : j + 1]) / (8 * ROWS)
            back = back + jnp.where(real, dvel, 0.0) * head
        scaled = back * gain
        mean = jnp.mean(resid * scaled, axis=1, keepdims=True)
        dresid = inverse * scaled - inverse * inverse * inverse * resid * mean
        dresid = dresid.astype(BF16).astype(F32)
        own = jnp.where(first, dresid[:, :512], dresid[:, 512:])
        for i in range(3):
            agz[i] = own[:, i * 128 : (i + 1) * 128]
        for d in far:
            gz_copy(d).start()
        stats = jnp.where(lane < 32, top, rolled(total, 32))
        for h in range(4):
            delta = jnp.sum(products[h] * dresid, axis=1, keepdims=True)
            stats = jnp.where(lane == 64 + h, delta, stats)
        agx[0] = own[:, 384:]
        agx[1] = stats
        for d in near:
            gx_copy(d).start()
        gz[c, x, tile] = agz[...]
        gx[c, tile, x] = agx[...]
        for h in range(4):
            attn_all[4 * other + h] = prec[8 + h]
        for zz in range(NZ):
            aga[zz] = attn_all[zz]
        ga[c, x, tile] = aga[z]
        for d in range(1, NX):
            gx_arrival(d).wait_recv()
        for d in far:
            gxz_copy(d).start()
        for d in far:
            ga_copy(d).start()

    def gzx_copy(d):
        return remote(gz.at[c, x], gz.at[c, x], gzx_ss.at[d], gzx_rs.at[d], {"seq_1": xp[d]})

    def gzx_arrival(d):
        return remote(gz.at[c, xm[d]], gz.at[c, xm[d]], gzx_ss.at[d], gzx_rs.at[d], {"seq_1": xm[d]})

    def gzc_copy(d):
        return remote(gz.at[c, xm[d]], gz.at[c, xm[d]], gzc_ss.at[d], gzc_rs.at[d], sibling)

    def gzc_arrival(d):
        return remote(gz.at[other, xm[d]], gz.at[other, xm[d]], gzc_ss.at[d], gzc_rs.at[d], sibling)

    gxc = remote(gx.at[c], gx.at[c], gxc_ss, gxc_rs, sibling)
    gxc_arrival = remote(gx.at[other], gx.at[other], gxc_ss, gxc_rs, sibling)

    def gax_copy(d):
        return remote(ga.at[c, x], ga.at[c, x], gax_ss.at[d], gax_rs.at[d], {"seq_1": xp[d]})

    def gax_arrival(d):
        return remote(ga.at[c, xm[d]], ga.at[c, xm[d]], gax_ss.at[d], gax_rs.at[d], {"seq_1": xm[d]})

    gac = remote(ga.at[c], ga.at[c], gac_ss, gac_rs, sibling)
    gac_arrival = remote(ga.at[other], ga.at[other], gac_ss, gac_rs, sibling)

    for d in range(1, NZ):

        @pl.when(zm[d] < ZT)
        def _():
            gz_arrival(d).wait_recv()

    for d in near:
        gzx_copy(d).start()
    gzc_copy(0).start()
    for d in (1, 3, 2):
        gzx_arrival(d).wait_recv()
        gzc_copy(d).start()
    for d in range(1, NZ):

        @pl.when(zm[d] < ZT)
        def _():
            gxz_arrival(d).wait_recv()

    gxc.start()
    for d in range(1, NZ):

        @pl.when(zm[d] < ZT)
        def _():
            ga_arrival(d).wait_recv()

    for d in near:
        gax_copy(d).start()
    for d in range(NX):
        gzc_arrival(d).wait_recv()
    gxc_arrival.wait_recv()

    for t in range(0, 28, 2):
        for core in range(2):
            for i in range(4):
                both = []
                for u in (t, t + 1):
                    xx, zz = u // 7, u % 7
                    both.append(gz[core, xx, zz, i] if i < 3 else gx[core, zz, xx, 0])
                lo = core * 512 + i * 128
                db[t * 8 : t * 8 + 16, lo : lo + 128] = jnp.concatenate(both, axis=0).astype(BF16)

    def core2(s):
        return remote(gq.at[0, s], cbuf2.at[s], c2_ss.at[s], c2_rs.at[s], sibling)

    def z2_copy(d):
        return remote(zs2.at[zp[d]], zbuf2.at[z], z2_ss.at[d], z2_rs.at[d], {"seq_0": zp[d]})

    def z2_arrival(d):
        return remote(zs2.at[zm[d]], zbuf2.at[zm[d]], z2_ss.at[d], z2_rs.at[d], {"seq_0": zm[d]})

    def x2_copy(d):
        return remote(xs2.at[xp[d]], xbuf2.at[x], x2_ss.at[d], x2_rs.at[d], {"seq_1": xp[d]})

    def x2_arrival(d):
        return remote(xs2.at[xm[d]], xbuf2.at[xm[d]], x2_ss.at[d], x2_rs.at[d], {"seq_1": xm[d]})

    for i in range(2):
        half = other if i == 0 else c
        for t in range(28):
            xx, zz = t // 7, t % 7
            stats = gx[half, zz, xx, 1]
            scale = jnp.exp(rolled(local_peak[i, xx], -4 * zz) - stats) / rolled(stats, 96)
            for h in range(4):
                scale_ref[h, t * 8 : t * 8 + 8] = jnp.broadcast_to(scale[:, h : h + 1], (8, 128))
                delta_ref[h, t * 8 : t * 8 + 8] = jnp.broadcast_to(stats[:, 64 + h : 65 + h], (8, 128))
        start = pl.multiple_of(half * 1024, 1024)
        dattn = dot_nt(db[...], wo[pl.ds(start, 1024), :]).astype(BF16)
        for s in (1, 0):
            rows = slice(s * PAD, (s + 1) * PAD)
            stacked = jnp.concatenate(
                [dattn[rows, h * HD : (h + 1) * HD] for h in range(4)], axis=0
            )
            dvalues = dot_nt(stacked, v_ref[s])
            parts = []
            for h in range(4):
                delta = delta_ref[h, rows]
                scale = scale_ref[h, rows]
                line = []
                for k in range(4):
                    cols = slice(k * 128, (k + 1) * 128)
                    dv = dvalues[h * PAD : (h + 1) * PAD, cols]
                    line.append((weights_ref[i, h, rows, cols] * scale * (dv - delta)).astype(BF16))
                parts.append(jnp.concatenate(line, axis=1))
            dscore = jnp.concatenate(parts, axis=0)
            grads = jnp.dot(dscore, k_ref[s], preferred_element_type=F32) * (1.0 / math.sqrt(HD))
            grads = grads.astype(BF16).astype(F32)
            for h in range(4):
                for k in range(2):
                    gq[i, s, 2 * h + k] = grads[h * PAD : (h + 1) * PAD, k * 128 : (k + 1) * 128]
            if i == 0:
                core2(s).start()
            elif s == 1:
                core2(1).wait_recv()
                for k in range(NZ):
                    zs2[k] = gq[1, 1, k] + cbuf2[1, k]
                for d in far:
                    z2_copy(d).start()
                zbuf2[z] = zs2[z]
    core2(0).wait_recv()
    blank = jnp.zeros((16, 128), F32)
    for k in range(NZ):
        turned = jnp.concatenate([gq[1, 0, k] + cbuf2[0, k], blank], axis=0).T
        for xx in range(NX):
            xs2[xx, k] = turned[xx * 32 : (xx + 1) * 32]
    for d in near:
        x2_copy(d).start()
    xbuf2[x] = xs2[x]

    for d in range(1, NX):
        gax_arrival(d).wait_recv()
    gac.start()
    gac_arrival.wait_recv()
    half_core = x // 2
    for t in range(0, 28, 2):
        both = jnp.concatenate([ga[half_core, u // 7, u % 7] for u in (t, t + 1)], axis=0)
        az[t * 8 : t * 8 + 16, :] = both.astype(BF16)
    ro_all[...] = dot_tn(az[...], db[...])
    offset = lax.rem(x, 2) * 64 + c * 32
    for bb in range(NB):
        ro[bb] = ro_all[pl.ds(pl.multiple_of(offset + 8 * bb, 8), 8), :]

    def y_copy(d):
        return remote(ro.at[bp[d]], yrec.at[b], y_ss.at[d], y_rs.at[d], {"batch": bp[d]})

    def y_arrival(d):
        return remote(ro.at[bm[d]], yrec.at[bm[d]], y_ss.at[d], y_rs.at[d], {"batch": bm[d]})

    for d in near:
        y_copy(d).start()
    yrec[b] = ro[b]

    def zx2_copy(d):
        return remote(zx2.at[xp[d]], zxbuf2.at[x], zx2_ss.at[d], zx2_rs.at[d], {"seq_1": xp[d]})

    def zx2_arrival(d):
        return remote(zx2.at[xm[d]], zxbuf2.at[xm[d]], zx2_ss.at[d], zx2_rs.at[d], {"seq_1": xm[d]})

    def w2_copy(d):
        return remote(ws2.at[zp[d]], wbuf2.at[z], w2_ss.at[d], w2_rs.at[d], {"seq_0": zp[d]})

    def w2_arrival(d):
        return remote(ws2.at[zm[d]], wbuf2.at[zm[d]], w2_ss.at[d], w2_rs.at[d], {"seq_0": zm[d]})

    for d in (1, 3, 2):
        x2_arrival(d).wait_recv()
    for k in range(NZ):
        ws2[k] = xbuf2[0, k] + xbuf2[1, k] + xbuf2[2, k] + xbuf2[3, k]
    for d in far:
        w2_copy(d).start()
    wbuf2[z] = ws2[z]
    for d in (1, 7, 2, 6, 3, 5, 4):
        z2_arrival(d).wait_recv()
    late = zbuf2[0]
    for k in range(1, NZ):
        late = late + zbuf2[k]
    turned = jnp.concatenate([late, blank], axis=0).T
    for xx in range(NX):
        zx2[xx] = turned[xx * 32 : (xx + 1) * 32]
    for d in near:
        zx2_copy(d).start()
    zxbuf2[x] = zx2[x]
    for d in range(1, NB):
        y_arrival(d).wait_recv()
    raw_o = yrec[0] + yrec[1] + yrec[2] + yrec[3]
    ro_all[0:8] = raw_o
    squares_o = jnp.sum(raw_o * raw_o, keepdims=True)
    for d in (1, 3, 2):
        zx2_arrival(d).wait_recv()
    late = zxbuf2[0] + zxbuf2[1] + zxbuf2[2] + zxbuf2[3]
    for d in (1, 7, 2, 6, 3, 5, 4):
        w2_arrival(d).wait_recv()
    early = wbuf2[0]
    for k in range(1, NZ):
        early = early + wbuf2[k]
    columns = jnp.concatenate([early, late], axis=1)
    product = jnp.dot(jnp.concatenate(thirds(columns), axis=0), nperm[...], preferred_element_type=F32)
    product = product[0:32] + (product[32:64] + product[64:96])
    for bb in range(NB):
        bsend[bb] = product[:, bb * 256 : (bb + 1) * 256]

    def b_copy(d):
        return remote(bsend.at[bp[d]], brec.at[b], b_ss.at[d], b_rs.at[d], {"batch": bp[d]})

    def b_arrival(d):
        return remote(bsend.at[bm[d]], brec.at[bm[d]], b_ss.at[d], b_rs.at[d], {"batch": bm[d]})

    for d in near:
        b_copy(d).start()
    brec[b] = bsend[b]
    for d in range(1, NB):
        b_arrival(d).wait_recv()
    raw_t = brec[0] + brec[1] + brec[2] + brec[3]
    squares = jnp.sum(raw_t * raw_t, keepdims=True) + squares_o
    e_send[...] = jnp.broadcast_to(squares, (1, 128))
    flats = [(dx, dy) for dx in (2, 1, 3, 0) for dy in (2, 1, 3, 0) if dx or dy]
    deeps = [(dz, dc) for dz in (4, 3, 5, 2, 6, 1, 7, 0) for dc in (1, 0) if dz or dc]
    alls = [(dz, dx, dc) for dz in (4, 3, 5, 2, 6, 1, 7, 0) for dx in (2, 1, 3, 0) for dc in (1, 0) if dz or dx or dc]

    def e_copy(i):
        dx, dy = flats[i]
        return remote(e_send, e_rec.at[flat], e_ss.at[i], e_rs.at[i], {"seq_1": xp[dx], "batch": bp[dy]})

    def e_arrival(i):
        dx, dy = flats[i]
        slot = e_rec.at[xm[dx] * NB + bm[dy]]
        return remote(e_send, slot, e_ss.at[i], e_rs.at[i], {"seq_1": xm[dx], "batch": bm[dy]})

    def f_copy(i):
        dz, dc = deeps[i]
        return remote(f_send, f_rec.at[deep], f_ss.at[i], f_rs.at[i], {"seq_0": zp[dz], "seq_2": cp[dc]})

    def f_arrival(i):
        dz, dc = deeps[i]
        slot = f_rec.at[zm[dz] * 2 + cp[dc]]
        return remote(f_send, slot, f_ss.at[i], f_rs.at[i], {"seq_0": zm[dz], "seq_2": cp[dc]})

    def d_copy(i):
        dz, dx, dc = alls[i]
        peer = zp[dz] * 8 + xp[dx] * 2 + cp[dc]
        device = {"seq_0": zp[dz], "seq_1": xp[dx], "seq_2": cp[dc]}
        return remote(drows.at[peer], drec.at[me], d_ss.at[i], d_rs.at[i], device)

    def d_arrival(i):
        dz, dx, dc = alls[i]
        peer = zm[dz] * 8 + xm[dx] * 2 + cp[dc]
        device = {"seq_0": zm[dz], "seq_1": xm[dx], "seq_2": cp[dc]}
        return remote(drows.at[peer], drec.at[peer], d_ss.at[i], d_rs.at[i], device)

    for i in range(15):
        e_copy(i).start()
    e_rec[flat] = e_send[...]
    spread = jnp.concatenate([jnp.where(x == i, raw_t, 0.0) for i in range(4)], axis=0).T
    for i in range(64):
        drows[i] = spread[4 * i : 4 * i + 4]
    for i in range(63):
        d_copy(i).start()
    drec[me] = drows[me]
    for i in range(15):
        e_arrival(i).wait_recv()
    f_send[...] = jnp.sum(e_rec[...], axis=0)
    for i in range(15):
        f_copy(i).start()
    f_rec[deep] = f_send[...]
    for i in range(63):
        d_arrival(i).wait_recv()
    blocks = []
    for core in range(2):
        for zz in range(NZ):
            base = zz * 8 + core
            blocks.append(drec[base] + drec[base + 2] + drec[base + 4] + drec[base + 6])
    raw_q = jnp.concatenate(blocks, axis=1)
    for i in range(15):
        f_arrival(i).wait_recv()
    norm = jnp.sqrt(jnp.sum(f_rec[...], axis=0))
    factor = jnp.minimum(1.0, 1.0 / (norm + 1e-06))[0:1, 0:1]
    q_out[...] = raw_q * factor
    o_out[...] = ro_all[0:8] * factor

    for d in range(NX):
        core_copy(d).wait_send()
        gzc_copy(d).wait_send()

        @pl.when(x != d)
        def _():
            x_copy(d).wait_send()

        if d:
            gzx_copy(d).wait_send()
            gax_copy(d).wait_send()
            x2_copy(d).wait_send()
            zx2_copy(d).wait_send()
            y_copy(d).wait_send()
            b_copy(d).wait_send()
    for s in range(2):
        core2(s).wait_send()
    gxc.wait_send()
    gac.wait_send()
    for d in range(1, NZ):
        z2_copy(d).wait_send()
        w2_copy(d).wait_send()

        @pl.when(zp[d] < ZT)
        def _():
            z_copy(d).wait_send()
            zf_copy(d).wait_send()

    @pl.when(active)
    def _():
        pair.wait_send()
        for d in range(1, NX):
            zx_copy(d).wait_send()
            gx_copy(d).wait_send()
        for d in range(1, NZ):
            gz_copy(d).wait_send()
            gxz_copy(d).wait_send()
            ga_copy(d).wait_send()

    for i in range(15):
        e_copy(i).wait_send()
        f_copy(i).wait_send()
    for i in range(63):
        d_copy(i).wait_send()


def local(
    actions,
    noise,
    times,
    embodiment,
    prefix_blocks,
    prefix_keys,
    prefix_values,
    input_heads,
    attn_gain,
    w_query,
    w_output,
    out_gain,
    output_heads,
):
    dma = pltpu.SemaphoreType.DMA

    def v(*shape, kind=F32):
        return pltpu.VMEM(shape, kind)

    def pairs(*counts):
        return [dma((n,)) if n else dma for n in counts for _ in range(2)]

    return pl.pallas_call(
        step_kernel,
        out_shape=(
            jax.ShapeDtypeStruct((4, HEADS * HD), F32),
            jax.ShapeDtypeStruct((8, D), F32),
        ),
        in_specs=[SMEM] * 3 + [VMEM] * 4 + [ANY] * 6,
        out_specs=(VMEM, VMEM),
        scratch_shapes=[
            v(4, ADIM, D), v(2, KEYS, HD, kind=BF16), v(2, KEYS, HD, kind=BF16), v(2, D, 1024, kind=BF16),
            v(2048, D, kind=BF16), v(4, ADIM, D), v(4, ADIM, 128), v(4, 128, ADIM), v(4, HALF, D),
            v(ALL, D, kind=BF16), v(256, D, kind=BF16),
            v(2, 4, ALL, KEYS), v(2, NX, 8, 128), v(2, NX, 58, 8, 128), v(NX, 58, 8, 128),
            v(NX, 44, 8, 128), v(NX, 44, 8, 128), v(ZT, 9, 8, 128), v(NZ, 9, 8, 128),
            v(NX, 3, 8, 128), v(NX, 3, 8, 128), v(ZT, 7, 8, 128), v(NZ, 7, 8, 128),
            v(12, 8, 128), v(12, 8, 128), v(8, 8, 128), v(3, 8, 128), v(2, 8, 128), v(NZ, 8, 128),
            v(2, NX, ZT, 3, 8, 128), v(2, ZT, NX, 2, 8, 128), v(2, NX, ZT, 8, 128),
            v(ALL, D, kind=BF16), v(4, ALL, 128), v(4, ALL, 128), v(ALL, 128, kind=BF16), v(128, D),
            v(NB, 8, D), v(2, 2, NZ, PAD, 128), v(2, NZ, PAD, 128), v(NZ, PAD, 128), v(NZ, PAD, 128),
            v(NX, 32, 128), v(NX, 32, 128), v(NX, NZ, 32, 128), v(NX, NZ, 32, 128),
            v(NZ, 32, 128), v(NZ, 32, 128), v(NB, 32, 256), v(NB, 32, 256), v(NB, 8, D),
            v(64, 4, 128), v(64, 4, 128), v(1, 128), v(16, 1, 128), v(1, 128), v(16, 1, 128),
            dma((7,)),
        ]
        + pairs(NX, NX, NZ, NX, NZ, 0, NZ, NX, NX, NX, NZ, 0, NZ, NX, 0, 2, NZ, NX, NX, NZ, NB, NB, 64, 16, 16),
        compiler_params=pltpu.CompilerParams(
            collective_id=0, has_side_effects=True, vmem_limit_bytes=44 * 1024 * 1024
        ),
    )(
        times, embodiment, prefix_blocks, jnp.swapaxes(actions, 1, 2), jnp.swapaxes(noise, 2, 3),
        attn_gain[None, :], out_gain[None, :], input_heads, prefix_keys, prefix_values, w_query, w_output,
        jnp.swapaxes(output_heads, 1, 2),
    )


def solution(mesh):
    torus = Mesh(
        mesh.devices.reshape(NZ, NX, 2, mesh.shape["batch"]), ("seq_0", "seq_1", "seq_2", "batch")
    )
    placed = (
        P("batch", None, None),
        P("batch", None, None, None),
        P("batch", None),
        P("batch"),
        P("batch"),
        P("batch", SEQ, None),
        P("batch", SEQ, None),
        P(),
        P(),
        P(),
        P(),
        P(),
        P(),
    )
    return jax.shard_map(
        local,
        mesh=torus,
        in_specs=placed,
        out_specs=(P(SEQ_BATCH, None), P(SEQ_BATCH, None)),
        check_vma=False,
    )
```

```python
import math

import jax
import jax.numpy as jnp
from jax import lax
from jax.experimental import pallas as pl
from jax.experimental.pallas import tpu as pltpu
from jax.sharding import Mesh
from jax.sharding import PartitionSpec as P

D = 1024
HEADS = 8
HD = 256
ACT = 50
ADIM = 32
TSTEPS = 2
BLOCK = 128
ROWS = TSTEPS * ACT
PAD = 112
HALF = 56
ALL = 2 * PAD
KEYS = 512
NZ = 8
NX = 4
NB = 4
ZT = 7
SEQ = ("seq_0", "seq_1", "seq_2")
SEQ_BATCH = ("seq_0", "seq_1", "seq_2", "batch")
MESH = pl.DeviceIdType.MESH
F32 = jnp.float32
BF16 = jnp.bfloat16
VMEM = pl.BlockSpec(memory_space=pltpu.VMEM)
HBM = pl.BlockSpec(memory_space=pltpu.HBM)


def dot_nt(a, b):
    return lax.dot_general(a, b, (((1,), (1,)), ((), ())), preferred_element_type=F32)


def dot_tn(a, b):
    return lax.dot_general(a, b, (((0,), (0,)), ((), ())), preferred_element_type=F32)


def lanes_of(shape=(8, 128)):
    return lax.broadcasted_iota(jnp.int32, shape, len(shape) - 1)


def thirds(value):
    high = value.astype(BF16)
    rest = value - high.astype(F32)
    middle = rest.astype(BF16)
    return high, middle, (rest - middle.astype(F32)).astype(BF16)


def remote(src, dst, ss, rs, device):
    return pltpu.make_async_remote_copy(
        src_ref=src, dst_ref=dst, send_sem=ss, recv_sem=rs, device_id=device, device_id_type=MESH
    )


def rolled(value, lanes):
    lanes = lanes % 128
    return pltpu.roll(value, lanes, axis=1) if lanes else value


def merge(parts, peaks, totals, entries, put):
    top = peaks[0]
    for one in peaks[1:]:
        top = jnp.maximum(top, one)
    scales = [jnp.exp(one - top) for one in peaks]
    total = scales[0] * totals[0]
    for scale, one in zip(scales[1:], totals[1:]):
        total = total + scale * one
    for column, first, key in entries:
        wide = [jnp.broadcast_to(scale[:, column : column + 1], (8, 128)) for scale in scales]
        for half in range(2):
            value = wide[0] * parts[0][first + half]
            for scale, part in zip(wide[1:], parts[1:]):
                value = value + scale * part[first + half]
            put(key, half, value)
    return top, total


def merge_packed(parts, stat, entries, put):
    stats = [part[stat] for part in parts]
    return merge(parts, stats, [rolled(one, 96) for one in stats], entries, put)


def step_kernel(
    times_hbm, emb_hbm, blocks_hbm,
    act_hbm, noise_hbm, ag_hbm, og_hbm, ih_hbm, k_hbm, v_hbm, wq_hbm, wo_hbm, oh_hbm,
    q_out, o_out,
    times_ref, emb_ref, blocks_ref, act_ref, noise_ref, ag_ref, og_ref, ih, k_ref, v_ref, wq, wo, oh, mixed_in, goal, hid, nrm, nperm,
    weights_ref, local_peak, sums, cbuf, acc, xbuf, zf, zfbuf, zx, zxbuf, zsend, zbuf,
    psend, prec, attn_all, agz, aga, g, ga,
    db, scale_ref, delta_ref, az, ro_all, ro, gq, cbuf2, zs2, zbuf2, zx2, zxbuf2, xs2, xbuf2, ws2, wbuf2,
    bsend, brec, yrec, drows, drec, e_send, e_rec, f_send, f_rec,
    load, c_ss, c_rs, x_ss, x_rs, zf_ss, zf_rs, zx_ss, zx_rs, z_ss, z_rs, p_ss, p_rs,
    gz_ss, gz_rs, gzx_ss, gzx_rs, gzc_ss, gzc_rs,
    ga_ss, ga_rs, gax_ss, gax_rs, gac_ss, gac_rs,
    c2_ss, c2_rs, z2_ss, z2_rs, zx2_ss, zx2_rs, x2_ss, x2_rs, w2_ss, w2_rs,
    y_ss, y_rs, b_ss, b_rs, d_ss, d_rs, e_ss, e_rs, f_ss, f_rs,
):
    z = lax.axis_index("seq_0")
    x = lax.axis_index("seq_1")
    c = lax.axis_index("seq_2")
    b = lax.axis_index("batch")
    other = 1 - c
    me = (z * NX + x) * 2 + c
    flat = x * NB + b
    deep = z * 2 + c
    tile = jnp.minimum(z, ZT - 1)
    active = z < ZT
    lane = lanes_of()
    zp = [lax.rem(z + d, NZ) for d in range(NZ)]
    zm = [lax.rem(z + NZ - d, NZ) for d in range(NZ)]
    xp = [lax.rem(x + d, NX) for d in range(NX)]
    xm = [lax.rem(x + NX - d, NX) for d in range(NX)]
    bp = [lax.rem(b + d, NB) for d in range(NB)]
    bm = [lax.rem(b + NB - d, NB) for d in range(NB)]
    cp = [c, other]
    zt = [jnp.minimum(one, ZT - 1) for one in zp]
    zmt = [jnp.minimum(one, ZT - 1) for one in zm]
    far = (4, 3, 5, 2, 6, 1, 7)
    near = (2, 1, 3)
    sibling = {"seq_2": other}

    barrier = pltpu.get_barrier_semaphore()
    pl.semaphore_signal(barrier, inc=1, device_id=sibling, device_id_type=MESH)
    for d in far:
        pl.semaphore_signal(barrier, inc=1, device_id={"seq_0": zp[d]}, device_id_type=MESH)
    for d in near:
        pl.semaphore_signal(barrier, inc=1, device_id={"seq_1": xp[d]}, device_id_type=MESH)
        pl.semaphore_signal(barrier, inc=1, device_id={"batch": bp[d]}, device_id_type=MESH)

    def wq_half(half):
        return wq_hbm.at[:, pl.ds(pl.multiple_of(half * 1024, 1024), 1024)]

    plan = (
        (times_hbm, times_ref), (act_hbm, act_ref), (noise_hbm, noise_ref), (emb_hbm, emb_ref),
        (ih_hbm, ih), (ag_hbm, ag_ref), (wq_half(other), wq.at[0]), (blocks_hbm, blocks_ref),
        (k_hbm, k_ref), (v_hbm, v_ref), (wq_half(c), wq.at[1]), (wo_hbm, wo), (oh_hbm, oh), (og_hbm, og_ref),
    )

    def loads(i):
        return pltpu.make_async_copy(plan[i][0], plan[i][1], load.at[i])

    for i in range(14):
        loads(i).start()
    loads(0).wait()

    channel = lax.broadcasted_iota(jnp.int32, (8, 512), 1).astype(F32)
    frequency = jnp.exp(-math.log(10000.0) * channel / 512)
    row = lax.broadcasted_iota(jnp.int32, (8, 512), 0)
    moment = jnp.zeros((8, 512), F32)
    for st in range(4):
        moment = jnp.where(row == st, times_ref[st // 2, st % 2], moment)
    phase = moment * 1000.0 * frequency
    temb = jnp.concatenate([jnp.sin(phase), jnp.cos(phase)], axis=1)
    mixed_in[...] = jnp.zeros((4, ADIM, 128), F32)
    for i in (1, 2):
        loads(i).wait()
    for s in range(2):
        act = act_ref[s]
        for t in range(2):
            noise = noise_ref[s, t]
            level = times_ref[s, t]
            mixed_in[2 * s + t, :, 0:ACT] = noise - act
            goal[2 * s + t] = mixed_in[2 * s + t].T
            mixed_in[2 * s + t, :, 0:ACT] = level * noise + (1.0 - level) * act
    for i in (3, 4, 5):
        loads(i).wait()
    for s in range(2):
        wh, wm, wl = thirds(ih[emb_ref[s]])
        right = jnp.concatenate([wh, wm, wh, wl, wm, wh], axis=0)
        both = []
        for t in range(2):
            ah, am, al = thirds(mixed_in[2 * s + t])
            left = jnp.concatenate([ah, ah, am, ah, am, al], axis=0)
            hidden = dot_tn(left, right)[0:HALF] + temb[2 * s + t : 2 * s + t + 1, :]
            hid[2 * s + t] = hidden
            both.append(hidden)
        hidden = jnp.concatenate(both, axis=0)
        inverse = lax.rsqrt(jnp.mean(hidden * hidden, axis=1, keepdims=True) + 1e-06)
        nrm[s * PAD : (s + 1) * PAD, :] = (hidden * inverse * ag_ref[...]).astype(BF16)

    def core_copy(chunk):
        return remote(sums.at[0, chunk], cbuf.at[chunk], c_ss.at[chunk], c_rs.at[chunk], sibling)

    for i in range(2):
        loads(6 if i == 0 else 10).wait()
        q = jnp.dot(nrm[...], wq[i], preferred_element_type=F32)
        q = (q * (1.0 / math.sqrt(HD))).astype(BF16)
        if i == 0:
            for n in (7, 8, 9):
                loads(n).wait()
        for s in range(2):
            qs = jnp.concatenate(
                [q[s * PAD : (s + 1) * PAD, h * HD : (h + 1) * HD] for h in range(4)], axis=0
            )
            scores = dot_nt(qs, k_ref[s])
            limit = BLOCK * blocks_ref[s] - me * KEYS
            valid = lax.broadcasted_iota(jnp.int32, scores.shape, 1) < limit
            scores = jnp.where(valid, scores, -1e30)
            peak = jnp.max(scores, axis=1, keepdims=True)
            weights = jnp.where(valid, jnp.exp(scores - peak), 0.0)
            total = jnp.sum(weights, axis=1, keepdims=True)
            mixed = jnp.dot(weights.astype(BF16), v_ref[s], preferred_element_type=F32)
            for h in range(4):
                weights_ref[i, h, s * PAD : (s + 1) * PAD, :] = weights[h * PAD : (h + 1) * PAD]
            for xx in (2 * s, 2 * s + 1):
                peaks = jnp.zeros((8, 128), F32)
                totals = jnp.ones((8, 128), F32)
                for zz in range(ZT):
                    for h in range(4):
                        j = zz * 4 + h
                        at = h * PAD + (7 * xx + zz - 14 * s) * 8
                        peaks = jnp.where(lane == j, peak[at : at + 8], peaks)
                        totals = jnp.where(lane == j, total[at : at + 8], totals)
                        sums[i, xx, 2 * j] = mixed[at : at + 8, :128]
                        sums[i, xx, 2 * j + 1] = mixed[at : at + 8, 128:]
                sums[i, xx, 56] = peaks
                sums[i, xx, 57] = totals
                local_peak[i, xx] = peaks
            if i == 0:
                if s == 0:
                    pl.semaphore_wait(barrier, 1 + NX - 1 + NZ - 1 + NB - 1)
                core_copy(2 * s).start()
                core_copy(2 * s + 1).start()

    def x_copy(xx):
        return remote(acc.at[xx], xbuf.at[x], x_ss.at[xx], x_rs.at[x], {"seq_1": xx})

    def x_arrival(d):
        return remote(acc.at[xm[d]], xbuf.at[xm[d]], x_ss.at[xm[d]], x_rs.at[xm[d]], {"seq_1": xm[d]})

    def zf_copy(d):
        return remote(zf.at[zt[d]], zfbuf.at[z], zf_ss.at[d], zf_rs.at[d], {"seq_0": zp[d]})

    def zf_arrival(d):
        return remote(zf.at[0], zfbuf.at[zm[d]], zf_ss.at[d], zf_rs.at[d], {"seq_0": zm[d]})

    tops = []
    for xx in range(NX):
        core_copy(xx).wait_recv()

        def put_core(key, half, value):
            zz, h = key
            if h < 3:
                acc[xx, (zz * 3 + h) * 2 + half] = value
            else:
                zf[zz, xx * 2 + half] = value

        parts = (sums.at[1, xx], cbuf.at[xx])
        entries = [(zz * 4 + h, 2 * (zz * 4 + h), (zz, h)) for zz in range(ZT) for h in range(4)]
        top, total = merge(parts, [p[56] for p in parts], [p[57] for p in parts], entries, put_core)
        acc[xx, 42] = top
        acc[xx, 43] = total
        tops.append((top, total))

        @pl.when(x != xx)
        def _():
            x_copy(xx).start()

    for zz in range(ZT):
        stats = jnp.zeros((8, 128), F32)
        for xx in range(NX):
            top, total = tops[xx]
            stats = jnp.where(lane == xx, rolled(top, xx - 4 * zz - 3), stats)
            stats = jnp.where(lane == 32 + xx, rolled(total, 32 + xx - 4 * zz - 3), stats)
        zf[zz, 8] = stats
    for d in far:

        @pl.when(zp[d] < ZT)
        def _():
            zf_copy(d).start()

    for bb in range(NB):
        col = lax.broadcasted_iota(jnp.int32, (D, 256), 1)
        natural = (col // 4) * 16 + bb * 4 + lax.rem(col, 4)
        pick = (lax.broadcasted_iota(jnp.int32, (D, 256), 0) == natural).astype(F32).astype(BF16)
        placed = jnp.dot(nrm[...], pick, preferred_element_type=F32).astype(BF16)
        cols = slice(bb * 256, (bb + 1) * 256)
        nperm[0:ALL, cols] = placed
    nperm[ALL:, :] = jnp.zeros((256 - ALL, D), BF16)
    for i in (11, 12, 13):
        loads(i).wait()

    def zx_copy(d):
        return remote(zx.at[xp[d]], zxbuf.at[x], zx_ss.at[d], zx_rs.at[d], {"seq_1": xp[d]})

    def zx_arrival(d):
        return remote(zx.at[xm[d]], zxbuf.at[xm[d]], zx_ss.at[d], zx_rs.at[d], {"seq_1": xm[d]})

    @pl.when(active)
    def _():
        for d in range(1, NZ):
            zf_arrival(d).wait_recv()

        def put_zx(key, half, value):
            zx[key, half] = value

        parts = [zf.at[tile]] + [zfbuf.at[zm[d]] for d in range(1, NZ)]
        top, total = merge_packed(parts, 8, [(xx, 2 * xx, xx) for xx in range(NX)], put_zx)
        for xx in range(NX):
            zx[xx, 2] = jnp.where(lane < 32, rolled(top, -xx), rolled(total, 32 - xx))
        for d in near:
            zx_copy(d).start()

    for d in (1, 3, 2):
        x_arrival(d).wait_recv()

    def put_z(key, half, value):
        zz, h = key
        zsend[zz, h * 2 + half] = value

    parts = [acc.at[x]] + [xbuf.at[xm[d]] for d in range(1, NX)]
    entries = [(zz * 4 + h, 2 * (zz * 3 + h), (zz, h)) for zz in range(ZT) for h in range(3)]
    top, total = merge(parts, [p[42] for p in parts], [p[43] for p in parts], entries, put_z)
    for zz in range(ZT):
        zsend[zz, 6] = jnp.where(lane < 32, rolled(top, -4 * zz), rolled(total, 32 - 4 * zz))

    def z_copy(d):
        return remote(zsend.at[zt[d]], zbuf.at[z], z_ss.at[d], z_rs.at[d], {"seq_0": zp[d]})

    def z_arrival(d):
        return remote(zsend.at[0], zbuf.at[zm[d]], z_ss.at[d], z_rs.at[d], {"seq_0": zm[d]})

    for d in far:

        @pl.when(zp[d] < ZT)
        def _():
            z_copy(d).start()

    pair = remote(psend, prec, p_ss, p_rs, sibling)

    def gz_copy(d):
        return remote(agz, g.at[c, x, tile], gz_ss.at[d], gz_rs.at[d], {"seq_0": zp[d]})

    def gz_arrival(d):
        return remote(agz, g.at[c, x, zmt[d]], gz_ss.at[d], gz_rs.at[d], {"seq_0": zm[d]})

    def gzx_copy(d, dx):
        own = g.at[c, x, zmt[d]]
        return remote(own, own, gzx_ss.at[d, dx], gzx_rs.at[d, dx], {"seq_1": xp[dx]})

    def gzx_arrival(d, dx):
        slot = g.at[c, xm[dx], zmt[d]]
        return remote(slot, slot, gzx_ss.at[d, dx], gzx_rs.at[d, dx], {"seq_1": xm[dx]})

    def ga_copy(d):
        return remote(aga.at[zp[d]], ga.at[c, x, tile], ga_ss.at[d], ga_rs.at[d], {"seq_0": zp[d]})

    def ga_arrival(d):
        return remote(aga.at[0], ga.at[c, x, zmt[d]], ga_ss.at[d], ga_rs.at[d], {"seq_0": zm[d]})

    @pl.when(active)
    def _():
        for d in range(1, NX):
            zx_arrival(d).wait_recv()
        values = {}

        def keep(key, half, value):
            values[key, half] = value

        parts = [zx.at[x]] + [zxbuf.at[xm[d]] for d in range(1, NX)]
        last_top, last_total = merge_packed(parts, 2, [(0, 0, 3)], keep)
        for d in range(1, NZ):
            z_arrival(d).wait_recv()
        parts = [zsend.at[tile]] + [zbuf.at[zm[d]] for d in range(1, NZ)]
        top, total = merge_packed(parts, 6, [(h, 2 * h, h) for h in range(3)], keep)
        top = jnp.where(lane == 3, rolled(last_top, 3), top)
        total = jnp.where(lane == 3, rolled(last_total, 3), total)
        first = c == 0
        products = []
        for h in range(4):
            whole = jnp.broadcast_to(total[:, h : h + 1], (8, 128))
            halves = [(values[h, half] / whole).astype(BF16) for half in range(2)]
            attn = jnp.concatenate(halves, axis=1)
            start = pl.multiple_of(c * 1024 + h * HD, HD)
            products.append(jnp.dot(attn, wo[pl.ds(start, HD), :], preferred_element_type=F32))
            low, high = halves[0].astype(F32), halves[1].astype(F32)
            attn_all[4 * c + h] = jnp.where(first, low, high)
            psend[8 + h] = jnp.where(first, high, low)
        partial = products[0] + products[1] + products[2] + products[3]
        for i in range(8):
            psend[i] = partial[:, i * 128 : (i + 1) * 128]
        pair.start()
        start = pl.multiple_of(tile * 8, 8)
        own_hidden = hid[x, pl.ds(start, 8), :]
        target = goal[x, pl.ds(start, 8), :]
        which = emb_ref[x // 2]
        pair.wait_recv()
        resid = own_hidden + (partial + jnp.concatenate([prec[i] for i in range(8)], axis=1))
        inverse = lax.rsqrt(jnp.mean(resid * resid, axis=1, keepdims=True) + 1e-06)
        gain = og_ref[...]
        normed = resid * inverse * gain
        real = start + lax.broadcasted_iota(jnp.int32, (8, 1), 0) < ACT
        heads = oh[which]
        back = jnp.zeros((8, D), F32)
        for j in range(ADIM):
            head = heads[j : j + 1, :]
            velocity = jnp.sum(normed * head, axis=1, keepdims=True)
            dvel = 2.0 * (velocity - target[:, j : j + 1]) / (8 * ROWS)
            back = back + jnp.where(real, dvel, 0.0) * head
        scaled = back * gain
        mean = jnp.mean(resid * scaled, axis=1, keepdims=True)
        dresid = inverse * scaled - inverse * inverse * inverse * resid * mean
        dresid = dresid.astype(BF16).astype(F32)
        own = jnp.where(first, dresid[:, :512], dresid[:, 512:])
        stats = jnp.where(lane < 32, top, rolled(total, 32))
        for h in range(4):
            delta = jnp.sum(products[h] * dresid, axis=1, keepdims=True)
            stats = jnp.where(lane == 64 + h, delta, stats)
        for i in range(4):
            agz[i] = own[:, i * 128 : (i + 1) * 128]
        agz[4] = stats
        for d in far:
            gz_copy(d).start()
        g[c, x, tile] = agz[...]
        for dx in near:
            gzx_copy(0, dx).start()
        for h in range(4):
            attn_all[4 * other + h] = prec[8 + h]
        for zz in range(NZ):
            aga[zz] = attn_all[zz]
        ga[c, x, tile] = aga[z]
        for d in far:
            ga_copy(d).start()

    def gzc_copy(d):
        return remote(g.at[c, xm[d]], g.at[c, xm[d]], gzc_ss.at[d], gzc_rs.at[d], sibling)

    def gzc_arrival(d):
        return remote(g.at[other, xm[d]], g.at[other, xm[d]], gzc_ss.at[d], gzc_rs.at[d], sibling)

    def gax_copy(d):
        return remote(ga.at[c, x], ga.at[c, x], gax_ss.at[d], gax_rs.at[d], {"seq_1": xp[d]})

    def gax_arrival(d):
        return remote(ga.at[c, xm[d]], ga.at[c, xm[d]], gax_ss.at[d], gax_rs.at[d], {"seq_1": xm[d]})

    gac = remote(ga.at[c], ga.at[c], gac_ss, gac_rs, sibling)
    gac_arrival = remote(ga.at[other], ga.at[other], gac_ss, gac_rs, sibling)

    for d in (1, 7, 2, 6, 3, 5, 4):

        @pl.when(zm[d] < ZT)
        def _():
            gz_arrival(d).wait_recv()
            for dx in near:
                gzx_copy(d, dx).start()

    gzc_copy(0).start()
    for dx in (1, 3, 2):
        for d in range(NZ):

            @pl.when(zm[d] < ZT)
            def _():
                gzx_arrival(d, dx).wait_recv()

        gzc_copy(dx).start()
    for d in range(1, NZ):

        @pl.when(zm[d] < ZT)
        def _():
            ga_arrival(d).wait_recv()

    for d in near:
        gax_copy(d).start()
    for d in range(NX):
        gzc_arrival(d).wait_recv()

    for t in range(0, 28, 2):
        for core in range(2):
            for i in range(4):
                both = []
                for u in (t, t + 1):
                    xx, zz = u // 7, u % 7
                    both.append(g[core, xx, zz, i])
                lo = core * 512 + i * 128
                db[t * 8 : t * 8 + 16, lo : lo + 128] = jnp.concatenate(both, axis=0).astype(BF16)

    def core2(s):
        return remote(gq.at[0, s], cbuf2.at[s], c2_ss.at[s], c2_rs.at[s], sibling)

    def z2_copy(d):
        return remote(zs2.at[zp[d]], zbuf2.at[z], z2_ss.at[d], z2_rs.at[d], {"seq_0": zp[d]})

    def z2_arrival(d):
        return remote(zs2.at[zm[d]], zbuf2.at[zm[d]], z2_ss.at[d], z2_rs.at[d], {"seq_0": zm[d]})

    def x2_copy(d):
        return remote(xs2.at[xp[d]], xbuf2.at[x], x2_ss.at[d], x2_rs.at[d], {"seq_1": xp[d]})

    def x2_arrival(d):
        return remote(xs2.at[xm[d]], xbuf2.at[xm[d]], x2_ss.at[d], x2_rs.at[d], {"seq_1": xm[d]})

    for i in range(2):
        half = other if i == 0 else c
        for t in range(28):
            xx, zz = t // 7, t % 7
            stats = g[half, xx, zz, 4]
            scale = jnp.exp(rolled(local_peak[i, xx], -4 * zz) - stats) / rolled(stats, 96)
            for h in range(4):
                scale_ref[h, t * 8 : t * 8 + 8] = jnp.broadcast_to(scale[:, h : h + 1], (8, 128))
                delta_ref[h, t * 8 : t * 8 + 8] = jnp.broadcast_to(stats[:, 64 + h : 65 + h], (8, 128))
        start = pl.multiple_of(half * 1024, 1024)
        dattn = dot_nt(db[...], wo[pl.ds(start, 1024), :]).astype(BF16)
        for s in (1, 0):
            rows = slice(s * PAD, (s + 1) * PAD)
            stacked = jnp.concatenate(
                [dattn[rows, h * HD : (h + 1) * HD] for h in range(4)], axis=0
            )
            dvalues = dot_nt(stacked, v_ref[s])
            parts = []
            for h in range(4):
                delta = delta_ref[h, rows]
                scale = scale_ref[h, rows]
                line = []
                for k in range(4):
                    cols = slice(k * 128, (k + 1) * 128)
                    dv = dvalues[h * PAD : (h + 1) * PAD, cols]
                    line.append((weights_ref[i, h, rows, cols] * scale * (dv - delta)).astype(BF16))
                parts.append(jnp.concatenate(line, axis=1))
            dscore = jnp.concatenate(parts, axis=0)
            grads = jnp.dot(dscore, k_ref[s], preferred_element_type=F32) * (1.0 / math.sqrt(HD))
            grads = grads.astype(BF16).astype(F32)
            for h in range(4):
                for k in range(2):
                    gq[i, s, 2 * h + k] = grads[h * PAD : (h + 1) * PAD, k * 128 : (k + 1) * 128]
            if i == 0:
                core2(s).start()
            elif s == 1:
                core2(1).wait_recv()
                for k in range(NZ):
                    zs2[k] = gq[1, 1, k, 16:] + cbuf2[1, k, 16:]
                for d in far:
                    z2_copy(d).start()
                zbuf2[z] = zs2[z]
    core2(0).wait_recv()
    for k in range(NZ):
        first = gq[1, 0, k] + cbuf2[0, k]
        turned = jnp.concatenate([first, gq[1, 1, k, 0:16] + cbuf2[1, k, 0:16]], axis=0).T
        for xx in range(NX):
            xs2[xx, k] = turned[xx * 32 : (xx + 1) * 32]
    for d in near:
        x2_copy(d).start()
    xbuf2[x] = xs2[x]

    for d in range(1, NX):
        gax_arrival(d).wait_recv()
    gac.start()
    gac_arrival.wait_recv()
    half_core = x // 2
    for t in range(0, 28, 2):
        both = jnp.concatenate([ga[half_core, u // 7, u % 7] for u in (t, t + 1)], axis=0)
        az[t * 8 : t * 8 + 16, :] = both.astype(BF16)
    ro_all[...] = dot_tn(az[...], db[...])
    offset = lax.rem(x, 2) * 64 + c * 32
    for bb in range(NB):
        ro[bb] = ro_all[pl.ds(pl.multiple_of(offset + 8 * bb, 8), 8), :]

    def y_copy(d):
        return remote(ro.at[bp[d]], yrec.at[b], y_ss.at[d], y_rs.at[d], {"batch": bp[d]})

    def y_arrival(d):
        return remote(ro.at[bm[d]], yrec.at[bm[d]], y_ss.at[d], y_rs.at[d], {"batch": bm[d]})

    for d in near:
        y_copy(d).start()
    yrec[b] = ro[b]

    def zx2_copy(d):
        return remote(zx2.at[xp[d]], zxbuf2.at[x], zx2_ss.at[d], zx2_rs.at[d], {"seq_1": xp[d]})

    def zx2_arrival(d):
        return remote(zx2.at[xm[d]], zxbuf2.at[xm[d]], zx2_ss.at[d], zx2_rs.at[d], {"seq_1": xm[d]})

    def w2_copy(d):
        return remote(ws2.at[zp[d]], wbuf2.at[z], w2_ss.at[d], w2_rs.at[d], {"seq_0": zp[d]})

    def w2_arrival(d):
        return remote(ws2.at[zm[d]], wbuf2.at[zm[d]], w2_ss.at[d], w2_rs.at[d], {"seq_0": zm[d]})

    for d in (1, 3, 2):
        x2_arrival(d).wait_recv()
    for k in range(NZ):
        ws2[k] = xbuf2[0, k] + xbuf2[1, k] + xbuf2[2, k] + xbuf2[3, k]
    for d in far:
        w2_copy(d).start()
    wbuf2[z] = ws2[z]
    for d in (1, 7, 2, 6, 3, 5, 4):
        z2_arrival(d).wait_recv()
    late = zbuf2[0]
    for k in range(1, NZ):
        late = late + zbuf2[k]
    turned = jnp.concatenate([late, jnp.zeros((32, 128), F32)], axis=0).T
    for xx in range(NX):
        zx2[xx] = turned[xx * 32 : (xx + 1) * 32]
    for d in near:
        zx2_copy(d).start()
    zxbuf2[x] = zx2[x]
    for d in range(1, NB):
        y_arrival(d).wait_recv()
    raw_o = yrec[0] + yrec[1] + yrec[2] + yrec[3]
    ro_all[0:8] = raw_o
    squares_o = jnp.sum(raw_o * raw_o, keepdims=True)
    for d in (1, 3, 2):
        zx2_arrival(d).wait_recv()
    late = zxbuf2[0] + zxbuf2[1] + zxbuf2[2] + zxbuf2[3]
    for d in (1, 7, 2, 6, 3, 5, 4):
        w2_arrival(d).wait_recv()
    early = wbuf2[0]
    for k in range(1, NZ):
        early = early + wbuf2[k]
    columns = jnp.concatenate([early, late], axis=1)
    product = jnp.dot(jnp.concatenate(thirds(columns), axis=0), nperm[...], preferred_element_type=F32)
    product = product[0:32] + (product[32:64] + product[64:96])
    for bb in range(NB):
        bsend[bb] = product[:, bb * 256 : (bb + 1) * 256]

    def b_copy(d):
        return remote(bsend.at[bp[d]], brec.at[b], b_ss.at[d], b_rs.at[d], {"batch": bp[d]})

    def b_arrival(d):
        return remote(bsend.at[bm[d]], brec.at[bm[d]], b_ss.at[d], b_rs.at[d], {"batch": bm[d]})

    for d in near:
        b_copy(d).start()
    brec[b] = bsend[b]
    for d in range(1, NB):
        b_arrival(d).wait_recv()
    raw_t = brec[0] + brec[1] + brec[2] + brec[3]
    squares = jnp.sum(raw_t * raw_t, keepdims=True) + squares_o
    e_send[...] = jnp.broadcast_to(squares, (1, 128))
    flats = [(dx, dy) for dx in (2, 1, 3, 0) for dy in (2, 1, 3, 0) if dx or dy]
    deeps = [(dz, dc) for dz in (4, 3, 5, 2, 6, 1, 7, 0) for dc in (1, 0) if dz or dc]
    alls = [(dz, dx, dc) for dz in (4, 3, 5, 2, 6, 1, 7, 0) for dx in (2, 1, 3, 0) for dc in (1, 0) if dz or dx or dc]

    def e_copy(i):
        dx, dy = flats[i]
        return remote(e_send, e_rec.at[flat], e_ss.at[i], e_rs.at[i], {"seq_1": xp[dx], "batch": bp[dy]})

    def e_arrival(i):
        dx, dy = flats[i]
        slot = e_rec.at[xm[dx] * NB + bm[dy]]
        return remote(e_send, slot, e_ss.at[i], e_rs.at[i], {"seq_1": xm[dx], "batch": bm[dy]})

    def f_copy(i):
        dz, dc = deeps[i]
        return remote(f_send, f_rec.at[deep], f_ss.at[i], f_rs.at[i], {"seq_0": zp[dz], "seq_2": cp[dc]})

    def f_arrival(i):
        dz, dc = deeps[i]
        slot = f_rec.at[zm[dz] * 2 + cp[dc]]
        return remote(f_send, slot, f_ss.at[i], f_rs.at[i], {"seq_0": zm[dz], "seq_2": cp[dc]})

    def d_copy(i):
        dz, dx, dc = alls[i]
        peer = zp[dz] * 8 + xp[dx] * 2 + cp[dc]
        device = {"seq_0": zp[dz], "seq_1": xp[dx], "seq_2": cp[dc]}
        return remote(drows.at[peer], drec.at[me], d_ss.at[i], d_rs.at[i], device)

    def d_arrival(i):
        dz, dx, dc = alls[i]
        peer = zm[dz] * 8 + xm[dx] * 2 + cp[dc]
        device = {"seq_0": zm[dz], "seq_1": xm[dx], "seq_2": cp[dc]}
        return remote(drows.at[peer], drec.at[peer], d_ss.at[i], d_rs.at[i], device)

    for i in range(15):
        e_copy(i).start()
    e_rec[flat] = e_send[...]
    spread = jnp.concatenate([jnp.where(x == i, raw_t, 0.0) for i in range(4)], axis=0).T
    for i in range(64):
        drows[i] = spread[4 * i : 4 * i + 4]
    for i in range(63):
        d_copy(i).start()
    drec[me] = drows[me]
    for i in range(15):
        e_arrival(i).wait_recv()
    f_send[...] = jnp.sum(e_rec[...], axis=0)
    for i in range(15):
        f_copy(i).start()
    f_rec[deep] = f_send[...]
    for i in range(63):
        d_arrival(i).wait_recv()
    blocks = []
    for core in range(2):
        for zz in range(NZ):
            base = zz * 8 + core
            blocks.append(drec[base] + drec[base + 2] + drec[base + 4] + drec[base + 6])
    raw_q = jnp.concatenate(blocks, axis=1)
    for i in range(15):
        f_arrival(i).wait_recv()
    norm = jnp.sqrt(jnp.sum(f_rec[...], axis=0))
    factor = jnp.minimum(1.0, 1.0 / (norm + 1e-06))[0:1, 0:1]
    q_out[...] = raw_q * factor
    o_out[...] = ro_all[0:8] * factor

    for d in range(NX):
        core_copy(d).wait_send()
        gzc_copy(d).wait_send()

        @pl.when(x != d)
        def _():
            x_copy(d).wait_send()

        if d:
            gax_copy(d).wait_send()
            x2_copy(d).wait_send()
            zx2_copy(d).wait_send()
            y_copy(d).wait_send()
            b_copy(d).wait_send()
    for s in range(2):
        core2(s).wait_send()
    gac.wait_send()
    for d in range(NZ):

        @pl.when(zm[d] < ZT)
        def _():
            for dx in range(1, NX):
                gzx_copy(d, dx).wait_send()

    for d in range(1, NZ):
        z2_copy(d).wait_send()
        w2_copy(d).wait_send()

        @pl.when(zp[d] < ZT)
        def _():
            z_copy(d).wait_send()
            zf_copy(d).wait_send()

    @pl.when(active)
    def _():
        pair.wait_send()
        for d in range(1, NX):
            zx_copy(d).wait_send()
        for d in range(1, NZ):
            gz_copy(d).wait_send()
            ga_copy(d).wait_send()

    for i in range(15):
        e_copy(i).wait_send()
        f_copy(i).wait_send()
    for i in range(63):
        d_copy(i).wait_send()


def local(
    actions,
    noise,
    times,
    embodiment,
    prefix_blocks,
    prefix_keys,
    prefix_values,
    input_heads,
    attn_gain,
    w_query,
    w_output,
    out_gain,
    output_heads,
):
    dma = pltpu.SemaphoreType.DMA

    def v(*shape, kind=F32):
        return pltpu.VMEM(shape, kind)

    def pairs(*counts):
        return [dma((n,)) if n else dma for n in counts for _ in range(2)]

    return pl.pallas_call(
        step_kernel,
        out_shape=(
            jax.ShapeDtypeStruct((4, HEADS * HD), F32),
            jax.ShapeDtypeStruct((8, D), F32),
        ),
        in_specs=[HBM] * 13,
        out_specs=(VMEM, VMEM),
        scratch_shapes=[
            pltpu.SMEM((2, 2), F32), pltpu.SMEM((2,), jnp.int32), pltpu.SMEM((2,), jnp.int32),
            v(2, ADIM, ACT), v(2, 2, ADIM, ACT), v(1, D), v(1, D),
            v(4, ADIM, D), v(2, KEYS, HD, kind=BF16), v(2, KEYS, HD, kind=BF16), v(2, D, 1024, kind=BF16),
            v(2048, D, kind=BF16), v(4, ADIM, D), v(4, ADIM, 128), v(4, 128, ADIM), v(4, HALF, D),
            v(ALL, D, kind=BF16), v(256, D, kind=BF16),
            v(2, 4, ALL, KEYS), v(2, NX, 8, 128), v(2, NX, 58, 8, 128), v(NX, 58, 8, 128),
            v(NX, 44, 8, 128), v(NX, 44, 8, 128), v(ZT, 9, 8, 128), v(NZ, 9, 8, 128),
            v(NX, 3, 8, 128), v(NX, 3, 8, 128), v(ZT, 7, 8, 128), v(NZ, 7, 8, 128),
            v(12, 8, 128), v(12, 8, 128), v(8, 8, 128), v(5, 8, 128), v(NZ, 8, 128),
            v(2, NX, ZT, 5, 8, 128), v(2, NX, ZT, 8, 128),
            v(ALL, D, kind=BF16), v(4, ALL, 128), v(4, ALL, 128), v(ALL, 128, kind=BF16), v(128, D),
            v(NB, 8, D), v(2, 2, NZ, PAD, 128), v(2, NZ, PAD, 128), v(NZ, 96, 128), v(NZ, 96, 128),
            v(NX, 32, 128), v(NX, 32, 128), v(NX, NZ, 32, 128), v(NX, NZ, 32, 128),
            v(NZ, 32, 128), v(NZ, 32, 128), v(NB, 32, 256), v(NB, 32, 256), v(NB, 8, D),
            v(64, 4, 128), v(64, 4, 128), v(1, 128), v(16, 1, 128), v(1, 128), v(16, 1, 128),
            dma((14,)),
        ]
        + pairs(NX, NX, NZ, NX, NZ, 0, NZ)
        + [dma((NZ, NX)), dma((NZ, NX))]
        + pairs(NX, NZ, NX, 0, 2, NZ, NX, NX, NZ, NB, NB, 64, 16, 16),
        compiler_params=pltpu.CompilerParams(
            collective_id=0, has_side_effects=True, vmem_limit_bytes=44 * 1024 * 1024
        ),
    )(
        *(
            pltpu.with_memory_space_constraint(one, pltpu.HBM)
            for one in (
                times, embodiment, prefix_blocks, jnp.swapaxes(actions, 1, 2), jnp.swapaxes(noise, 2, 3),
                attn_gain[None, :], out_gain[None, :], input_heads, prefix_keys, prefix_values,
                w_query, w_output, jnp.swapaxes(output_heads, 1, 2),
            )
        )
    )


def solution(mesh):
    torus = Mesh(
        mesh.devices.reshape(NZ, NX, 2, mesh.shape["batch"]), ("seq_0", "seq_1", "seq_2", "batch")
    )
    placed = (
        P("batch", None, None),
        P("batch", None, None, None),
        P("batch", None),
        P("batch"),
        P("batch"),
        P("batch", SEQ, None),
        P("batch", SEQ, None),
        P(),
        P(),
        P(),
        P(),
        P(),
        P(),
    )
    return jax.shard_map(
        local,
        mesh=torus,
        in_specs=placed,
        out_specs=(P(SEQ_BATCH, None), P(SEQ_BATCH, None)),
        check_vma=False,
    )
```

```python
import math

import jax
import jax.numpy as jnp
from jax import lax
from jax.experimental import pallas as pl
from jax.experimental.pallas import tpu as pltpu
from jax.sharding import Mesh
from jax.sharding import PartitionSpec as P

D = 1024
HEADS = 8
HD = 256
ACT = 50
ADIM = 32
TSTEPS = 2
BLOCK = 128
ROWS = TSTEPS * ACT
PAD = 112
HALF = 56
ALL = 2 * PAD
KEYS = 512
NZ = 8
NX = 4
NB = 4
ZT = 7
SEQ = ("seq_0", "seq_1", "seq_2")
SEQ_BATCH = ("seq_0", "seq_1", "seq_2", "batch")
MESH = pl.DeviceIdType.MESH
F32 = jnp.float32
BF16 = jnp.bfloat16
VMEM = pl.BlockSpec(memory_space=pltpu.VMEM)
HBM = pl.BlockSpec(memory_space=pltpu.HBM)


def dot_nt(a, b):
    return lax.dot_general(a, b, (((1,), (1,)), ((), ())), preferred_element_type=F32)


def dot_tn(a, b):
    return lax.dot_general(a, b, (((0,), (0,)), ((), ())), preferred_element_type=F32)


def lanes_of(shape=(8, 128)):
    return lax.broadcasted_iota(jnp.int32, shape, len(shape) - 1)


def thirds(value):
    high = value.astype(BF16)
    rest = value - high.astype(F32)
    middle = rest.astype(BF16)
    return high, middle, (rest - middle.astype(F32)).astype(BF16)


def remote(src, dst, ss, rs, device):
    return pltpu.make_async_remote_copy(
        src_ref=src, dst_ref=dst, send_sem=ss, recv_sem=rs, device_id=device, device_id_type=MESH
    )


def rolled(value, lanes):
    lanes = lanes % 128
    return pltpu.roll(value, lanes, axis=1) if lanes else value


def weigh(peaks, totals):
    top = peaks[0]
    for one in peaks[1:]:
        top = jnp.maximum(top, one)
    scales = [jnp.exp(one - top) for one in peaks]
    total = scales[0] * totals[0]
    for scale, one in zip(scales[1:], totals[1:]):
        total = total + scale * one
    return top, total, scales


def weigh_packed(stats):
    return weigh(stats, [rolled(one, 96) for one in stats])


def blend(parts, scales, column, first, put):
    wide = [jnp.broadcast_to(scale[:, column : column + 1], (8, 128)) for scale in scales]
    for half in range(2):
        value = wide[0] * parts[0][first + half]
        for scale, part in zip(wide[1:], parts[1:]):
            value = value + scale * part[first + half]
        put(half, value)


def step_kernel(
    times_hbm, emb_hbm, blocks_hbm,
    act_hbm, noise_hbm, ag_hbm, og_hbm, ih_hbm, k_hbm, v_hbm, wq_hbm, wo_hbm, oh_hbm,
    q_out, o_out,
    times_ref, emb_ref, blocks_ref, act_ref, noise_ref, ag_ref, og_ref, ih, k_ref, v_ref, wq, wo, oh, mixed_in, goal, hid, nrm, nperm,
    weights_ref, local_peak, sums, cbuf, acc, xbuf, zf, zfbuf, zx, zxbuf, zsend, zbuf,
    psend, prec, attn_all, agz, aga, g, ga,
    db, scale_ref, delta_ref, az, ro_all, ro, gq, cbuf2, zs2, zbuf2, zx2, zxbuf2, xs2, xbuf2, ws2, wbuf2,
    bsend, brec, yrec, drows, drec, q_raw, e_send, e_rec,
    load, c_ss, c_rs, x_ss, x_rs, zf_ss, zf_rs, zx_ss, zx_rs, z_ss, z_rs, p_ss, p_rs,
    gz_ss, gz_rs, gzx_ss, gzx_rs, gzc_ss, gzc_rs,
    ga_ss, ga_rs, gax_ss, gax_rs, gac_ss, gac_rs,
    c2_ss, c2_rs, z2_ss, z2_rs, zx2_ss, zx2_rs, x2_ss, x2_rs, w2_ss, w2_rs,
    y_ss, y_rs, b_ss, b_rs, d_ss, d_rs, e_ss, e_rs,
):
    z = lax.axis_index("seq_0")
    x = lax.axis_index("seq_1")
    c = lax.axis_index("seq_2")
    b = lax.axis_index("batch")
    other = 1 - c
    me = (z * NX + x) * 2 + c
    tile = jnp.minimum(z, ZT - 1)
    active = z < ZT
    lane = lanes_of()
    wide_lane = lanes_of((16, 128))
    zp = [lax.rem(z + d, NZ) for d in range(NZ)]
    zm = [lax.rem(z + NZ - d, NZ) for d in range(NZ)]
    xp = [lax.rem(x + d, NX) for d in range(NX)]
    xm = [lax.rem(x + NX - d, NX) for d in range(NX)]
    bp = [lax.rem(b + d, NB) for d in range(NB)]
    bm = [lax.rem(b + NB - d, NB) for d in range(NB)]
    cp = [c, other]
    zt = [jnp.minimum(one, ZT - 1) for one in zp]
    zmt = [jnp.minimum(one, ZT - 1) for one in zm]
    far = (4, 3, 5, 2, 6, 1, 7)
    close = (1, 7, 2, 6, 3, 5, 4)
    near = (2, 1, 3)
    sibling = {"seq_2": other}

    barrier = pltpu.get_barrier_semaphore()
    pl.semaphore_signal(barrier, inc=1, device_id=sibling, device_id_type=MESH)
    for d in far:
        pl.semaphore_signal(barrier, inc=1, device_id={"seq_0": zp[d]}, device_id_type=MESH)
    for d in near:
        pl.semaphore_signal(barrier, inc=1, device_id={"seq_1": xp[d]}, device_id_type=MESH)
        pl.semaphore_signal(barrier, inc=1, device_id={"batch": bp[d]}, device_id_type=MESH)

    def wq_half(half):
        return wq_hbm.at[:, pl.ds(pl.multiple_of(half * 1024, 1024), 1024)]

    plan = (
        (times_hbm, times_ref), (act_hbm, act_ref), (noise_hbm, noise_ref), (emb_hbm, emb_ref),
        (ih_hbm, ih), (ag_hbm, ag_ref), (wq_half(other), wq.at[0]), (blocks_hbm, blocks_ref),
        (k_hbm, k_ref), (v_hbm, v_ref), (wq_half(c), wq.at[1]), (wo_hbm, wo), (oh_hbm, oh), (og_hbm, og_ref),
    )

    def loads(i):
        return pltpu.make_async_copy(plan[i][0], plan[i][1], load.at[i])

    for i in range(14):
        loads(i).start()
    loads(0).wait()

    channel = lax.broadcasted_iota(jnp.int32, (8, 512), 1).astype(F32)
    frequency = jnp.exp(-math.log(10000.0) * channel / 512)
    row = lax.broadcasted_iota(jnp.int32, (8, 512), 0)
    moment = jnp.zeros((8, 512), F32)
    for st in range(4):
        moment = jnp.where(row == st, times_ref[st // 2, st % 2], moment)
    phase = moment * 1000.0 * frequency
    temb = jnp.concatenate([jnp.sin(phase), jnp.cos(phase)], axis=1)
    mixed_in[...] = jnp.zeros((4, ADIM, 128), F32)
    for i in (1, 2):
        loads(i).wait()
    for s in range(2):
        act = act_ref[s]
        for t in range(2):
            noise = noise_ref[s, t]
            level = times_ref[s, t]
            mixed_in[2 * s + t, :, 0:ACT] = noise - act
            goal[2 * s + t] = mixed_in[2 * s + t].T
            mixed_in[2 * s + t, :, 0:ACT] = level * noise + (1.0 - level) * act
    for i in (3, 4, 5):
        loads(i).wait()
    for s in range(2):
        wh, wm, wl = thirds(ih[emb_ref[s]])
        right = jnp.concatenate([wh, wm, wh, wl, wm, wh], axis=0)
        both = []
        for t in range(2):
            ah, am, al = thirds(mixed_in[2 * s + t])
            left = jnp.concatenate([ah, ah, am, ah, am, al], axis=0)
            hidden = dot_tn(left, right)[0:HALF] + temb[2 * s + t : 2 * s + t + 1, :]
            hid[2 * s + t] = hidden
            both.append(hidden)
        hidden = jnp.concatenate(both, axis=0)
        inverse = lax.rsqrt(jnp.mean(hidden * hidden, axis=1, keepdims=True) + 1e-06)
        nrm[s * PAD : (s + 1) * PAD, :] = (hidden * inverse * ag_ref[...]).astype(BF16)

    def core_copy(chunk):
        return remote(sums.at[0, chunk], cbuf.at[chunk], c_ss.at[chunk], c_rs.at[chunk], sibling)

    for i in range(2):
        loads(6 if i == 0 else 10).wait()
        q = jnp.dot(nrm[...], wq[i], preferred_element_type=F32)
        q = (q * (1.0 / math.sqrt(HD))).astype(BF16)
        if i == 0:
            for n in (7, 8, 9):
                loads(n).wait()
        for s in range(2):
            qs = jnp.concatenate(
                [q[s * PAD : (s + 1) * PAD, h * HD : (h + 1) * HD] for h in range(4)], axis=0
            )
            scores = dot_nt(qs, k_ref[s])
            limit = BLOCK * blocks_ref[s] - me * KEYS
            valid = lax.broadcasted_iota(jnp.int32, scores.shape, 1) < limit
            scores = jnp.where(valid, scores, -1e30)
            peak = jnp.max(scores, axis=1, keepdims=True)
            weights = jnp.where(valid, jnp.exp(scores - peak), 0.0)
            total = jnp.sum(weights, axis=1, keepdims=True)
            mixed = jnp.dot(weights.astype(BF16), v_ref[s], preferred_element_type=F32)
            for h in range(4):
                weights_ref[i, h, s * PAD : (s + 1) * PAD, :] = weights[h * PAD : (h + 1) * PAD]
            for xx in (2 * s, 2 * s + 1):
                peaks = jnp.zeros((8, 128), F32)
                totals = jnp.ones((8, 128), F32)
                for zz in range(ZT):
                    for h in range(4):
                        j = zz * 4 + h
                        at = h * PAD + (7 * xx + zz - 14 * s) * 8
                        peaks = jnp.where(lane == j, peak[at : at + 8], peaks)
                        totals = jnp.where(lane == j, total[at : at + 8], totals)
                        sums[i, xx, 2 * j] = mixed[at : at + 8, :128]
                        sums[i, xx, 2 * j + 1] = mixed[at : at + 8, 128:]
                sums[i, xx, 56] = peaks
                sums[i, xx, 57] = totals
                local_peak[i, xx] = peaks
            if i == 0:
                if s == 0:
                    pl.semaphore_wait(barrier, 1 + NX - 1 + NZ - 1 + NB - 1)
                core_copy(2 * s).start()
                core_copy(2 * s + 1).start()

    cuts = (pl.ds(0, 16), pl.ds(16, 14), pl.ds(30, 14))

    def x_copy(xx, h):
        src, dst = acc.at[xx, cuts[h]], xbuf.at[x, cuts[h]]
        return remote(src, dst, x_ss.at[xx, h], x_rs.at[x, h], {"seq_1": xx})

    def x_arrival(d, h):
        src, dst = acc.at[xm[d], cuts[h]], xbuf.at[xm[d], cuts[h]]
        return remote(src, dst, x_ss.at[xm[d], h], x_rs.at[xm[d], h], {"seq_1": xm[d]})

    def zf_copy(d):
        return remote(zf.at[zt[d]], zfbuf.at[z], zf_ss.at[d], zf_rs.at[d], {"seq_0": zp[d]})

    def zf_arrival(d):
        return remote(zf.at[0], zfbuf.at[zm[d]], zf_ss.at[d], zf_rs.at[d], {"seq_0": zm[d]})

    tops = []
    for h in range(4):
        for xx in range(NX):
            parts = (sums.at[1, xx], cbuf.at[xx])
            if h == 0:
                core_copy(xx).wait_recv()
                tops.append(weigh([p[56] for p in parts], [p[57] for p in parts]))
                acc[xx, 0] = tops[xx][0]
                acc[xx, 1] = tops[xx][1]
            for zz in range(ZT):

                def put_core(half, value):
                    if h < 3:
                        acc[xx, 2 + (h * ZT + zz) * 2 + half] = value
                    else:
                        zf[zz, xx * 2 + half] = value

                blend(parts, tops[xx][2], zz * 4 + h, 2 * (zz * 4 + h), put_core)
            if h < 3:

                @pl.when(x != xx)
                def _():
                    x_copy(xx, h).start()

    for zz in range(ZT):
        stats = jnp.zeros((8, 128), F32)
        for xx in range(NX):
            top, total = tops[xx][:2]
            stats = jnp.where(lane == xx, rolled(top, xx - 4 * zz - 3), stats)
            stats = jnp.where(lane == 32 + xx, rolled(total, 32 + xx - 4 * zz - 3), stats)
        zf[zz, 8] = stats
    for d in far:

        @pl.when(zp[d] < ZT)
        def _():
            zf_copy(d).start()

    for bb in range(NB):
        col = lax.broadcasted_iota(jnp.int32, (D, 256), 1)
        natural = lax.rem(col, 64) * 16 + bb * 4 + col // 64
        pick = (lax.broadcasted_iota(jnp.int32, (D, 256), 0) == natural).astype(F32).astype(BF16)
        placed = jnp.dot(nrm[...], pick, preferred_element_type=F32).astype(BF16)
        cols = slice(bb * 256, (bb + 1) * 256)
        nperm[0:ALL, cols] = placed
    nperm[ALL:, :] = jnp.zeros((256 - ALL, D), BF16)
    for i in (11, 12, 13):
        loads(i).wait()

    def zx_copy(d):
        return remote(zx.at[xp[d]], zxbuf.at[x], zx_ss.at[d], zx_rs.at[d], {"seq_1": xp[d]})

    def zx_arrival(d):
        return remote(zx.at[xm[d]], zxbuf.at[xm[d]], zx_ss.at[d], zx_rs.at[d], {"seq_1": xm[d]})

    def z_slice(h):
        return pl.ds(0, 3) if h == 0 else pl.ds(1 + 2 * h, 2)

    def z_copy(d, h):
        src, dst = zsend.at[zt[d], z_slice(h)], zbuf.at[z, z_slice(h)]
        return remote(src, dst, z_ss.at[d, h], z_rs.at[d, h], {"seq_0": zp[d]})

    def z_arrival(d, h):
        src, dst = zsend.at[0, z_slice(h)], zbuf.at[zm[d], z_slice(h)]
        return remote(src, dst, z_ss.at[d, h], z_rs.at[d, h], {"seq_0": zm[d]})

    columns = [acc.at[x]] + [xbuf.at[xm[d]] for d in range(1, NX)]
    mix = []
    for h in range(3):
        if h == 2:

            @pl.when(active)
            def _():
                for d in range(1, NZ):
                    zf_arrival(d).wait_recv()

                parts = [zf.at[tile]] + [zfbuf.at[zm[d]] for d in range(1, NZ)]
                top, total, scales = weigh_packed([part[8] for part in parts])
                for xx in range(NX):

                    def put_zx(half, value):
                        zx[xx, half] = value

                    blend(parts, scales, xx, 2 * xx, put_zx)
                    zx[xx, 2] = jnp.where(lane < 32, rolled(top, -xx), rolled(total, 32 - xx))
                for d in near:
                    zx_copy(d).start()

        for d in (1, 3, 2):
            x_arrival(d, h).wait_recv()
        if h == 0:
            mix.append(weigh([p[0] for p in columns], [p[1] for p in columns]))
            top, total = mix[0][:2]
            for zz in range(ZT):
                zsend[zz, 0] = jnp.where(lane < 32, rolled(top, -4 * zz), rolled(total, 32 - 4 * zz))
        for zz in range(ZT):

            def put_z(half, value):
                zsend[zz, 1 + 2 * h + half] = value

            blend(columns, mix[0][2], zz * 4 + h, 2 + (h * ZT + zz) * 2, put_z)
        for d in far:

            @pl.when(zp[d] < ZT)
            def _():
                z_copy(d, h).start()

    pair = remote(psend, prec, p_ss, p_rs, sibling)

    def gz_copy(d):
        return remote(agz, g.at[c, x, tile], gz_ss.at[d], gz_rs.at[d], {"seq_0": zp[d]})

    def gz_arrival(d):
        return remote(agz, g.at[c, x, zmt[d]], gz_ss.at[d], gz_rs.at[d], {"seq_0": zm[d]})

    def gzx_copy(d, dx):
        own = g.at[c, x, zmt[d]]
        return remote(own, own, gzx_ss.at[d, dx], gzx_rs.at[d, dx], {"seq_1": xp[dx]})

    def gzx_arrival(d, dx):
        slot = g.at[c, xm[dx], zmt[d]]
        return remote(slot, slot, gzx_ss.at[d, dx], gzx_rs.at[d, dx], {"seq_1": xm[dx]})

    def ga_copy(d):
        return remote(aga.at[zp[d]], ga.at[c, x, tile], ga_ss.at[d], ga_rs.at[d], {"seq_0": zp[d]})

    def ga_arrival(d):
        return remote(aga.at[0], ga.at[c, x, zmt[d]], ga_ss.at[d], ga_rs.at[d], {"seq_0": zm[d]})

    @pl.when(active)
    def _():
        for d in range(1, NX):
            zx_arrival(d).wait_recv()
        values = {}

        parts = [zx.at[x]] + [zxbuf.at[xm[d]] for d in range(1, NX)]
        last_top, last_total, scales = weigh_packed([part[2] for part in parts])

        def keep_last(half, value):
            values[3, half] = value

        blend(parts, scales, 0, 0, keep_last)
        parts = [zsend.at[tile]] + [zbuf.at[zm[d]] for d in range(1, NZ)]
        for h in range(3):
            for d in range(1, NZ):
                z_arrival(d, h).wait_recv()
            if h == 0:
                top, total, scales = weigh_packed([part[0] for part in parts])

            def keep(half, value):
                values[h, half] = value

            blend(parts, scales, h, 1 + 2 * h, keep)
        top = jnp.where(lane == 3, rolled(last_top, 3), top)
        total = jnp.where(lane == 3, rolled(last_total, 3), total)
        first = c == 0
        products = []
        for h in range(4):
            whole = jnp.broadcast_to(total[:, h : h + 1], (8, 128))
            halves = [(values[h, half] / whole).astype(BF16) for half in range(2)]
            attn = jnp.concatenate(halves, axis=1)
            start = pl.multiple_of(c * 1024 + h * HD, HD)
            products.append(jnp.dot(attn, wo[pl.ds(start, HD), :], preferred_element_type=F32))
            low, high = halves[0].astype(F32), halves[1].astype(F32)
            attn_all[4 * c + h] = jnp.where(first, low, high)
            psend[8 + h] = jnp.where(first, high, low)
        partial = products[0] + products[1] + products[2] + products[3]
        for i in range(8):
            psend[i] = partial[:, i * 128 : (i + 1) * 128]
        pair.start()
        start = pl.multiple_of(tile * 8, 8)
        own_hidden = hid[x, pl.ds(start, 8), :]
        target = goal[x, pl.ds(start, 8), :]
        which = emb_ref[x // 2]
        pair.wait_recv()
        resid = own_hidden + (partial + jnp.concatenate([prec[i] for i in range(8)], axis=1))
        inverse = lax.rsqrt(jnp.mean(resid * resid, axis=1, keepdims=True) + 1e-06)
        gain = og_ref[...]
        normed = resid * inverse * gain
        real = start + lax.broadcasted_iota(jnp.int32, (8, 1), 0) < ACT
        heads = oh[which]
        back = jnp.zeros((8, D), F32)
        for j in range(ADIM):
            head = heads[j : j + 1, :]
            velocity = jnp.sum(normed * head, axis=1, keepdims=True)
            dvel = 2.0 * (velocity - target[:, j : j + 1]) / (8 * ROWS)
            back = back + jnp.where(real, dvel, 0.0) * head
        scaled = back * gain
        mean = jnp.mean(resid * scaled, axis=1, keepdims=True)
        dresid = inverse * scaled - inverse * inverse * inverse * resid * mean
        dresid = dresid.astype(BF16).astype(F32)
        own = jnp.where(first, dresid[:, :512], dresid[:, 512:])
        stats = jnp.where(lane < 32, top, rolled(total, 32))
        for h in range(4):
            delta = jnp.sum(products[h] * dresid, axis=1, keepdims=True)
            stats = jnp.where(lane == 64 + h, delta, stats)
        for i in range(4):
            agz[i] = own[:, i * 128 : (i + 1) * 128]
        agz[4] = stats
        for d in close:
            gz_copy(d).start()
        g[c, x, tile] = agz[...]
        for dx in near:
            gzx_copy(0, dx).start()
        for h in range(4):
            attn_all[4 * other + h] = prec[8 + h]
        for zz in range(NZ):
            aga[zz] = attn_all[zz]
        ga[c, x, tile] = aga[z]
        for d in far:
            ga_copy(d).start()

    def gzc_copy(d):
        return remote(g.at[c, xm[d]], g.at[c, xm[d]], gzc_ss.at[d], gzc_rs.at[d], sibling)

    def gzc_arrival(d):
        return remote(g.at[other, xm[d]], g.at[other, xm[d]], gzc_ss.at[d], gzc_rs.at[d], sibling)

    def gax_copy(d):
        return remote(ga.at[c, x], ga.at[c, x], gax_ss.at[d], gax_rs.at[d], {"seq_1": xp[d]})

    def gax_arrival(d):
        return remote(ga.at[c, xm[d]], ga.at[c, xm[d]], gax_ss.at[d], gax_rs.at[d], {"seq_1": xm[d]})

    gac = remote(ga.at[c], ga.at[c], gac_ss, gac_rs, sibling)
    gac_arrival = remote(ga.at[other], ga.at[other], gac_ss, gac_rs, sibling)

    for d in close:

        @pl.when(zm[d] < ZT)
        def _():
            gz_arrival(d).wait_recv()
            for dx in near:
                gzx_copy(d, dx).start()

    gzc_copy(0).start()
    for dx in (1, 3, 2):
        for d in range(NZ):

            @pl.when(zm[d] < ZT)
            def _():
                gzx_arrival(d, dx).wait_recv()

        gzc_copy(dx).start()
    for d in range(1, NZ):

        @pl.when(zm[d] < ZT)
        def _():
            ga_arrival(d).wait_recv()

    for d in near:
        gax_copy(d).start()
    for d in range(NX):
        gzc_arrival(d).wait_recv()

    for t in range(0, 28, 2):
        for core in range(2):
            for i in range(4):
                both = []
                for u in (t, t + 1):
                    xx, zz = u // 7, u % 7
                    both.append(g[core, xx, zz, i])
                lo = core * 512 + i * 128
                db[t * 8 : t * 8 + 16, lo : lo + 128] = jnp.concatenate(both, axis=0).astype(BF16)

    def core2(s):
        return remote(gq.at[0, s], cbuf2.at[s], c2_ss.at[s], c2_rs.at[s], sibling)

    def z2_copy(d):
        return remote(zs2.at[zp[d]], zbuf2.at[z], z2_ss.at[d], z2_rs.at[d], {"seq_0": zp[d]})

    def z2_arrival(d):
        return remote(zs2.at[zm[d]], zbuf2.at[zm[d]], z2_ss.at[d], z2_rs.at[d], {"seq_0": zm[d]})

    def x2_copy(d):
        return remote(xs2.at[xp[d]], xbuf2.at[x], x2_ss.at[d], x2_rs.at[d], {"seq_1": xp[d]})

    def x2_arrival(d):
        return remote(xs2.at[xm[d]], xbuf2.at[xm[d]], x2_ss.at[d], x2_rs.at[d], {"seq_1": xm[d]})

    dattn = []
    for i in range(2):
        half = other if i == 0 else c
        for t in range(28):
            xx, zz = t // 7, t % 7
            stats = g[half, xx, zz, 4]
            scale = jnp.exp(rolled(local_peak[i, xx], -4 * zz) - stats) / rolled(stats, 96)
            for h in range(4):
                n = 4 * i + h
                scale_ref[n, t * 8 : t * 8 + 8] = jnp.broadcast_to(scale[:, h : h + 1], (8, 128))
                delta_ref[n, t * 8 : t * 8 + 8] = jnp.broadcast_to(stats[:, 64 + h : 65 + h], (8, 128))

    def backward(i, s):
        rows = slice(s * PAD, (s + 1) * PAD)
        stacked = jnp.concatenate(
            [dattn[i][rows, h * HD : (h + 1) * HD] for h in range(4)], axis=0
        )
        dvalues = dot_nt(stacked, v_ref[s])
        parts = []
        for h in range(4):
            delta = delta_ref[4 * i + h, rows]
            scale = scale_ref[4 * i + h, rows]
            line = []
            for k in range(4):
                cols = slice(k * 128, (k + 1) * 128)
                dv = dvalues[h * PAD : (h + 1) * PAD, cols]
                line.append((weights_ref[i, h, rows, cols] * scale * (dv - delta)).astype(BF16))
            parts.append(jnp.concatenate(line, axis=1))
        dscore = jnp.concatenate(parts, axis=0)
        grads = jnp.dot(dscore, k_ref[s], preferred_element_type=F32) * (1.0 / math.sqrt(HD))
        grads = grads.astype(BF16).astype(F32)
        for h in range(4):
            for k in range(2):
                gq[i, s, 2 * h + k] = grads[h * PAD : (h + 1) * PAD, k * 128 : (k + 1) * 128]

    for i in range(2):
        start = pl.multiple_of((other if i == 0 else c) * 1024, 1024)
        dattn.append(dot_nt(db[...], wo[pl.ds(start, 1024), :]).astype(BF16))
        backward(i, 1)
        if i == 0:
            core2(1).start()
    core2(1).wait_recv()
    for k in range(NZ):
        zs2[k] = gq[1, 1, k, 16:] + cbuf2[1, k, 16:]
    for d in far:
        z2_copy(d).start()
    zbuf2[z] = zs2[z]
    backward(0, 0)
    core2(0).start()
    backward(1, 0)
    core2(0).wait_recv()
    for k in range(NZ):
        first = gq[1, 0, k] + cbuf2[0, k]
        turned = jnp.concatenate([first, gq[1, 1, k, 0:16] + cbuf2[1, k, 0:16]], axis=0).T
        for xx in range(NX):
            xs2[xx, k] = turned[xx * 32 : (xx + 1) * 32]
    for d in near:
        x2_copy(d).start()
    xbuf2[x] = xs2[x]

    for d in range(1, NX):
        gax_arrival(d).wait_recv()
    gac.start()
    gac_arrival.wait_recv()
    half_core = x // 2
    for t in range(0, 28, 2):
        both = jnp.concatenate([ga[half_core, u // 7, u % 7] for u in (t, t + 1)], axis=0)
        az[t * 8 : t * 8 + 16, :] = both.astype(BF16)
    ro_all[...] = dot_tn(az[...], db[...])
    offset = lax.rem(x, 2) * 64 + c * 32
    for bb in range(NB):
        ro[bb] = ro_all[pl.ds(pl.multiple_of(offset + 8 * bb, 8), 8), :]

    def y_copy(d):
        return remote(ro.at[bp[d]], yrec.at[b], y_ss.at[d], y_rs.at[d], {"batch": bp[d]})

    def y_arrival(d):
        return remote(ro.at[bm[d]], yrec.at[bm[d]], y_ss.at[d], y_rs.at[d], {"batch": bm[d]})

    for d in near:
        y_copy(d).start()
    yrec[b] = ro[b]

    def zx2_copy(d):
        return remote(zx2.at[xp[d]], zxbuf2.at[x], zx2_ss.at[d], zx2_rs.at[d], {"seq_1": xp[d]})

    def zx2_arrival(d):
        return remote(zx2.at[xm[d]], zxbuf2.at[xm[d]], zx2_ss.at[d], zx2_rs.at[d], {"seq_1": xm[d]})

    def w2_copy(d):
        return remote(ws2.at[zp[d]], wbuf2.at[z], w2_ss.at[d], w2_rs.at[d], {"seq_0": zp[d]})

    def w2_arrival(d):
        return remote(ws2.at[zm[d]], wbuf2.at[zm[d]], w2_ss.at[d], w2_rs.at[d], {"seq_0": zm[d]})

    for d in (1, 3, 2):
        x2_arrival(d).wait_recv()
    for k in range(NZ):
        ws2[k] = xbuf2[0, k] + xbuf2[1, k] + xbuf2[2, k] + xbuf2[3, k]
    for d in far:
        w2_copy(d).start()
    wbuf2[z] = ws2[z]
    for d in (1, 7, 2, 6, 3, 5, 4):
        z2_arrival(d).wait_recv()
    late = zbuf2[0]
    for k in range(1, NZ):
        late = late + zbuf2[k]
    turned = jnp.concatenate([late, jnp.zeros((32, 128), F32)], axis=0).T
    for xx in range(NX):
        zx2[xx] = turned[xx * 32 : (xx + 1) * 32]
    for d in near:
        zx2_copy(d).start()
    zxbuf2[x] = zx2[x]
    for d in range(1, NB):
        y_arrival(d).wait_recv()
    raw_o = yrec[0] + yrec[1] + yrec[2] + yrec[3]
    ro_all[0:8] = raw_o
    squares_o = jnp.sum(raw_o * raw_o, keepdims=True)
    for d in (1, 3, 2):
        zx2_arrival(d).wait_recv()
    late = zxbuf2[0] + zxbuf2[1] + zxbuf2[2] + zxbuf2[3]
    for d in (1, 7, 2, 6, 3, 5, 4):
        w2_arrival(d).wait_recv()
    early = wbuf2[0]
    for k in range(1, NZ):
        early = early + wbuf2[k]
    columns = jnp.concatenate([early, late], axis=1)
    product = jnp.dot(jnp.concatenate(thirds(columns), axis=0), nperm[...], preferred_element_type=F32)
    product = product[0:32] + (product[32:64] + product[64:96])
    for bb in range(NB):
        bsend[bb] = product[:, bb * 256 : (bb + 1) * 256]

    def b_copy(d):
        return remote(bsend.at[bp[d]], brec.at[b], b_ss.at[d], b_rs.at[d], {"batch": bp[d]})

    def b_arrival(d):
        return remote(bsend.at[bm[d]], brec.at[bm[d]], b_ss.at[d], b_rs.at[d], {"batch": bm[d]})

    for d in near:
        b_copy(d).start()
    brec[b] = bsend[b]
    for d in range(1, NB):
        b_arrival(d).wait_recv()
    raw_t = brec[0] + brec[1] + brec[2] + brec[3]
    squares = jnp.sum(raw_t * raw_t, keepdims=True) + squares_o
    alls = [(dz, dx, dc) for dz in (4, 3, 5, 2, 6, 1, 7, 0) for dx in (2, 1, 3, 0) for dc in (1, 0) if dz or dx or dc]

    def d_copy(i):
        dz, dx, dc = alls[i]
        peer = zp[dz] * 8 + xp[dx] * 2 + cp[dc]
        device = {"seq_0": zp[dz], "seq_1": xp[dx], "seq_2": cp[dc]}
        return remote(drows.at[peer], drec.at[x, c * 8 + z], d_ss.at[i], d_rs.at[i], device)

    def d_arrival(i):
        dz, dx, dc = alls[i]
        peer = zm[dz] * 8 + xm[dx] * 2 + cp[dc]
        device = {"seq_0": zm[dz], "seq_1": xm[dx], "seq_2": cp[dc]}
        slot = drec.at[xm[dx], cp[dc] * 8 + zm[dz]]
        return remote(drows.at[peer], slot, d_ss.at[i], d_rs.at[i], device)

    stacked = jnp.concatenate([raw_t[:, r * 64 : (r + 1) * 64] for r in range(4)], axis=0)
    stacked = jnp.concatenate([stacked, jnp.zeros((128, 64), F32)], axis=1).T
    drows[:, 0, :] = stacked[0:64]
    drows[:, 1, :] = jnp.broadcast_to(squares, (64, 128))
    for i in range(63):
        d_copy(i).start()
    drec[x, c * 8 + z] = drows[me]
    for i in range(63):
        d_arrival(i).wait_recv()
    e_send[...] = jnp.sum(jnp.sum(drec[:, :, 1, :], axis=0), axis=0, keepdims=True)

    def e_copy(d):
        return remote(e_send, e_rec.at[b], e_ss.at[d], e_rs.at[d], {"batch": bp[d]})

    def e_arrival(d):
        return remote(e_send, e_rec.at[bm[d]], e_ss.at[d], e_rs.at[d], {"batch": bm[d]})

    for d in near:
        e_copy(d).start()
    e_rec[b] = e_send[...]
    blocks = [drec[i, :, 0, :] for i in range(NX)]
    for r in range(4):
        line = rolled(blocks[0], -32 * r)
        for i in range(1, NX):
            line = jnp.where(wide_lane // 32 == i, rolled(blocks[i], 32 * (i - r)), line)
        for t in range(16):
            q_raw[r : r + 1, t * 128 : (t + 1) * 128] = line[t : t + 1]
    for d in range(1, NB):
        e_arrival(d).wait_recv()
    norm = jnp.sqrt(e_rec[0] + e_rec[1] + e_rec[2] + e_rec[3])
    factor = jnp.minimum(1.0, 1.0 / (norm + 1e-06))[0:1, 0:1]
    q_out[...] = q_raw[...] * factor
    o_out[...] = ro_all[0:8] * factor

    for d in range(NX):
        core_copy(d).wait_send()
        gzc_copy(d).wait_send()

        @pl.when(x != d)
        def _():
            for h in range(3):
                x_copy(d, h).wait_send()

        if d:
            gax_copy(d).wait_send()
            x2_copy(d).wait_send()
            zx2_copy(d).wait_send()
            y_copy(d).wait_send()
            b_copy(d).wait_send()
            e_copy(d).wait_send()
    for s in range(2):
        core2(s).wait_send()
    gac.wait_send()
    for d in range(NZ):

        @pl.when(zm[d] < ZT)
        def _():
            for dx in range(1, NX):
                gzx_copy(d, dx).wait_send()

    for d in range(1, NZ):
        z2_copy(d).wait_send()
        w2_copy(d).wait_send()

        @pl.when(zp[d] < ZT)
        def _():
            for h in range(3):
                z_copy(d, h).wait_send()
            zf_copy(d).wait_send()

    @pl.when(active)
    def _():
        pair.wait_send()
        for d in range(1, NX):
            zx_copy(d).wait_send()
        for d in range(1, NZ):
            gz_copy(d).wait_send()
            ga_copy(d).wait_send()

    for i in range(63):
        d_copy(i).wait_send()


def local(
    actions,
    noise,
    times,
    embodiment,
    prefix_blocks,
    prefix_keys,
    prefix_values,
    input_heads,
    attn_gain,
    w_query,
    w_output,
    out_gain,
    output_heads,
):
    dma = pltpu.SemaphoreType.DMA

    def v(*shape, kind=F32):
        return pltpu.VMEM(shape, kind)

    def pairs(*counts):
        return [dma((n,)) if n else dma for n in counts for _ in range(2)]

    return pl.pallas_call(
        step_kernel,
        out_shape=(
            jax.ShapeDtypeStruct((4, HEADS * HD), F32),
            jax.ShapeDtypeStruct((8, D), F32),
        ),
        in_specs=[HBM] * 13,
        out_specs=(VMEM, VMEM),
        scratch_shapes=[
            pltpu.SMEM((2, 2), F32), pltpu.SMEM((2,), jnp.int32), pltpu.SMEM((2,), jnp.int32),
            v(2, ADIM, ACT), v(2, 2, ADIM, ACT), v(1, D), v(1, D),
            v(4, ADIM, D), v(2, KEYS, HD, kind=BF16), v(2, KEYS, HD, kind=BF16), v(2, D, 1024, kind=BF16),
            v(2048, D, kind=BF16), v(4, ADIM, D), v(4, ADIM, 128), v(4, 128, ADIM), v(4, HALF, D),
            v(ALL, D, kind=BF16), v(256, D, kind=BF16),
            v(2, 4, ALL, KEYS), v(2, NX, 8, 128), v(2, NX, 58, 8, 128), v(NX, 58, 8, 128),
            v(NX, 44, 8, 128), v(NX, 44, 8, 128), v(ZT, 9, 8, 128), v(NZ, 9, 8, 128),
            v(NX, 3, 8, 128), v(NX, 3, 8, 128), v(ZT, 7, 8, 128), v(NZ, 7, 8, 128),
            v(12, 8, 128), v(12, 8, 128), v(8, 8, 128), v(5, 8, 128), v(NZ, 8, 128),
            v(2, NX, ZT, 5, 8, 128), v(2, NX, ZT, 8, 128),
            v(ALL, D, kind=BF16), v(8, ALL, 128), v(8, ALL, 128), v(ALL, 128, kind=BF16), v(128, D),
            v(NB, 8, D), v(2, 2, NZ, PAD, 128), v(2, NZ, PAD, 128), v(NZ, 96, 128), v(NZ, 96, 128),
            v(NX, 32, 128), v(NX, 32, 128), v(NX, NZ, 32, 128), v(NX, NZ, 32, 128),
            v(NZ, 32, 128), v(NZ, 32, 128), v(NB, 32, 256), v(NB, 32, 256), v(NB, 8, D),
            v(64, 2, 128), v(NX, 16, 2, 128), v(4, HEADS * HD), v(1, 128), v(NB, 1, 128),
            dma((14,)),
        ]
        + pairs(NX)
        + [dma((NX, 3)), dma((NX, 3))]
        + pairs(NZ, NX)
        + [dma((NZ, 3)), dma((NZ, 3))]
        + pairs(0, NZ)
        + [dma((NZ, NX)), dma((NZ, NX))]
        + pairs(NX, NZ, NX, 0, 2, NZ, NX, NX, NZ, NB, NB, 64, NB),
        compiler_params=pltpu.CompilerParams(
            collective_id=0, has_side_effects=True, vmem_limit_bytes=44 * 1024 * 1024
        ),
    )(
        *(
            pltpu.with_memory_space_constraint(one, pltpu.HBM)
            for one in (
                times, embodiment, prefix_blocks, jnp.swapaxes(actions, 1, 2), jnp.swapaxes(noise, 2, 3),
                attn_gain[None, :], out_gain[None, :], input_heads, prefix_keys, prefix_values,
                w_query, w_output, jnp.swapaxes(output_heads, 1, 2),
            )
        )
    )


def solution(mesh):
    torus = Mesh(
        mesh.devices.reshape(NZ, NX, 2, mesh.shape["batch"]), ("seq_0", "seq_1", "seq_2", "batch")
    )
    placed = (
        P("batch", None, None),
        P("batch", None, None, None),
        P("batch", None),
        P("batch"),
        P("batch"),
        P("batch", SEQ, None),
        P("batch", SEQ, None),
        P(),
        P(),
        P(),
        P(),
        P(),
        P(),
    )
    return jax.shard_map(
        local,
        mesh=torus,
        in_specs=placed,
        out_specs=(P(SEQ_BATCH, None), P(SEQ_BATCH, None)),
        check_vma=False,
    )
```

```python
import math

import jax
import jax.numpy as jnp
from jax import lax
from jax.experimental import pallas as pl
from jax.experimental.pallas import tpu as pltpu
from jax.sharding import Mesh
from jax.sharding import PartitionSpec as P

D = 1024
HEADS = 8
HD = 256
ACT = 50
ADIM = 32
TSTEPS = 2
BLOCK = 128
ROWS = TSTEPS * ACT
PAD = 112
HALF = 56
ALL = 2 * PAD
KEYS = 512
NZ = 8
NX = 4
NB = 4
ZT = 7
SEQ = ("seq_0", "seq_1", "seq_2")
SEQ_BATCH = ("seq_0", "seq_1", "seq_2", "batch")
MESH = pl.DeviceIdType.MESH
F32 = jnp.float32
BF16 = jnp.bfloat16
VMEM = pl.BlockSpec(memory_space=pltpu.VMEM)
HBM = pl.BlockSpec(memory_space=pltpu.HBM)


def dot_nt(a, b):
    return lax.dot_general(a, b, (((1,), (1,)), ((), ())), preferred_element_type=F32)


def dot_tn(a, b):
    return lax.dot_general(a, b, (((0,), (0,)), ((), ())), preferred_element_type=F32)


def lanes_of(shape=(8, 128)):
    return lax.broadcasted_iota(jnp.int32, shape, len(shape) - 1)


def thirds(value):
    high = value.astype(BF16)
    rest = value - high.astype(F32)
    middle = rest.astype(BF16)
    return high, middle, (rest - middle.astype(F32)).astype(BF16)


def remote(src, dst, ss, rs, device):
    return pltpu.make_async_remote_copy(
        src_ref=src, dst_ref=dst, send_sem=ss, recv_sem=rs, device_id=device, device_id_type=MESH
    )


def rolled(value, lanes):
    lanes = lanes % 128
    return pltpu.roll(value, lanes, axis=1) if lanes else value


def weigh(peaks, totals):
    top = peaks[0]
    for one in peaks[1:]:
        top = jnp.maximum(top, one)
    scales = [jnp.exp(one - top) for one in peaks]
    total = scales[0] * totals[0]
    for scale, one in zip(scales[1:], totals[1:]):
        total = total + scale * one
    return top, total, scales


def weigh_packed(stats):
    return weigh(stats, [rolled(one, 96) for one in stats])


def blend(parts, scales, column, first, put):
    wide = [jnp.broadcast_to(scale[:, column : column + 1], (8, 128)) for scale in scales]
    for half in range(2):
        value = wide[0] * parts[0][first + half]
        for scale, part in zip(wide[1:], parts[1:]):
            value = value + scale * part[first + half]
        put(half, value)


def step_kernel(
    times_hbm, emb_hbm, blocks_hbm,
    act_hbm, noise_hbm, ag_hbm, og_hbm, ih_hbm, k_hbm, v_hbm, wq_hbm, wo_hbm, oh_hbm,
    q_out, o_out,
    times_ref, emb_ref, blocks_ref, act_ref, noise_ref, ag_ref, og_ref, ih, k_ref, v_ref, wq, wo, oh, mixed_in, goal, hid, nrm, nperm,
    weights_ref, local_peak, sums, cbuf, acc, xbuf, zf, zfbuf, zx, zxbuf, zsend, zbuf,
    psend, prec, attn_all, agz, aga, g, ga,
    db, scale_ref, delta_ref, az, ro_all, ro, gq, cbuf2, zs2, zbuf2, zx2, zxbuf2, xs2, xbuf2, ws2, wbuf2,
    bsend, brec, yrec, drows, drec, q_raw, e_send, e_rec,
    load, c_ss, c_rs, x_ss, x_rs, zf_ss, zf_rs, zx_ss, zx_rs, z_ss, z_rs, p_ss, p_rs,
    gz_ss, gz_rs, gzx_ss, gzx_rs, gzc_ss, gzc_rs,
    ga_ss, ga_rs, gax_ss, gax_rs, gac_ss, gac_rs,
    c2_ss, c2_rs, z2_ss, z2_rs, zx2_ss, zx2_rs, x2_ss, x2_rs, w2_ss, w2_rs,
    y_ss, y_rs, b_ss, b_rs, d_ss, d_rs, e_ss, e_rs,
):
    z = lax.axis_index("seq_0")
    x = lax.axis_index("seq_1")
    c = lax.axis_index("seq_2")
    b = lax.axis_index("batch")
    other = 1 - c
    me = (z * NX + x) * 2 + c
    tile = jnp.minimum(z, ZT - 1)
    active = z < ZT
    lane = lanes_of()
    wide_lane = lanes_of((16, 128))
    zp = [lax.rem(z + d, NZ) for d in range(NZ)]
    zm = [lax.rem(z + NZ - d, NZ) for d in range(NZ)]
    xp = [lax.rem(x + d, NX) for d in range(NX)]
    xm = [lax.rem(x + NX - d, NX) for d in range(NX)]
    bp = [lax.rem(b + d, NB) for d in range(NB)]
    bm = [lax.rem(b + NB - d, NB) for d in range(NB)]
    cp = [c, other]
    zt = [jnp.minimum(one, ZT - 1) for one in zp]
    zmt = [jnp.minimum(one, ZT - 1) for one in zm]
    far = (4, 3, 5, 2, 6, 1, 7)
    close = (1, 7, 2, 6, 3, 5, 4)
    near = (2, 1, 3)
    sibling = {"seq_2": other}

    barrier = pltpu.get_barrier_semaphore()
    pl.semaphore_signal(barrier, inc=1, device_id=sibling, device_id_type=MESH)
    for d in far:
        pl.semaphore_signal(barrier, inc=1, device_id={"seq_0": zp[d]}, device_id_type=MESH)
    for d in near:
        pl.semaphore_signal(barrier, inc=1, device_id={"seq_1": xp[d]}, device_id_type=MESH)
        pl.semaphore_signal(barrier, inc=1, device_id={"batch": bp[d]}, device_id_type=MESH)

    def wq_half(half):
        return wq_hbm.at[:, pl.ds(pl.multiple_of(half * 1024, 1024), 1024)]

    plan = (
        (times_hbm, times_ref), (act_hbm, act_ref), (noise_hbm, noise_ref), (emb_hbm, emb_ref),
        (ih_hbm, ih), (ag_hbm, ag_ref), (wq_half(other), wq.at[0]), (blocks_hbm, blocks_ref),
        (k_hbm, k_ref), (v_hbm, v_ref), (wq_half(c), wq.at[1]), (wo_hbm, wo), (oh_hbm, oh), (og_hbm, og_ref),
    )

    def loads(i):
        return pltpu.make_async_copy(plan[i][0], plan[i][1], load.at[i])

    for i in range(10):
        loads(i).start()
    loads(0).wait()

    channel = lax.broadcasted_iota(jnp.int32, (8, 512), 1).astype(F32)
    frequency = jnp.exp(-math.log(10000.0) * channel / 512)
    row = lax.broadcasted_iota(jnp.int32, (8, 512), 0)
    moment = jnp.zeros((8, 512), F32)
    for st in range(4):
        moment = jnp.where(row == st, times_ref[st // 2, st % 2], moment)
    phase = moment * 1000.0 * frequency
    temb = jnp.concatenate([jnp.sin(phase), jnp.cos(phase)], axis=1)
    mixed_in[...] = jnp.zeros((4, ADIM, 128), F32)
    for i in (1, 2):
        loads(i).wait()
    for s in range(2):
        act = act_ref[s]
        for t in range(2):
            noise = noise_ref[s, t]
            level = times_ref[s, t]
            mixed_in[2 * s + t, :, 0:ACT] = noise - act
            goal[2 * s + t] = mixed_in[2 * s + t].T
            mixed_in[2 * s + t, :, 0:ACT] = level * noise + (1.0 - level) * act
    for i in (3, 4, 5):
        loads(i).wait()
    for s in range(2):
        wh, wm, wl = thirds(ih[emb_ref[s]])
        right = jnp.concatenate([wh, wm, wh, wl, wm, wh], axis=0)
        both = []
        for t in range(2):
            ah, am, al = thirds(mixed_in[2 * s + t])
            left = jnp.concatenate([ah, ah, am, ah, am, al], axis=0)
            hidden = dot_tn(left, right)[0:HALF] + temb[2 * s + t : 2 * s + t + 1, :]
            hid[2 * s + t] = hidden
            both.append(hidden)
        hidden = jnp.concatenate(both, axis=0)
        inverse = lax.rsqrt(jnp.mean(hidden * hidden, axis=1, keepdims=True) + 1e-06)
        nrm[s * PAD : (s + 1) * PAD, :] = (hidden * inverse * ag_ref[...]).astype(BF16)

    def core_copy(chunk):
        return remote(sums.at[0, chunk], cbuf.at[chunk], c_ss.at[chunk], c_rs.at[chunk], sibling)

    for i in range(2):
        loads(6 if i == 0 else 10).wait()
        if i == 0:
            for n in (10, 11, 12, 13):
                loads(n).start()
        q = jnp.dot(nrm[...], wq[i], preferred_element_type=F32)
        q = (q * (1.0 / math.sqrt(HD))).astype(BF16)
        if i == 0:
            for n in (7, 8, 9):
                loads(n).wait()
        for s in range(2):
            qs = jnp.concatenate(
                [q[s * PAD : (s + 1) * PAD, h * HD : (h + 1) * HD] for h in range(4)], axis=0
            )
            scores = dot_nt(qs, k_ref[s])
            limit = BLOCK * blocks_ref[s] - me * KEYS
            valid = lax.broadcasted_iota(jnp.int32, scores.shape, 1) < limit
            scores = jnp.where(valid, scores, -1e30)
            peak = jnp.max(scores, axis=1, keepdims=True)
            weights = jnp.where(valid, jnp.exp(scores - peak), 0.0)
            total = jnp.sum(weights, axis=1, keepdims=True)
            mixed = jnp.dot(weights.astype(BF16), v_ref[s], preferred_element_type=F32)
            for h in range(4):
                weights_ref[i, h, s * PAD : (s + 1) * PAD, :] = weights[h * PAD : (h + 1) * PAD]
            for xx in (2 * s, 2 * s + 1):
                peaks = jnp.zeros((8, 128), F32)
                totals = jnp.ones((8, 128), F32)
                for zz in range(ZT):
                    for h in range(4):
                        j = zz * 4 + h
                        at = h * PAD + (7 * xx + zz - 14 * s) * 8
                        peaks = jnp.where(lane == j, peak[at : at + 8], peaks)
                        totals = jnp.where(lane == j, total[at : at + 8], totals)
                        sums[i, xx, 2 * j] = mixed[at : at + 8, :128]
                        sums[i, xx, 2 * j + 1] = mixed[at : at + 8, 128:]
                sums[i, xx, 56] = peaks
                sums[i, xx, 57] = totals
                local_peak[i, xx] = peaks
            if i == 0:
                if s == 0:
                    pl.semaphore_wait(barrier, 1 + NX - 1 + NZ - 1 + NB - 1)
                core_copy(2 * s).start()
                core_copy(2 * s + 1).start()

    cuts = (pl.ds(0, 16), pl.ds(16, 14), pl.ds(30, 14))

    def x_copy(xx, h):
        src, dst = acc.at[xx, cuts[h]], xbuf.at[x, cuts[h]]
        return remote(src, dst, x_ss.at[xx, h], x_rs.at[x, h], {"seq_1": xx})

    def x_arrival(d, h):
        src, dst = acc.at[xm[d], cuts[h]], xbuf.at[xm[d], cuts[h]]
        return remote(src, dst, x_ss.at[xm[d], h], x_rs.at[xm[d], h], {"seq_1": xm[d]})

    def zf_copy(d):
        return remote(zf.at[zt[d]], zfbuf.at[z], zf_ss.at[d], zf_rs.at[d], {"seq_0": zp[d]})

    def zf_arrival(d):
        return remote(zf.at[0], zfbuf.at[zm[d]], zf_ss.at[d], zf_rs.at[d], {"seq_0": zm[d]})

    tops = []
    for h in range(4):
        for xx in range(NX):
            parts = (sums.at[1, xx], cbuf.at[xx])
            if h == 0:
                core_copy(xx).wait_recv()
                tops.append(weigh([p[56] for p in parts], [p[57] for p in parts]))
                acc[xx, 0] = tops[xx][0]
                acc[xx, 1] = tops[xx][1]
            for zz in range(ZT):

                def put_core(half, value):
                    if h < 3:
                        acc[xx, 2 + (h * ZT + zz) * 2 + half] = value
                    else:
                        zf[zz, xx * 2 + half] = value

                blend(parts, tops[xx][2], zz * 4 + h, 2 * (zz * 4 + h), put_core)
            if h < 3:

                @pl.when(x != xx)
                def _():
                    x_copy(xx, h).start()

    for zz in range(ZT):
        stats = jnp.zeros((8, 128), F32)
        for xx in range(NX):
            top, total = tops[xx][:2]
            stats = jnp.where(lane == xx, rolled(top, xx - 4 * zz - 3), stats)
            stats = jnp.where(lane == 32 + xx, rolled(total, 32 + xx - 4 * zz - 3), stats)
        zf[zz, 8] = stats
    for d in far:

        @pl.when(zp[d] < ZT)
        def _():
            zf_copy(d).start()

    for bb in range(NB):
        col = lax.broadcasted_iota(jnp.int32, (D, 256), 1)
        natural = lax.rem(col, 64) * 16 + bb * 4 + col // 64
        pick = (lax.broadcasted_iota(jnp.int32, (D, 256), 0) == natural).astype(F32).astype(BF16)
        placed = jnp.dot(nrm[...], pick, preferred_element_type=F32).astype(BF16)
        cols = slice(bb * 256, (bb + 1) * 256)
        nperm[0:ALL, cols] = placed
    nperm[ALL:, :] = jnp.zeros((256 - ALL, D), BF16)
    for i in (11, 12, 13):
        loads(i).wait()

    def zx_copy(d):
        return remote(zx.at[xp[d]], zxbuf.at[x], zx_ss.at[d], zx_rs.at[d], {"seq_1": xp[d]})

    def zx_arrival(d):
        return remote(zx.at[xm[d]], zxbuf.at[xm[d]], zx_ss.at[d], zx_rs.at[d], {"seq_1": xm[d]})

    def z_slice(h):
        return pl.ds(0, 3) if h == 0 else pl.ds(1 + 2 * h, 2)

    def z_copy(d, h):
        src, dst = zsend.at[zt[d], z_slice(h)], zbuf.at[z, z_slice(h)]
        return remote(src, dst, z_ss.at[d, h], z_rs.at[d, h], {"seq_0": zp[d]})

    def z_arrival(d, h):
        src, dst = zsend.at[0, z_slice(h)], zbuf.at[zm[d], z_slice(h)]
        return remote(src, dst, z_ss.at[d, h], z_rs.at[d, h], {"seq_0": zm[d]})

    columns = [acc.at[x]] + [xbuf.at[xm[d]] for d in range(1, NX)]
    mix = []
    for h in range(3):
        if h == 2:

            @pl.when(active)
            def _():
                for d in range(1, NZ):
                    zf_arrival(d).wait_recv()

                parts = [zf.at[tile]] + [zfbuf.at[zm[d]] for d in range(1, NZ)]
                top, total, scales = weigh_packed([part[8] for part in parts])
                for xx in range(NX):

                    def put_zx(half, value):
                        zx[xx, half] = value

                    blend(parts, scales, xx, 2 * xx, put_zx)
                    zx[xx, 2] = jnp.where(lane < 32, rolled(top, -xx), rolled(total, 32 - xx))
                for d in near:
                    zx_copy(d).start()

        for d in (1, 3, 2):
            x_arrival(d, h).wait_recv()
        if h == 0:
            mix.append(weigh([p[0] for p in columns], [p[1] for p in columns]))
            top, total = mix[0][:2]
            for zz in range(ZT):
                zsend[zz, 0] = jnp.where(lane < 32, rolled(top, -4 * zz), rolled(total, 32 - 4 * zz))
        for zz in range(ZT):

            def put_z(half, value):
                zsend[zz, 1 + 2 * h + half] = value

            blend(columns, mix[0][2], zz * 4 + h, 2 + (h * ZT + zz) * 2, put_z)
        for d in far:

            @pl.when(zp[d] < ZT)
            def _():
                z_copy(d, h).start()

    pair = remote(psend, prec, p_ss, p_rs, sibling)

    def gz_copy(d):
        return remote(agz, g.at[c, x, tile], gz_ss.at[d], gz_rs.at[d], {"seq_0": zp[d]})

    def gz_arrival(d):
        return remote(agz, g.at[c, x, zmt[d]], gz_ss.at[d], gz_rs.at[d], {"seq_0": zm[d]})

    def gzx_copy(d, dx):
        own = g.at[c, x, zmt[d]]
        return remote(own, own, gzx_ss.at[d, dx], gzx_rs.at[d, dx], {"seq_1": xp[dx]})

    def gzx_arrival(d, dx):
        slot = g.at[c, xm[dx], zmt[d]]
        return remote(slot, slot, gzx_ss.at[d, dx], gzx_rs.at[d, dx], {"seq_1": xm[dx]})

    def ga_copy(d):
        return remote(aga.at[zp[d]], ga.at[c, x, tile], ga_ss.at[d], ga_rs.at[d], {"seq_0": zp[d]})

    def ga_arrival(d):
        return remote(aga.at[0], ga.at[c, x, zmt[d]], ga_ss.at[d], ga_rs.at[d], {"seq_0": zm[d]})

    @pl.when(active)
    def _():
        for d in range(1, NX):
            zx_arrival(d).wait_recv()
        values = {}

        parts = [zx.at[x]] + [zxbuf.at[xm[d]] for d in range(1, NX)]
        last_top, last_total, scales = weigh_packed([part[2] for part in parts])

        def keep_last(half, value):
            values[3, half] = value

        blend(parts, scales, 0, 0, keep_last)
        parts = [zsend.at[tile]] + [zbuf.at[zm[d]] for d in range(1, NZ)]
        for h in range(3):
            for d in range(1, NZ):
                z_arrival(d, h).wait_recv()
            if h == 0:
                top, total, scales = weigh_packed([part[0] for part in parts])

            def keep(half, value):
                values[h, half] = value

            blend(parts, scales, h, 1 + 2 * h, keep)
        top = jnp.where(lane == 3, rolled(last_top, 3), top)
        total = jnp.where(lane == 3, rolled(last_total, 3), total)
        first = c == 0
        products = []
        for h in range(4):
            whole = jnp.broadcast_to(total[:, h : h + 1], (8, 128))
            halves = [(values[h, half] / whole).astype(BF16) for half in range(2)]
            attn = jnp.concatenate(halves, axis=1)
            start = pl.multiple_of(c * 1024 + h * HD, HD)
            products.append(jnp.dot(attn, wo[pl.ds(start, HD), :], preferred_element_type=F32))
            low, high = halves[0].astype(F32), halves[1].astype(F32)
            attn_all[4 * c + h] = jnp.where(first, low, high)
            psend[8 + h] = jnp.where(first, high, low)
        partial = products[0] + products[1] + products[2] + products[3]
        for i in range(8):
            psend[i] = partial[:, i * 128 : (i + 1) * 128]
        pair.start()
        start = pl.multiple_of(tile * 8, 8)
        own_hidden = hid[x, pl.ds(start, 8), :]
        target = goal[x, pl.ds(start, 8), :]
        which = emb_ref[x // 2]
        pair.wait_recv()
        resid = own_hidden + (partial + jnp.concatenate([prec[i] for i in range(8)], axis=1))
        inverse = lax.rsqrt(jnp.mean(resid * resid, axis=1, keepdims=True) + 1e-06)
        gain = og_ref[...]
        normed = resid * inverse * gain
        real = start + lax.broadcasted_iota(jnp.int32, (8, 1), 0) < ACT
        heads = oh[which]
        back = jnp.zeros((8, D), F32)
        for j in range(ADIM):
            head = heads[j : j + 1, :]
            velocity = jnp.sum(normed * head, axis=1, keepdims=True)
            dvel = 2.0 * (velocity - target[:, j : j + 1]) / (8 * ROWS)
            back = back + jnp.where(real, dvel, 0.0) * head
        scaled = back * gain
        mean = jnp.mean(resid * scaled, axis=1, keepdims=True)
        dresid = inverse * scaled - inverse * inverse * inverse * resid * mean
        dresid = dresid.astype(BF16).astype(F32)
        own = jnp.where(first, dresid[:, :512], dresid[:, 512:])
        stats = jnp.where(lane < 32, top, rolled(total, 32))
        for h in range(4):
            delta = jnp.sum(products[h] * dresid, axis=1, keepdims=True)
            stats = jnp.where(lane == 64 + h, delta, stats)
        for i in range(4):
            agz[i] = own[:, i * 128 : (i + 1) * 128]
        agz[4] = stats
        for d in close:
            gz_copy(d).start()
        g[c, x, tile] = agz[...]
        for dx in near:
            gzx_copy(0, dx).start()
        for h in range(4):
            attn_all[4 * other + h] = prec[8 + h]
        for zz in range(NZ):
            aga[zz] = attn_all[zz]
        ga[c, x, tile] = aga[z]
        for d in far:
            ga_copy(d).start()

    def gzc_copy(d):
        return remote(g.at[c, xm[d]], g.at[c, xm[d]], gzc_ss.at[d], gzc_rs.at[d], sibling)

    def gzc_arrival(d):
        return remote(g.at[other, xm[d]], g.at[other, xm[d]], gzc_ss.at[d], gzc_rs.at[d], sibling)

    def gax_copy(d):
        return remote(ga.at[c, x], ga.at[c, x], gax_ss.at[d], gax_rs.at[d], {"seq_1": xp[d]})

    def gax_arrival(d):
        return remote(ga.at[c, xm[d]], ga.at[c, xm[d]], gax_ss.at[d], gax_rs.at[d], {"seq_1": xm[d]})

    gac = remote(ga.at[c], ga.at[c], gac_ss, gac_rs, sibling)
    gac_arrival = remote(ga.at[other], ga.at[other], gac_ss, gac_rs, sibling)

    for d in close:

        @pl.when(zm[d] < ZT)
        def _():
            gz_arrival(d).wait_recv()
            for dx in near:
                gzx_copy(d, dx).start()

    gzc_copy(0).start()
    for dx in (1, 3, 2):
        for d in range(NZ):

            @pl.when(zm[d] < ZT)
            def _():
                gzx_arrival(d, dx).wait_recv()

        gzc_copy(dx).start()
    for d in range(1, NZ):

        @pl.when(zm[d] < ZT)
        def _():
            ga_arrival(d).wait_recv()

    for d in near:
        gax_copy(d).start()
    for d in range(NX):
        gzc_arrival(d).wait_recv()

    for t in range(0, 28, 2):
        for core in range(2):
            for i in range(4):
                both = []
                for u in (t, t + 1):
                    xx, zz = u // 7, u % 7
                    both.append(g[core, xx, zz, i])
                lo = core * 512 + i * 128
                db[t * 8 : t * 8 + 16, lo : lo + 128] = jnp.concatenate(both, axis=0).astype(BF16)

    def core2(s):
        return remote(gq.at[0, s], cbuf2.at[s], c2_ss.at[s], c2_rs.at[s], sibling)

    def z2_copy(d):
        return remote(zs2.at[zp[d]], zbuf2.at[z], z2_ss.at[d], z2_rs.at[d], {"seq_0": zp[d]})

    def z2_arrival(d):
        return remote(zs2.at[zm[d]], zbuf2.at[zm[d]], z2_ss.at[d], z2_rs.at[d], {"seq_0": zm[d]})

    def x2_copy(d, part):
        src, dst = xs2.at[xp[d], pl.ds(4 * part, 4)], xbuf2.at[x, pl.ds(4 * part, 4)]
        return remote(src, dst, x2_ss.at[d, part], x2_rs.at[d, part], {"seq_1": xp[d]})

    def x2_arrival(d, part):
        src, dst = xs2.at[xm[d], pl.ds(4 * part, 4)], xbuf2.at[xm[d], pl.ds(4 * part, 4)]
        return remote(src, dst, x2_ss.at[d, part], x2_rs.at[d, part], {"seq_1": xm[d]})

    dattn = []

    def row_scales(i, s):
        half = other if i == 0 else c
        for t in range(14 * s, 14 * s + 14):
            xx, zz = t // 7, t % 7
            stats = g[half, xx, zz, 4]
            scale = jnp.exp(rolled(local_peak[i, xx], -4 * zz) - stats) / rolled(stats, 96)
            for h in range(4):
                n = 4 * i + h
                scale_ref[n, t * 8 : t * 8 + 8] = jnp.broadcast_to(scale[:, h : h + 1], (8, 128))
                delta_ref[n, t * 8 : t * 8 + 8] = jnp.broadcast_to(stats[:, 64 + h : 65 + h], (8, 128))

    def backward(i, s):
        row_scales(i, s)
        rows = slice(s * PAD, (s + 1) * PAD)
        stacked = jnp.concatenate(
            [dattn[i][rows, h * HD : (h + 1) * HD] for h in range(4)], axis=0
        )
        dvalues = dot_nt(stacked, v_ref[s])
        parts = []
        for h in range(4):
            delta = delta_ref[4 * i + h, rows]
            scale = scale_ref[4 * i + h, rows]
            line = []
            for k in range(4):
                cols = slice(k * 128, (k + 1) * 128)
                dv = dvalues[h * PAD : (h + 1) * PAD, cols]
                line.append((weights_ref[i, h, rows, cols] * scale * (dv - delta)).astype(BF16))
            parts.append(jnp.concatenate(line, axis=1))
        dscore = jnp.concatenate(parts, axis=0)
        grads = jnp.dot(dscore, k_ref[s], preferred_element_type=F32) * (1.0 / math.sqrt(HD))
        grads = grads.astype(BF16).astype(F32)
        for h in range(4):
            for k in range(2):
                gq[i, s, 2 * h + k] = grads[h * PAD : (h + 1) * PAD, k * 128 : (k + 1) * 128]

    for i in range(2):
        start = pl.multiple_of((other if i == 0 else c) * 1024, 1024)
        dattn.append(dot_nt(db[...], wo[pl.ds(start, 1024), :]).astype(BF16))
        backward(i, 1)
        if i == 0:
            core2(1).start()
    core2(1).wait_recv()
    for k in range(NZ):
        zs2[k] = gq[1, 1, k, 16:] + cbuf2[1, k, 16:]
    for d in far:
        z2_copy(d).start()
    zbuf2[z] = zs2[z]
    backward(0, 0)
    core2(0).start()
    backward(1, 0)
    core2(0).wait_recv()
    for k in range(NZ):
        first = gq[1, 0, k] + cbuf2[0, k]
        turned = jnp.concatenate([first, gq[1, 1, k, 0:16] + cbuf2[1, k, 0:16]], axis=0).T
        for xx in range(NX):
            xs2[xx, k] = turned[xx * 32 : (xx + 1) * 32]
        if k % 4 == 3:
            for d in near:
                x2_copy(d, k // 4).start()
    xbuf2[x] = xs2[x]

    for d in range(1, NX):
        gax_arrival(d).wait_recv()
    gac.start()
    gac_arrival.wait_recv()
    half_core = x // 2
    for t in range(0, 28, 2):
        both = jnp.concatenate([ga[half_core, u // 7, u % 7] for u in (t, t + 1)], axis=0)
        az[t * 8 : t * 8 + 16, :] = both.astype(BF16)
    ro_all[...] = dot_tn(az[...], db[...])
    offset = lax.rem(x, 2) * 64 + c * 32
    for bb in range(NB):
        ro[bb] = ro_all[pl.ds(pl.multiple_of(offset + 8 * bb, 8), 8), :]

    def y_copy(d):
        return remote(ro.at[bp[d]], yrec.at[b], y_ss.at[d], y_rs.at[d], {"batch": bp[d]})

    def y_arrival(d):
        return remote(ro.at[bm[d]], yrec.at[bm[d]], y_ss.at[d], y_rs.at[d], {"batch": bm[d]})

    for d in near:
        y_copy(d).start()
    yrec[b] = ro[b]

    def zx2_copy(d):
        return remote(zx2.at[xp[d]], zxbuf2.at[x], zx2_ss.at[d], zx2_rs.at[d], {"seq_1": xp[d]})

    def zx2_arrival(d):
        return remote(zx2.at[xm[d]], zxbuf2.at[xm[d]], zx2_ss.at[d], zx2_rs.at[d], {"seq_1": xm[d]})

    def w2_copy(k):
        return remote(ws2.at[k], wbuf2.at[z], w2_ss.at[k], w2_rs.at[z], {"seq_0": k})

    def w2_arrival(d):
        return remote(ws2.at[zm[d]], wbuf2.at[zm[d]], w2_ss.at[zm[d]], w2_rs.at[zm[d]], {"seq_0": zm[d]})

    for part in range(2):
        for d in (1, 3, 2):
            x2_arrival(d, part).wait_recv()
        for k in range(4 * part, 4 * part + 4):
            ws2[k] = xbuf2[0, k] + xbuf2[1, k] + xbuf2[2, k] + xbuf2[3, k]

            @pl.when(z != k)
            def _():
                w2_copy(k).start()

    wbuf2[z] = ws2[z]
    for d in (1, 7, 2, 6, 3, 5, 4):
        z2_arrival(d).wait_recv()
    late = zbuf2[0]
    for k in range(1, NZ):
        late = late + zbuf2[k]
    turned = jnp.concatenate([late, jnp.zeros((32, 128), F32)], axis=0).T
    for xx in range(NX):
        zx2[xx] = turned[xx * 32 : (xx + 1) * 32]
    for d in near:
        zx2_copy(d).start()
    zxbuf2[x] = zx2[x]
    for d in range(1, NB):
        y_arrival(d).wait_recv()
    raw_o = yrec[0] + yrec[1] + yrec[2] + yrec[3]
    ro_all[0:8] = raw_o
    squares_o = jnp.sum(raw_o * raw_o, keepdims=True)
    for d in (1, 3, 2):
        zx2_arrival(d).wait_recv()
    late = zxbuf2[0] + zxbuf2[1] + zxbuf2[2] + zxbuf2[3]
    for d in (1, 7, 2, 6, 3, 5, 4):
        w2_arrival(d).wait_recv()
    early = wbuf2[0]
    for k in range(1, NZ):
        early = early + wbuf2[k]
    columns = jnp.concatenate([early, late], axis=1)
    product = jnp.dot(jnp.concatenate(thirds(columns), axis=0), nperm[...], preferred_element_type=F32)
    product = product[0:32] + (product[32:64] + product[64:96])
    for bb in range(NB):
        bsend[bb] = product[:, bb * 256 : (bb + 1) * 256]

    def b_copy(d):
        return remote(bsend.at[bp[d]], brec.at[b], b_ss.at[d], b_rs.at[d], {"batch": bp[d]})

    def b_arrival(d):
        return remote(bsend.at[bm[d]], brec.at[bm[d]], b_ss.at[d], b_rs.at[d], {"batch": bm[d]})

    for d in near:
        b_copy(d).start()
    brec[b] = bsend[b]
    for d in range(1, NB):
        b_arrival(d).wait_recv()
    raw_t = brec[0] + brec[1] + brec[2] + brec[3]
    squares = jnp.sum(raw_t * raw_t, keepdims=True) + squares_o
    alls = [(dz, dx, dc) for dz in (4, 3, 5, 2, 6, 1, 7, 0) for dx in (2, 1, 3, 0) for dc in (1, 0) if dz or dx or dc]

    def d_copy(i):
        dz, dx, dc = alls[i]
        peer = zp[dz] * 8 + xp[dx] * 2 + cp[dc]
        device = {"seq_0": zp[dz], "seq_1": xp[dx], "seq_2": cp[dc]}
        return remote(drows.at[peer], drec.at[x, c * 8 + z], d_ss.at[i], d_rs.at[i], device)

    def d_arrival(i):
        dz, dx, dc = alls[i]
        peer = zm[dz] * 8 + xm[dx] * 2 + cp[dc]
        device = {"seq_0": zm[dz], "seq_1": xm[dx], "seq_2": cp[dc]}
        slot = drec.at[xm[dx], cp[dc] * 8 + zm[dz]]
        return remote(drows.at[peer], slot, d_ss.at[i], d_rs.at[i], device)

    stacked = jnp.concatenate([raw_t[:, r * 64 : (r + 1) * 64] for r in range(4)], axis=0)
    stacked = jnp.concatenate([stacked, jnp.zeros((128, 64), F32)], axis=1).T
    drows[:, 0, :] = stacked[0:64]
    drows[:, 1, :] = jnp.broadcast_to(squares, (64, 128))
    for i in range(63):
        d_copy(i).start()
    drec[x, c * 8 + z] = drows[me]
    for i in range(63):
        d_arrival(i).wait_recv()
    e_send[...] = jnp.sum(jnp.sum(drec[:, :, 1, :], axis=0), axis=0, keepdims=True)

    def e_copy(d):
        return remote(e_send, e_rec.at[b], e_ss.at[d], e_rs.at[d], {"batch": bp[d]})

    def e_arrival(d):
        return remote(e_send, e_rec.at[bm[d]], e_ss.at[d], e_rs.at[d], {"batch": bm[d]})

    for d in near:
        e_copy(d).start()
    e_rec[b] = e_send[...]
    blocks = [drec[i, :, 0, :] for i in range(NX)]
    for r in range(4):
        line = rolled(blocks[0], -32 * r)
        for i in range(1, NX):
            line = jnp.where(wide_lane // 32 == i, rolled(blocks[i], 32 * (i - r)), line)
        for t in range(16):
            q_raw[r : r + 1, t * 128 : (t + 1) * 128] = line[t : t + 1]
    for d in range(1, NB):
        e_arrival(d).wait_recv()
    norm = jnp.sqrt(e_rec[0] + e_rec[1] + e_rec[2] + e_rec[3])
    factor = jnp.minimum(1.0, 1.0 / (norm + 1e-06))[0:1, 0:1]
    q_out[...] = q_raw[...] * factor
    o_out[...] = ro_all[0:8] * factor

    for d in range(NX):
        core_copy(d).wait_send()
        gzc_copy(d).wait_send()

        @pl.when(x != d)
        def _():
            for h in range(3):
                x_copy(d, h).wait_send()

        if d:
            gax_copy(d).wait_send()
            x2_copy(d, 0).wait_send()
            x2_copy(d, 1).wait_send()
            zx2_copy(d).wait_send()
            y_copy(d).wait_send()
            b_copy(d).wait_send()
            e_copy(d).wait_send()
    for s in range(2):
        core2(s).wait_send()
    gac.wait_send()
    for d in range(NZ):

        @pl.when(z != d)
        def _():
            w2_copy(d).wait_send()

        @pl.when(zm[d] < ZT)
        def _():
            for dx in range(1, NX):
                gzx_copy(d, dx).wait_send()

    for d in range(1, NZ):
        z2_copy(d).wait_send()

        @pl.when(zp[d] < ZT)
        def _():
            for h in range(3):
                z_copy(d, h).wait_send()
            zf_copy(d).wait_send()

    @pl.when(active)
    def _():
        pair.wait_send()
        for d in range(1, NX):
            zx_copy(d).wait_send()
        for d in range(1, NZ):
            gz_copy(d).wait_send()
            ga_copy(d).wait_send()

    for i in range(63):
        d_copy(i).wait_send()


def local(
    actions,
    noise,
    times,
    embodiment,
    prefix_blocks,
    prefix_keys,
    prefix_values,
    input_heads,
    attn_gain,
    w_query,
    w_output,
    out_gain,
    output_heads,
):
    dma = pltpu.SemaphoreType.DMA

    def v(*shape, kind=F32):
        return pltpu.VMEM(shape, kind)

    def pairs(*counts):
        return [dma((n,)) if n else dma for n in counts for _ in range(2)]

    return pl.pallas_call(
        step_kernel,
        out_shape=(
            jax.ShapeDtypeStruct((4, HEADS * HD), F32),
            jax.ShapeDtypeStruct((8, D), F32),
        ),
        in_specs=[HBM] * 13,
        out_specs=(VMEM, VMEM),
        scratch_shapes=[
            pltpu.SMEM((2, 2), F32), pltpu.SMEM((2,), jnp.int32), pltpu.SMEM((2,), jnp.int32),
            v(2, ADIM, ACT), v(2, 2, ADIM, ACT), v(1, D), v(1, D),
            v(4, ADIM, D), v(2, KEYS, HD, kind=BF16), v(2, KEYS, HD, kind=BF16), v(2, D, 1024, kind=BF16),
            v(2048, D, kind=BF16), v(4, ADIM, D), v(4, ADIM, 128), v(4, 128, ADIM), v(4, HALF, D),
            v(ALL, D, kind=BF16), v(256, D, kind=BF16),
            v(2, 4, ALL, KEYS), v(2, NX, 8, 128), v(2, NX, 58, 8, 128), v(NX, 58, 8, 128),
            v(NX, 44, 8, 128), v(NX, 44, 8, 128), v(ZT, 9, 8, 128), v(NZ, 9, 8, 128),
            v(NX, 3, 8, 128), v(NX, 3, 8, 128), v(ZT, 7, 8, 128), v(NZ, 7, 8, 128),
            v(12, 8, 128), v(12, 8, 128), v(8, 8, 128), v(5, 8, 128), v(NZ, 8, 128),
            v(2, NX, ZT, 5, 8, 128), v(2, NX, ZT, 8, 128),
            v(ALL, D, kind=BF16), v(8, ALL, 128), v(8, ALL, 128), v(ALL, 128, kind=BF16), v(128, D),
            v(NB, 8, D), v(2, 2, NZ, PAD, 128), v(2, NZ, PAD, 128), v(NZ, 96, 128), v(NZ, 96, 128),
            v(NX, 32, 128), v(NX, 32, 128), v(NX, NZ, 32, 128), v(NX, NZ, 32, 128),
            v(NZ, 32, 128), v(NZ, 32, 128), v(NB, 32, 256), v(NB, 32, 256), v(NB, 8, D),
            v(64, 2, 128), v(NX, 16, 2, 128), v(4, HEADS * HD), v(1, 128), v(NB, 1, 128),
            dma((14,)),
        ]
        + pairs(NX)
        + [dma((NX, 3)), dma((NX, 3))]
        + pairs(NZ, NX)
        + [dma((NZ, 3)), dma((NZ, 3))]
        + pairs(0, NZ)
        + [dma((NZ, NX)), dma((NZ, NX))]
        + pairs(NX, NZ, NX, 0, 2, NZ, NX)
        + [dma((NX, 2)), dma((NX, 2))]
        + pairs(NZ, NB, NB, 64, NB),
        compiler_params=pltpu.CompilerParams(
            collective_id=0, has_side_effects=True, vmem_limit_bytes=44 * 1024 * 1024
        ),
    )(
        *(
            pltpu.with_memory_space_constraint(one, pltpu.HBM)
            for one in (
                times, embodiment, prefix_blocks, jnp.swapaxes(actions, 1, 2), jnp.swapaxes(noise, 2, 3),
                attn_gain[None, :], out_gain[None, :], input_heads, prefix_keys, prefix_values,
                w_query, w_output, jnp.swapaxes(output_heads, 1, 2),
            )
        )
    )


def solution(mesh):
    torus = Mesh(
        mesh.devices.reshape(NZ, NX, 2, mesh.shape["batch"]), ("seq_0", "seq_1", "seq_2", "batch")
    )
    placed = (
        P("batch", None, None),
        P("batch", None, None, None),
        P("batch", None),
        P("batch"),
        P("batch"),
        P("batch", SEQ, None),
        P("batch", SEQ, None),
        P(),
        P(),
        P(),
        P(),
        P(),
        P(),
    )
    return jax.shard_map(
        local,
        mesh=torus,
        in_specs=placed,
        out_specs=(P(SEQ_BATCH, None), P(SEQ_BATCH, None)),
        check_vma=False,
    )
```

```python
import math

import jax
import jax.numpy as jnp
from jax import lax
from jax.experimental import pallas as pl
from jax.experimental.pallas import tpu as pltpu
from jax.sharding import Mesh
from jax.sharding import PartitionSpec as P

D = 1024
HEADS = 8
HD = 256
ACT = 50
ADIM = 32
TSTEPS = 2
BLOCK = 128
ROWS = TSTEPS * ACT
PAD = 112
HALF = 56
ALL = 2 * PAD
KEYS = 512
NZ = 8
NX = 4
NB = 4
ZT = 7
SEQ = ("seq_0", "seq_1", "seq_2")
SEQ_BATCH = ("seq_0", "seq_1", "seq_2", "batch")
MESH = pl.DeviceIdType.MESH
F32 = jnp.float32
BF16 = jnp.bfloat16
VMEM = pl.BlockSpec(memory_space=pltpu.VMEM)
HBM = pl.BlockSpec(memory_space=pltpu.HBM)


def dot_nt(a, b):
    return lax.dot_general(a, b, (((1,), (1,)), ((), ())), preferred_element_type=F32)


def dot_tn(a, b):
    return lax.dot_general(a, b, (((0,), (0,)), ((), ())), preferred_element_type=F32)


def lanes_of(shape=(8, 128)):
    return lax.broadcasted_iota(jnp.int32, shape, len(shape) - 1)


def thirds(value):
    high = value.astype(BF16)
    rest = value - high.astype(F32)
    middle = rest.astype(BF16)
    return high, middle, (rest - middle.astype(F32)).astype(BF16)


def remote(src, dst, ss, rs, device):
    return pltpu.make_async_remote_copy(
        src_ref=src, dst_ref=dst, send_sem=ss, recv_sem=rs, device_id=device, device_id_type=MESH
    )


def rolled(value, lanes):
    lanes = lanes % 128
    return pltpu.roll(value, lanes, axis=1) if lanes else value


def weigh(peaks, totals):
    top = peaks[0]
    for one in peaks[1:]:
        top = jnp.maximum(top, one)
    scales = [jnp.exp(one - top) for one in peaks]
    total = scales[0] * totals[0]
    for scale, one in zip(scales[1:], totals[1:]):
        total = total + scale * one
    return top, total, scales


def weigh_packed(stats):
    return weigh(stats, [rolled(one, 96) for one in stats])


def blend(parts, scales, column, first, put):
    wide = [jnp.broadcast_to(scale[:, column : column + 1], (8, 128)) for scale in scales]
    for half in range(2):
        value = wide[0] * parts[0][first + half]
        for scale, part in zip(wide[1:], parts[1:]):
            value = value + scale * part[first + half]
        put(half, value)


def step_kernel(
    times_hbm, emb_hbm, blocks_hbm,
    act_hbm, noise_hbm, ag_hbm, og_hbm, ih_hbm, k_hbm, v_hbm, wq_hbm, wo_hbm, oh_hbm,
    q_out, o_out,
    times_ref, emb_ref, blocks_ref, act_ref, noise_ref, ag_ref, og_ref, ih, k_ref, v_ref, wq, wo, oh, mixed_in, goal, hid, nrm, nperm,
    weights_ref, local_peak, sums, cbuf, acc, xbuf, zf, zfbuf, zx, zxbuf, zsend, zbuf,
    psend, prec, attn_all, agz, aga, g, ga,
    db, scale_ref, delta_ref, az, ro_all, ro, gq, cbuf2, zs2, zbuf2, zx2, zxbuf2, xs2, xbuf2, ws2, wbuf2,
    bsend, brec, yrec, drows, drec, q_raw, e_send, e_rec,
    load, c_ss, c_rs, x_ss, x_rs, zf_ss, zf_rs, zx_ss, zx_rs, z_ss, z_rs, p_ss, p_rs,
    gz_ss, gz_rs, gzx_ss, gzx_rs, gzc_ss, gzc_rs,
    ga_ss, ga_rs, gax_ss, gax_rs, gac_ss, gac_rs,
    c2_ss, c2_rs, z2_ss, z2_rs, zx2_ss, zx2_rs, x2_ss, x2_rs, w2_ss, w2_rs,
    y_ss, y_rs, b_ss, b_rs, d_ss, d_rs, e_ss, e_rs,
):
    z = lax.axis_index("seq_0")
    x = lax.axis_index("seq_1")
    c = lax.axis_index("seq_2")
    b = lax.axis_index("batch")
    other = 1 - c
    me = (z * NX + x) * 2 + c
    tile = jnp.minimum(z, ZT - 1)
    active = z < ZT
    lane = lanes_of()
    wide_lane = lanes_of((16, 128))
    zp = [lax.rem(z + d, NZ) for d in range(NZ)]
    zm = [lax.rem(z + NZ - d, NZ) for d in range(NZ)]
    xp = [lax.rem(x + d, NX) for d in range(NX)]
    xm = [lax.rem(x + NX - d, NX) for d in range(NX)]
    bp = [lax.rem(b + d, NB) for d in range(NB)]
    bm = [lax.rem(b + NB - d, NB) for d in range(NB)]
    cp = [c, other]
    zt = [jnp.minimum(one, ZT - 1) for one in zp]
    zmt = [jnp.minimum(one, ZT - 1) for one in zm]
    far = (4, 3, 5, 2, 6, 1, 7)
    close = (1, 7, 2, 6, 3, 5, 4)
    near = (2, 1, 3)
    sibling = {"seq_2": other}

    barrier = pltpu.get_barrier_semaphore()
    pl.semaphore_signal(barrier, inc=1, device_id=sibling, device_id_type=MESH)
    for d in far:
        pl.semaphore_signal(barrier, inc=1, device_id={"seq_0": zp[d]}, device_id_type=MESH)
    for d in near:
        pl.semaphore_signal(barrier, inc=1, device_id={"seq_1": xp[d]}, device_id_type=MESH)
        pl.semaphore_signal(barrier, inc=1, device_id={"batch": bp[d]}, device_id_type=MESH)

    def wq_half(half):
        return wq_hbm.at[:, pl.ds(pl.multiple_of(half * 1024, 1024), 1024)]

    plan = (
        (times_hbm, times_ref), (act_hbm, act_ref), (noise_hbm, noise_ref), (emb_hbm, emb_ref),
        (ih_hbm, ih), (ag_hbm, ag_ref), (wq_half(other), wq.at[0]), (blocks_hbm, blocks_ref),
        (k_hbm, k_ref), (v_hbm, v_ref), (wq_half(c), wq.at[1]), (wo_hbm, wo), (oh_hbm, oh), (og_hbm, og_ref),
    )

    def loads(i):
        return pltpu.make_async_copy(plan[i][0], plan[i][1], load.at[i])

    for i in (0, 4, 6, 1, 2, 3, 5, 7, 8, 9):
        loads(i).start()
    loads(0).wait()

    channel = lax.broadcasted_iota(jnp.int32, (8, 512), 1).astype(F32)
    frequency = jnp.exp(-math.log(10000.0) * channel / 512)
    row = lax.broadcasted_iota(jnp.int32, (8, 512), 0)
    moment = jnp.zeros((8, 512), F32)
    for st in range(4):
        moment = jnp.where(row == st, times_ref[st // 2, st % 2], moment)
    phase = moment * 1000.0 * frequency
    temb = jnp.concatenate([jnp.sin(phase), jnp.cos(phase)], axis=1)
    mixed_in[...] = jnp.zeros((4, ADIM, 128), F32)
    for i in (1, 2):
        loads(i).wait()
    for s in range(2):
        act = act_ref[s]
        for t in range(2):
            noise = noise_ref[s, t]
            level = times_ref[s, t]
            mixed_in[2 * s + t, :, 0:ACT] = noise - act
            goal[2 * s + t] = mixed_in[2 * s + t].T
            mixed_in[2 * s + t, :, 0:ACT] = level * noise + (1.0 - level) * act
    for i in (3, 4, 5):
        loads(i).wait()
    for s in range(2):
        wh, wm, wl = thirds(ih[emb_ref[s]])
        right = jnp.concatenate([wh, wm, wh, wl, wm, wh], axis=0)
        both = []
        for t in range(2):
            ah, am, al = thirds(mixed_in[2 * s + t])
            left = jnp.concatenate([ah, ah, am, ah, am, al], axis=0)
            hidden = dot_tn(left, right)[0:HALF] + temb[2 * s + t : 2 * s + t + 1, :]
            hid[2 * s + t] = hidden
            both.append(hidden)
        hidden = jnp.concatenate(both, axis=0)
        inverse = lax.rsqrt(jnp.mean(hidden * hidden, axis=1, keepdims=True) + 1e-06)
        nrm[s * PAD : (s + 1) * PAD, :] = (hidden * inverse * ag_ref[...]).astype(BF16)

    def core_copy(chunk):
        return remote(sums.at[0, chunk], cbuf.at[chunk], c_ss.at[chunk], c_rs.at[chunk], sibling)

    for i in range(2):
        loads(6 if i == 0 else 10).wait()
        if i == 0:
            for n in (10, 11, 12, 13):
                loads(n).start()
        q = jnp.dot(nrm[...], wq[i], preferred_element_type=F32)
        q = (q * (1.0 / math.sqrt(HD))).astype(BF16)
        if i == 0:
            for n in (7, 8, 9):
                loads(n).wait()
        for s in range(2):
            qs = jnp.concatenate(
                [q[s * PAD : (s + 1) * PAD, h * HD : (h + 1) * HD] for h in range(4)], axis=0
            )
            scores = dot_nt(qs, k_ref[s])
            limit = BLOCK * blocks_ref[s] - me * KEYS
            valid = lax.broadcasted_iota(jnp.int32, scores.shape, 1) < limit
            scores = jnp.where(valid, scores, -1e30)
            peak = jnp.max(scores, axis=1, keepdims=True)
            weights = jnp.where(valid, jnp.exp(scores - peak), 0.0)
            total = jnp.sum(weights, axis=1, keepdims=True)
            mixed = jnp.dot(weights.astype(BF16), v_ref[s], preferred_element_type=F32)
            for h in range(4):
                weights_ref[i, h, s * PAD : (s + 1) * PAD, :] = weights[h * PAD : (h + 1) * PAD]
            for xx in (2 * s, 2 * s + 1):
                peaks = jnp.zeros((8, 128), F32)
                totals = jnp.ones((8, 128), F32)
                for zz in range(ZT):
                    for h in range(4):
                        j = zz * 4 + h
                        at = h * PAD + (7 * xx + zz - 14 * s) * 8
                        peaks = jnp.where(lane == j, peak[at : at + 8], peaks)
                        totals = jnp.where(lane == j, total[at : at + 8], totals)
                        sums[i, xx, 2 * j] = mixed[at : at + 8, :128]
                        sums[i, xx, 2 * j + 1] = mixed[at : at + 8, 128:]
                sums[i, xx, 56] = peaks
                sums[i, xx, 57] = totals
                local_peak[i, xx] = peaks
            if i == 0:
                if s == 0:
                    pl.semaphore_wait(barrier, 1 + NX - 1 + NZ - 1 + NB - 1)
                core_copy(2 * s).start()
                core_copy(2 * s + 1).start()

    cuts = (pl.ds(0, 16), pl.ds(16, 14), pl.ds(30, 14))

    def x_copy(xx, h):
        src, dst = acc.at[xx, cuts[h]], xbuf.at[x, cuts[h]]
        return remote(src, dst, x_ss.at[xx, h], x_rs.at[x, h], {"seq_1": xx})

    def x_arrival(d, h):
        src, dst = acc.at[xm[d], cuts[h]], xbuf.at[xm[d], cuts[h]]
        return remote(src, dst, x_ss.at[xm[d], h], x_rs.at[xm[d], h], {"seq_1": xm[d]})

    def zf_copy(d):
        return remote(zf.at[zt[d]], zfbuf.at[z], zf_ss.at[d], zf_rs.at[d], {"seq_0": zp[d]})

    def zf_arrival(d):
        return remote(zf.at[0], zfbuf.at[zm[d]], zf_ss.at[d], zf_rs.at[d], {"seq_0": zm[d]})

    tops = []
    for h in range(4):
        for xx in range(NX):
            parts = (sums.at[1, xx], cbuf.at[xx])
            if h == 0:
                core_copy(xx).wait_recv()
                tops.append(weigh([p[56] for p in parts], [p[57] for p in parts]))
                acc[xx, 0] = tops[xx][0]
                acc[xx, 1] = tops[xx][1]
            for zz in range(ZT):

                def put_core(half, value):
                    if h < 3:
                        acc[xx, 2 + (h * ZT + zz) * 2 + half] = value
                    else:
                        zf[zz, xx * 2 + half] = value

                blend(parts, tops[xx][2], zz * 4 + h, 2 * (zz * 4 + h), put_core)
            if h < 3:

                @pl.when(x != xx)
                def _():
                    x_copy(xx, h).start()

    for zz in range(ZT):
        stats = jnp.zeros((8, 128), F32)
        for xx in range(NX):
            top, total = tops[xx][:2]
            stats = jnp.where(lane == xx, rolled(top, xx - 4 * zz - 3), stats)
            stats = jnp.where(lane == 32 + xx, rolled(total, 32 + xx - 4 * zz - 3), stats)
        zf[zz, 8] = stats
    for d in far:

        @pl.when(zp[d] < ZT)
        def _():
            zf_copy(d).start()

    for bb in range(NB):
        col = lax.broadcasted_iota(jnp.int32, (D, 256), 1)
        natural = lax.rem(col, 64) * 16 + bb * 4 + col // 64
        pick = (lax.broadcasted_iota(jnp.int32, (D, 256), 0) == natural).astype(F32).astype(BF16)
        placed = jnp.dot(nrm[...], pick, preferred_element_type=F32).astype(BF16)
        cols = slice(bb * 256, (bb + 1) * 256)
        nperm[0:ALL, cols] = placed
    nperm[ALL:, :] = jnp.zeros((256 - ALL, D), BF16)
    for i in (11, 12, 13):
        loads(i).wait()

    def zx_copy(d):
        return remote(zx.at[xp[d]], zxbuf.at[x], zx_ss.at[d], zx_rs.at[d], {"seq_1": xp[d]})

    def zx_arrival(d):
        return remote(zx.at[xm[d]], zxbuf.at[xm[d]], zx_ss.at[d], zx_rs.at[d], {"seq_1": xm[d]})

    def z_slice(h):
        return pl.ds(0, 3) if h == 0 else pl.ds(1 + 2 * h, 2)

    def z_copy(d, h):
        src, dst = zsend.at[zt[d], z_slice(h)], zbuf.at[z, z_slice(h)]
        return remote(src, dst, z_ss.at[d, h], z_rs.at[d, h], {"seq_0": zp[d]})

    def z_arrival(d, h):
        src, dst = zsend.at[0, z_slice(h)], zbuf.at[zm[d], z_slice(h)]
        return remote(src, dst, z_ss.at[d, h], z_rs.at[d, h], {"seq_0": zm[d]})

    columns = [acc.at[x]] + [xbuf.at[xm[d]] for d in range(1, NX)]
    mix = []
    for h in range(3):
        if h == 2:

            @pl.when(active)
            def _():
                for d in range(1, NZ):
                    zf_arrival(d).wait_recv()

                parts = [zf.at[tile]] + [zfbuf.at[zm[d]] for d in range(1, NZ)]
                top, total, scales = weigh_packed([part[8] for part in parts])
                for xx in range(NX):

                    def put_zx(half, value):
                        zx[xx, half] = value

                    blend(parts, scales, xx, 2 * xx, put_zx)
                    zx[xx, 2] = jnp.where(lane < 32, rolled(top, -xx), rolled(total, 32 - xx))
                for d in near:
                    zx_copy(d).start()

        for d in (1, 3, 2):
            x_arrival(d, h).wait_recv()
        if h == 0:
            mix.append(weigh([p[0] for p in columns], [p[1] for p in columns]))
            top, total = mix[0][:2]
            for zz in range(ZT):
                zsend[zz, 0] = jnp.where(lane < 32, rolled(top, -4 * zz), rolled(total, 32 - 4 * zz))
        for zz in range(ZT):

            def put_z(half, value):
                zsend[zz, 1 + 2 * h + half] = value

            blend(columns, mix[0][2], zz * 4 + h, 2 + (h * ZT + zz) * 2, put_z)
        for d in far:

            @pl.when(zp[d] < ZT)
            def _():
                z_copy(d, h).start()

    pair = remote(psend, prec, p_ss, p_rs, sibling)

    def gz_copy(d):
        return remote(agz, g.at[c, x, tile], gz_ss.at[d], gz_rs.at[d], {"seq_0": zp[d]})

    def gz_arrival(d):
        return remote(agz, g.at[c, x, zmt[d]], gz_ss.at[d], gz_rs.at[d], {"seq_0": zm[d]})

    def gzx_copy(d, dx):
        own = g.at[c, x, zmt[d]]
        return remote(own, own, gzx_ss.at[d, dx], gzx_rs.at[d, dx], {"seq_1": xp[dx]})

    def gzx_arrival(d, dx):
        slot = g.at[c, xm[dx], zmt[d]]
        return remote(slot, slot, gzx_ss.at[d, dx], gzx_rs.at[d, dx], {"seq_1": xm[dx]})

    def ga_copy(d):
        return remote(aga.at[zp[d]], ga.at[c, x, tile], ga_ss.at[d], ga_rs.at[d], {"seq_0": zp[d]})

    def ga_arrival(d):
        return remote(aga.at[0], ga.at[c, x, zmt[d]], ga_ss.at[d], ga_rs.at[d], {"seq_0": zm[d]})

    @pl.when(active)
    def _():
        for d in range(1, NX):
            zx_arrival(d).wait_recv()
        values = {}

        parts = [zx.at[x]] + [zxbuf.at[xm[d]] for d in range(1, NX)]
        last_top, last_total, scales = weigh_packed([part[2] for part in parts])

        def keep_last(half, value):
            values[3, half] = value

        blend(parts, scales, 0, 0, keep_last)
        parts = [zsend.at[tile]] + [zbuf.at[zm[d]] for d in range(1, NZ)]
        for h in range(3):
            for d in range(1, NZ):
                z_arrival(d, h).wait_recv()
            if h == 0:
                top, total, scales = weigh_packed([part[0] for part in parts])

            def keep(half, value):
                values[h, half] = value

            blend(parts, scales, h, 1 + 2 * h, keep)
        top = jnp.where(lane == 3, rolled(last_top, 3), top)
        total = jnp.where(lane == 3, rolled(last_total, 3), total)
        first = c == 0
        products = []
        for h in range(4):
            whole = jnp.broadcast_to(total[:, h : h + 1], (8, 128))
            halves = [(values[h, half] / whole).astype(BF16) for half in range(2)]
            attn = jnp.concatenate(halves, axis=1)
            start = pl.multiple_of(c * 1024 + h * HD, HD)
            products.append(jnp.dot(attn, wo[pl.ds(start, HD), :], preferred_element_type=F32))
            low, high = halves[0].astype(F32), halves[1].astype(F32)
            attn_all[4 * c + h] = jnp.where(first, low, high)
            psend[8 + h] = jnp.where(first, high, low)
        partial = products[0] + products[1] + products[2] + products[3]
        for i in range(8):
            psend[i] = partial[:, i * 128 : (i + 1) * 128]
        pair.start()
        start = pl.multiple_of(tile * 8, 8)
        own_hidden = hid[x, pl.ds(start, 8), :]
        target = goal[x, pl.ds(start, 8), :]
        which = emb_ref[x // 2]
        pair.wait_recv()
        resid = own_hidden + (partial + jnp.concatenate([prec[i] for i in range(8)], axis=1))
        inverse = lax.rsqrt(jnp.mean(resid * resid, axis=1, keepdims=True) + 1e-06)
        gain = og_ref[...]
        normed = resid * inverse * gain
        real = start + lax.broadcasted_iota(jnp.int32, (8, 1), 0) < ACT
        heads = oh[which]
        back = jnp.zeros((8, D), F32)
        for j in range(ADIM):
            head = heads[j : j + 1, :]
            velocity = jnp.sum(normed * head, axis=1, keepdims=True)
            dvel = 2.0 * (velocity - target[:, j : j + 1]) / (8 * ROWS)
            back = back + jnp.where(real, dvel, 0.0) * head
        scaled = back * gain
        mean = jnp.mean(resid * scaled, axis=1, keepdims=True)
        dresid = inverse * scaled - inverse * inverse * inverse * resid * mean
        dresid = dresid.astype(BF16).astype(F32)
        own = jnp.where(first, dresid[:, :512], dresid[:, 512:])
        stats = jnp.where(lane < 32, top, rolled(total, 32))
        for h in range(4):
            delta = jnp.sum(products[h] * dresid, axis=1, keepdims=True)
            stats = jnp.where(lane == 64 + h, delta, stats)
        for i in range(4):
            agz[i] = own[:, i * 128 : (i + 1) * 128]
        agz[4] = stats
        for d in close:
            gz_copy(d).start()
        g[c, x, tile] = agz[...]
        for dx in near:
            gzx_copy(0, dx).start()
        for h in range(4):
            attn_all[4 * other + h] = prec[8 + h]
        for zz in range(NZ):
            aga[zz] = attn_all[zz]
        ga[c, x, tile] = aga[z]
        for d in far:
            ga_copy(d).start()

    def gzc_copy(d):
        return remote(g.at[c, xm[d]], g.at[c, xm[d]], gzc_ss.at[d], gzc_rs.at[d], sibling)

    def gzc_arrival(d):
        return remote(g.at[other, xm[d]], g.at[other, xm[d]], gzc_ss.at[d], gzc_rs.at[d], sibling)

    def gax_copy(d):
        return remote(ga.at[c, x], ga.at[c, x], gax_ss.at[d], gax_rs.at[d], {"seq_1": xp[d]})

    def gax_arrival(d):
        return remote(ga.at[c, xm[d]], ga.at[c, xm[d]], gax_ss.at[d], gax_rs.at[d], {"seq_1": xm[d]})

    gac = remote(ga.at[c], ga.at[c], gac_ss, gac_rs, sibling)
    gac_arrival = remote(ga.at[other], ga.at[other], gac_ss, gac_rs, sibling)

    for d in close:

        @pl.when(zm[d] < ZT)
        def _():
            gz_arrival(d).wait_recv()
            for dx in near:
                gzx_copy(d, dx).start()

    gzc_copy(0).start()
    for dx in (1, 3, 2):
        for d in range(NZ):

            @pl.when(zm[d] < ZT)
            def _():
                gzx_arrival(d, dx).wait_recv()

        gzc_copy(dx).start()
    for d in range(1, NZ):

        @pl.when(zm[d] < ZT)
        def _():
            ga_arrival(d).wait_recv()

    for d in near:
        gax_copy(d).start()
    def row_scales(i, s):
        half = other if i == 0 else c
        for t in range(14 * s, 14 * s + 14):
            xx, zz = t // 7, t % 7
            stats = g[half, xx, zz, 4]
            scale = jnp.exp(rolled(local_peak[i, xx], -4 * zz) - stats) / rolled(stats, 96)
            for h in range(4):
                n = 4 * i + h
                scale_ref[n, t * 8 : t * 8 + 8] = jnp.broadcast_to(scale[:, h : h + 1], (8, 128))
                delta_ref[n, t * 8 : t * 8 + 8] = jnp.broadcast_to(stats[:, 64 + h : 65 + h], (8, 128))

    def keep_rows(core):
        for t in range(0, 28, 2):
            for i in range(4):
                both = [g[core, u // 7, u % 7, i] for u in (t, t + 1)]
                lo = pl.multiple_of(core * 512 + i * 128, 128)
                db[t * 8 : t * 8 + 16, pl.ds(lo, 128)] = jnp.concatenate(both, axis=0).astype(BF16)

    keep_rows(c)
    row_scales(1, 1)
    for d in range(NX):
        gzc_arrival(d).wait_recv()
    keep_rows(other)
    row_scales(0, 1)

    def core2(s):
        return remote(gq.at[0, s], cbuf2.at[s], c2_ss.at[s], c2_rs.at[s], sibling)

    def z2_copy(d):
        return remote(zs2.at[zp[d]], zbuf2.at[z], z2_ss.at[d], z2_rs.at[d], {"seq_0": zp[d]})

    def z2_arrival(d):
        return remote(zs2.at[zm[d]], zbuf2.at[zm[d]], z2_ss.at[d], z2_rs.at[d], {"seq_0": zm[d]})

    def x2_copy(d, part):
        src, dst = xs2.at[xp[d], pl.ds(4 * part, 4)], xbuf2.at[x, pl.ds(4 * part, 4)]
        return remote(src, dst, x2_ss.at[d, part], x2_rs.at[d, part], {"seq_1": xp[d]})

    def x2_arrival(d, part):
        src, dst = xs2.at[xm[d], pl.ds(4 * part, 4)], xbuf2.at[xm[d], pl.ds(4 * part, 4)]
        return remote(src, dst, x2_ss.at[d, part], x2_rs.at[d, part], {"seq_1": xm[d]})

    dattn = []

    def backward(i, s):
        if s == 0:
            row_scales(i, s)
        rows = slice(s * PAD, (s + 1) * PAD)
        stacked = jnp.concatenate(
            [dattn[i][rows, h * HD : (h + 1) * HD] for h in range(4)], axis=0
        )
        dvalues = dot_nt(stacked, v_ref[s])
        parts = []
        for h in range(4):
            delta = delta_ref[4 * i + h, rows]
            scale = scale_ref[4 * i + h, rows]
            line = []
            for k in range(4):
                cols = slice(k * 128, (k + 1) * 128)
                dv = dvalues[h * PAD : (h + 1) * PAD, cols]
                line.append((weights_ref[i, h, rows, cols] * scale * (dv - delta)).astype(BF16))
            parts.append(jnp.concatenate(line, axis=1))
        dscore = jnp.concatenate(parts, axis=0)
        grads = jnp.dot(dscore, k_ref[s], preferred_element_type=F32) * (1.0 / math.sqrt(HD))
        grads = grads.astype(BF16).astype(F32)
        for h in range(4):
            for k in range(2):
                gq[i, s, 2 * h + k] = grads[h * PAD : (h + 1) * PAD, k * 128 : (k + 1) * 128]

    for i in range(2):
        start = pl.multiple_of((other if i == 0 else c) * 1024, 1024)
        dattn.append(dot_nt(db[...], wo[pl.ds(start, 1024), :]).astype(BF16))
        backward(i, 1)
        if i == 0:
            core2(1).start()
    core2(1).wait_recv()
    for k in range(NZ):
        zs2[k] = gq[1, 1, k, 16:] + cbuf2[1, k, 16:]
    for d in far:
        z2_copy(d).start()
    zbuf2[z] = zs2[z]
    backward(0, 0)
    core2(0).start()
    backward(1, 0)
    core2(0).wait_recv()
    for k in range(NZ):
        first = gq[1, 0, k] + cbuf2[0, k]
        turned = jnp.concatenate([first, gq[1, 1, k, 0:16] + cbuf2[1, k, 0:16]], axis=0).T
        for xx in range(NX):
            xs2[xx, k] = turned[xx * 32 : (xx + 1) * 32]
        if k % 4 == 3:
            for d in near:
                x2_copy(d, k // 4).start()
    xbuf2[x] = xs2[x]

    for d in range(1, NX):
        gax_arrival(d).wait_recv()
    gac.start()
    gac_arrival.wait_recv()
    half_core = x // 2
    for t in range(0, 28, 2):
        both = jnp.concatenate([ga[half_core, u // 7, u % 7] for u in (t, t + 1)], axis=0)
        az[t * 8 : t * 8 + 16, :] = both.astype(BF16)
    ro_all[...] = dot_tn(az[...], db[...])
    offset = lax.rem(x, 2) * 64 + c * 32
    for bb in range(NB):
        ro[bb] = ro_all[pl.ds(pl.multiple_of(offset + 8 * bb, 8), 8), :]

    def y_copy(d):
        return remote(ro.at[bp[d]], yrec.at[b], y_ss.at[d], y_rs.at[d], {"batch": bp[d]})

    def y_arrival(d):
        return remote(ro.at[bm[d]], yrec.at[bm[d]], y_ss.at[d], y_rs.at[d], {"batch": bm[d]})

    for d in near:
        y_copy(d).start()
    yrec[b] = ro[b]

    def zx2_copy(d):
        return remote(zx2.at[xp[d]], zxbuf2.at[x], zx2_ss.at[d], zx2_rs.at[d], {"seq_1": xp[d]})

    def zx2_arrival(d):
        return remote(zx2.at[xm[d]], zxbuf2.at[xm[d]], zx2_ss.at[d], zx2_rs.at[d], {"seq_1": xm[d]})

    def w2_copy(k):
        return remote(ws2.at[k], wbuf2.at[z], w2_ss.at[k], w2_rs.at[z], {"seq_0": k})

    def w2_arrival(d):
        return remote(ws2.at[zm[d]], wbuf2.at[zm[d]], w2_ss.at[zm[d]], w2_rs.at[zm[d]], {"seq_0": zm[d]})

    for part in range(2):
        for d in (1, 3, 2):
            x2_arrival(d, part).wait_recv()
        for k in range(4 * part, 4 * part + 4):
            ws2[k] = xbuf2[0, k] + xbuf2[1, k] + xbuf2[2, k] + xbuf2[3, k]

            @pl.when(z != k)
            def _():
                w2_copy(k).start()

    wbuf2[z] = ws2[z]
    for d in (1, 7, 2, 6, 3, 5, 4):
        z2_arrival(d).wait_recv()
    late = zbuf2[0]
    for k in range(1, NZ):
        late = late + zbuf2[k]
    turned = jnp.concatenate([late, jnp.zeros((32, 128), F32)], axis=0).T
    for xx in range(NX):
        zx2[xx] = turned[xx * 32 : (xx + 1) * 32]
    for d in near:
        zx2_copy(d).start()
    zxbuf2[x] = zx2[x]
    for d in range(1, NB):
        y_arrival(d).wait_recv()
    raw_o = yrec[0] + yrec[1] + yrec[2] + yrec[3]
    ro_all[0:8] = raw_o
    squares_o = jnp.sum(raw_o * raw_o, keepdims=True)
    for d in (1, 3, 2):
        zx2_arrival(d).wait_recv()
    late = zxbuf2[0] + zxbuf2[1] + zxbuf2[2] + zxbuf2[3]
    for d in (1, 7, 2, 6, 3, 5, 4):
        w2_arrival(d).wait_recv()
    early = wbuf2[0]
    for k in range(1, NZ):
        early = early + wbuf2[k]
    columns = jnp.concatenate([early, late], axis=1)
    product = jnp.dot(jnp.concatenate(thirds(columns), axis=0), nperm[...], preferred_element_type=F32)
    product = product[0:32] + (product[32:64] + product[64:96])
    for bb in range(NB):
        bsend[bb] = product[:, bb * 256 : (bb + 1) * 256]

    def b_copy(d):
        return remote(bsend.at[bp[d]], brec.at[b], b_ss.at[d], b_rs.at[d], {"batch": bp[d]})

    def b_arrival(d):
        return remote(bsend.at[bm[d]], brec.at[bm[d]], b_ss.at[d], b_rs.at[d], {"batch": bm[d]})

    for d in near:
        b_copy(d).start()
    brec[b] = bsend[b]
    for d in range(1, NB):
        b_arrival(d).wait_recv()
    raw_t = brec[0] + brec[1] + brec[2] + brec[3]
    squares = jnp.sum(raw_t * raw_t, keepdims=True) + squares_o
    alls = [(dz, dx, dc) for dz in (4, 3, 5, 2, 6, 1, 7, 0) for dx in (2, 1, 3, 0) for dc in (1, 0) if dz or dx or dc]

    def d_copy(i):
        dz, dx, dc = alls[i]
        peer = zp[dz] * 8 + xp[dx] * 2 + cp[dc]
        device = {"seq_0": zp[dz], "seq_1": xp[dx], "seq_2": cp[dc]}
        return remote(drows.at[peer], drec.at[x, c * 8 + z], d_ss.at[i], d_rs.at[i], device)

    def d_arrival(i):
        dz, dx, dc = alls[i]
        peer = zm[dz] * 8 + xm[dx] * 2 + cp[dc]
        device = {"seq_0": zm[dz], "seq_1": xm[dx], "seq_2": cp[dc]}
        slot = drec.at[xm[dx], cp[dc] * 8 + zm[dz]]
        return remote(drows.at[peer], slot, d_ss.at[i], d_rs.at[i], device)

    stacked = jnp.concatenate([raw_t[:, r * 64 : (r + 1) * 64] for r in range(4)], axis=0)
    stacked = jnp.concatenate([stacked, jnp.zeros((128, 64), F32)], axis=1).T
    drows[:, 0, :] = stacked[0:64]
    drows[:, 1, :] = jnp.broadcast_to(squares, (64, 128))
    for i in range(63):
        d_copy(i).start()
    drec[x, c * 8 + z] = drows[me]
    for i in range(63):
        d_arrival(i).wait_recv()
    e_send[...] = jnp.sum(jnp.sum(drec[:, :, 1, :], axis=0), axis=0, keepdims=True)

    def e_copy(d):
        return remote(e_send, e_rec.at[b], e_ss.at[d], e_rs.at[d], {"batch": bp[d]})

    def e_arrival(d):
        return remote(e_send, e_rec.at[bm[d]], e_ss.at[d], e_rs.at[d], {"batch": bm[d]})

    for d in near:
        e_copy(d).start()
    e_rec[b] = e_send[...]
    blocks = [drec[i, :, 0, :] for i in range(NX)]
    for r in range(4):
        line = rolled(blocks[0], -32 * r)
        for i in range(1, NX):
            line = jnp.where(wide_lane // 32 == i, rolled(blocks[i], 32 * (i - r)), line)
        for t in range(16):
            q_raw[r : r + 1, t * 128 : (t + 1) * 128] = line[t : t + 1]
    for d in range(1, NB):
        e_arrival(d).wait_recv()
    norm = jnp.sqrt(e_rec[0] + e_rec[1] + e_rec[2] + e_rec[3])
    factor = jnp.minimum(1.0, 1.0 / (norm + 1e-06))[0:1, 0:1]
    q_out[...] = q_raw[...] * factor
    o_out[...] = ro_all[0:8] * factor

    for d in range(NX):
        core_copy(d).wait_send()
        gzc_copy(d).wait_send()

        @pl.when(x != d)
        def _():
            for h in range(3):
                x_copy(d, h).wait_send()

        if d:
            gax_copy(d).wait_send()
            x2_copy(d, 0).wait_send()
            x2_copy(d, 1).wait_send()
            zx2_copy(d).wait_send()
            y_copy(d).wait_send()
            b_copy(d).wait_send()
            e_copy(d).wait_send()
    for s in range(2):
        core2(s).wait_send()
    gac.wait_send()
    for d in range(NZ):

        @pl.when(z != d)
        def _():
            w2_copy(d).wait_send()

        @pl.when(zm[d] < ZT)
        def _():
            for dx in range(1, NX):
                gzx_copy(d, dx).wait_send()

    for d in range(1, NZ):
        z2_copy(d).wait_send()

        @pl.when(zp[d] < ZT)
        def _():
            for h in range(3):
                z_copy(d, h).wait_send()
            zf_copy(d).wait_send()

    @pl.when(active)
    def _():
        pair.wait_send()
        for d in range(1, NX):
            zx_copy(d).wait_send()
        for d in range(1, NZ):
            gz_copy(d).wait_send()
            ga_copy(d).wait_send()

    for i in range(63):
        d_copy(i).wait_send()


def local(
    actions,
    noise,
    times,
    embodiment,
    prefix_blocks,
    prefix_keys,
    prefix_values,
    input_heads,
    attn_gain,
    w_query,
    w_output,
    out_gain,
    output_heads,
):
    dma = pltpu.SemaphoreType.DMA

    def v(*shape, kind=F32):
        return pltpu.VMEM(shape, kind)

    def pairs(*counts):
        return [dma((n,)) if n else dma for n in counts for _ in range(2)]

    return pl.pallas_call(
        step_kernel,
        out_shape=(
            jax.ShapeDtypeStruct((4, HEADS * HD), F32),
            jax.ShapeDtypeStruct((8, D), F32),
        ),
        in_specs=[HBM] * 13,
        out_specs=(VMEM, VMEM),
        scratch_shapes=[
            pltpu.SMEM((2, 2), F32), pltpu.SMEM((2,), jnp.int32), pltpu.SMEM((2,), jnp.int32),
            v(2, ADIM, ACT), v(2, 2, ADIM, ACT), v(1, D), v(1, D),
            v(4, ADIM, D), v(2, KEYS, HD, kind=BF16), v(2, KEYS, HD, kind=BF16), v(2, D, 1024, kind=BF16),
            v(2048, D, kind=BF16), v(4, ADIM, D), v(4, ADIM, 128), v(4, 128, ADIM), v(4, HALF, D),
            v(ALL, D, kind=BF16), v(256, D, kind=BF16),
            v(2, 4, ALL, KEYS), v(2, NX, 8, 128), v(2, NX, 58, 8, 128), v(NX, 58, 8, 128),
            v(NX, 44, 8, 128), v(NX, 44, 8, 128), v(ZT, 9, 8, 128), v(NZ, 9, 8, 128),
            v(NX, 3, 8, 128), v(NX, 3, 8, 128), v(ZT, 7, 8, 128), v(NZ, 7, 8, 128),
            v(12, 8, 128), v(12, 8, 128), v(8, 8, 128), v(5, 8, 128), v(NZ, 8, 128),
            v(2, NX, ZT, 5, 8, 128), v(2, NX, ZT, 8, 128),
            v(ALL, D, kind=BF16), v(8, ALL, 128), v(8, ALL, 128), v(ALL, 128, kind=BF16), v(128, D),
            v(NB, 8, D), v(2, 2, NZ, PAD, 128), v(2, NZ, PAD, 128), v(NZ, 96, 128), v(NZ, 96, 128),
            v(NX, 32, 128), v(NX, 32, 128), v(NX, NZ, 32, 128), v(NX, NZ, 32, 128),
            v(NZ, 32, 128), v(NZ, 32, 128), v(NB, 32, 256), v(NB, 32, 256), v(NB, 8, D),
            v(64, 2, 128), v(NX, 16, 2, 128), v(4, HEADS * HD), v(1, 128), v(NB, 1, 128),
            dma((14,)),
        ]
        + pairs(NX)
        + [dma((NX, 3)), dma((NX, 3))]
        + pairs(NZ, NX)
        + [dma((NZ, 3)), dma((NZ, 3))]
        + pairs(0, NZ)
        + [dma((NZ, NX)), dma((NZ, NX))]
        + pairs(NX, NZ, NX, 0, 2, NZ, NX)
        + [dma((NX, 2)), dma((NX, 2))]
        + pairs(NZ, NB, NB, 64, NB),
        compiler_params=pltpu.CompilerParams(
            collective_id=0, has_side_effects=True, vmem_limit_bytes=44 * 1024 * 1024
        ),
    )(
        *(
            pltpu.with_memory_space_constraint(one, pltpu.HBM)
            for one in (
                times, embodiment, prefix_blocks, jnp.swapaxes(actions, 1, 2), jnp.swapaxes(noise, 2, 3),
                attn_gain[None, :], out_gain[None, :], input_heads, prefix_keys, prefix_values,
                w_query, w_output, jnp.swapaxes(output_heads, 1, 2),
            )
        )
    )


def solution(mesh):
    torus = Mesh(
        mesh.devices.reshape(NZ, NX, 2, mesh.shape["batch"]), ("seq_0", "seq_1", "seq_2", "batch")
    )
    placed = (
        P("batch", None, None),
        P("batch", None, None, None),
        P("batch", None),
        P("batch"),
        P("batch"),
        P("batch", SEQ, None),
        P("batch", SEQ, None),
        P(),
        P(),
        P(),
        P(),
        P(),
        P(),
    )
    return jax.shard_map(
        local,
        mesh=torus,
        in_specs=placed,
        out_specs=(P(SEQ_BATCH, None), P(SEQ_BATCH, None)),
        check_vma=False,
    )
```
